128 devices in a mesh: subtree: 32 (over z, x, core), front: 4 (over y).
Axes of the slice: x: 4, y: 4, z: 4, core: 2. Of those that a mesh axis runs over, the one named last changes fastest.
Arguments:
- right_hand_sides: float32 [64, 851968], P(None, ('subtree', 'front')), may hold values from -6 to 6
- elimination_natural_index: int32 [851968], P(('subtree', 'front')), may hold values from 0 to 851967, as said below
- leaf_diagonal_inverse: bfloat16 [512, 512, 512], P(('subtree', 'front')), may hold values from -1 to 1.5
- leaf_update_block: bfloat16 [512, 512, 256], P(('subtree', 'front')), may hold values from -0.25 to 0.25
- leaf_parent_rows: int32 [512, 256], P(('subtree', 'front')), may hold values from 0 to 1023, as said below
- leaf_parent_node: int32 [512], P(('subtree', 'front')), may hold values from 0 to 255, as said below
- level1_diagonal_inverse: bfloat16 [256, 1024, 1024], P(('subtree', 'front')), may hold values from -1 to 1.5
- level1_update_block: bfloat16 [256, 1024, 512], P(('subtree', 'front')), may hold values from -0.1875 to 0.1875
- level1_parent_rows: int32 [256, 512], P(('subtree', 'front')), may hold values from 0 to 1535, as said below
- level1_parent_node: int32 [256], P(('subtree', 'front')), may hold values from 0 to 127, as said below
- level2_diagonal_inverse: bfloat16 [128, 1536, 1536], P('subtree', None, 'front'), may hold values from -1 to 1.5
- level2_update_block: bfloat16 [128, 1536, 768], P('subtree', 'front'), may hold values from -0.15625 to 0.15625
- level2_parent_rows: int32 [128, 768], P('subtree'), may hold values from 0 to 2047, as said below
- level2_parent_node: int32 [128], P('subtree'), may hold values from 0 to 63, as said below
- level3_diagonal_inverse: bfloat16 [64, 2048, 2048], P('subtree', None, 'front'), may hold values from -1 to 1.5
Outputs:
- solution: float32 [64, 851968], P(None, ('subtree', 'front'))
The draws below stay inside these ranges and needn't reach their ends.
Inputs may be any that keep to these rules, and one draw needn't show every extreme that they name: `elimination_natural_index`: A permutation of the unknowns; each device's block of 6656 elimination positions takes exactly 6656 / 128 unknowns from each device's block of natural positions. `leaf_parent_node`: the leaf with number (s * 4 + f) * 4 + c has a parent (t * 4 + f) * 2 + q with t equal to s or s xor 1; every level-1 supernode has exactly two children, one from each of the two subtree indices s and s xor 1. `level1_parent_node`: the level-1 supernode on subtree index s has a parent t * 4 + q with t equal to s or s xor 2; every level-2 supernode has exactly two children, one from each of the two subtree indices s and s xor 2. `level2_parent_node`: the level-2 supernode s * 4 + c has a parent t * 2 + q with t equal to s or s xor 4; every level-3 supernode has exactly two children, one from each of the two subtree indices s and s xor 4. `leaf_parent_rows`: distinct within each row. `level1_parent_rows`: distinct within each row; position j lies in the share j // (512 / 4) of the parent's rows, the share f being rows f * 1536 / 4 to (f + 1) * 1536 / 4 - 1. `level2_parent_rows`: distinct within each row; position j lies in the share j // (768 / 4) of the parent's rows, the share f being rows f * 2048 / 4 to (f + 1) * 2048 / 4 - 1.
All inputs are finite; a program needn't handle non-finite values.
Results may differ from the reference program's by a relative error of at most 0.0043.
Values may be sent and summed in bfloat16 or wider, within the bound.
No kernel may reach another device: no remote copies, remote signals or barrier semaphores. Data moves between devices by JAX's collectives and lax.ppermute only.
A program may use at most 320 MiB of HBM per device.

```python
import jax
import jax.numpy as jnp
from jax import lax

RHS_COLUMNS = 64
LEAVES = 4
LEAF = 512
SEP1 = 1024
SEP2 = 1536
SEP3 = 2048
BORDER0 = 256
BORDER1 = 512
BORDER2 = 768
NODES1 = 2
NODES2 = 4
NODES3 = 2
ROWS_PER_DEVICE = 6656
TOTAL = 851968
N_SUBTREE = 32
N_FRONT = 4
DEVICES = 128


def triangle(key, count, width):
    key_off, key_diag = jax.random.split(key)
    off_part = jnp.clip(jax.random.normal(key_off, (count, width, width), jnp.float32), -4.0, 4.0)
    diag_part = jax.random.uniform(key_diag, (count, 1, width), jnp.float32, 0.6, 1.4)
    row_ids = jnp.arange(width)[:, None]
    col_ids = jnp.arange(width)[None, :]
    upper = jnp.where(row_ids < col_ids, off_part * (0.5 / jnp.sqrt(jnp.float32(width))), 0.0)
    diagonal = jnp.where(row_ids == col_ids, diag_part, 0.0)
    return (upper + diagonal).astype(jnp.bfloat16)


def pair_parents(key, units, others, each, bit):
    half = each // 2
    unit_ids = jnp.arange(units)[:, None, None]
    other_ids = jnp.arange(others)[None, :, None]
    lower = unit_ids - (unit_ids & 1 << bit)
    orders = jax.vmap(lambda k: jax.random.permutation(k, each))(jax.random.split(key, units * others)).reshape(units, others, each)
    side_ids = orders // half
    slot_ids = orders % half
    owner_ids = lower + side_ids * (1 << bit)
    return ((owner_ids * others + other_ids) * half + slot_ids).reshape(-1).astype(jnp.int32)


def pick_rows(key, count, width, border):
    orders = jax.vmap(lambda k: jax.random.permutation(k, width))(jax.random.split(key, count))
    return orders[:, :border].astype(jnp.int32)


def pick_share_rows(key, count, width, border):
    share_width = width // N_FRONT
    share_count = border // N_FRONT
    orders = jax.vmap(lambda k: jax.random.permutation(k, share_width))(jax.random.split(key, count * N_FRONT))
    picked = orders[:, :share_count].reshape(count, N_FRONT, share_count)
    shifted = picked + (jnp.arange(N_FRONT) * share_width)[None, :, None]
    return shifted.reshape(count, border).astype(jnp.int32)


def draw_elimination_natural_index(key, part):
    device_list = N_SUBTREE * N_FRONT
    rows_per_peer = ROWS_PER_DEVICE // device_list
    key_src, key_dst = jax.random.split(jax.random.fold_in(key, 11))
    source_orders = jax.vmap(lambda k: jax.random.permutation(k, ROWS_PER_DEVICE))(jax.random.split(key_src, device_list))
    grouped = source_orders.reshape(device_list, device_list, rows_per_peer)
    dest_ids = jnp.arange(device_list)[:, None]
    source_ids = jnp.arange(device_list)[None, :]
    group_ids = (dest_ids - source_ids) % device_list
    picked = grouped[source_ids, group_ids]
    global_ids = picked + (source_ids * ROWS_PER_DEVICE)[:, :, None]
    flat = global_ids.reshape(device_list, ROWS_PER_DEVICE)
    shuffles = jax.vmap(lambda k: jax.random.permutation(k, ROWS_PER_DEVICE))(jax.random.split(key_dst, device_list))
    return jnp.take_along_axis(flat, shuffles, axis=1).reshape(-1).astype(jnp.int32)


def draw_leaf_diagonal_inverse(key, part):
    return triangle(jax.random.fold_in(key, 21), N_SUBTREE * N_FRONT * LEAVES, LEAF)


def draw_level1_diagonal_inverse(key, part):
    return triangle(jax.random.fold_in(key, 22), N_SUBTREE * N_FRONT * NODES1, SEP1)


def draw_level2_diagonal_inverse(key, part):
    return triangle(jax.random.fold_in(key, 23), N_SUBTREE * NODES2, SEP2)


def draw_level3_diagonal_inverse(key, part):
    return triangle(jax.random.fold_in(key, 24), N_SUBTREE * NODES3, SEP3)


def draw_leaf_parent_rows(key, part):
    return pick_rows(jax.random.fold_in(key, 31), N_SUBTREE * N_FRONT * LEAVES, SEP1, BORDER0)


def draw_level1_parent_rows(key, part):
    return pick_share_rows(jax.random.fold_in(key, 32), N_SUBTREE * N_FRONT * NODES1, SEP2, BORDER1)


def draw_level2_parent_rows(key, part):
    return pick_share_rows(jax.random.fold_in(key, 33), N_SUBTREE * NODES2, SEP3, BORDER2)


def draw_leaf_parent_node(key, part):
    return pair_parents(jax.random.fold_in(key, 41), N_SUBTREE, N_FRONT, LEAVES, 0)


def draw_level1_parent_node(key, part):
    return pair_parents(jax.random.fold_in(key, 42), N_SUBTREE, 1, N_FRONT * NODES1, 1)


def draw_level2_parent_node(key, part):
    return pair_parents(jax.random.fold_in(key, 43), N_SUBTREE, 1, NODES2, 2)


def steps_of(stream_key, extent, shards, least, top_value):
    def one(position, parts):
        steps = jax.random.uniform(jax.random.fold_in(jax.random.fold_in(stream_key, 6), position), (parts,), jnp.float32, least / len(shards), top_value / len(shards))
        return jnp.repeat(jnp.exp(steps), extent[position] // parts).reshape((-1,) + (1,) * (len(extent) - position - 1))

    loudness = one(*shards[0])
    for cut in shards[1:]:
        loudness = loudness * one(*cut)
    return loudness


def bell_draw(own_key, extent, spread, most, shards=(), dtype=jnp.bfloat16):
    result = spread * jax.random.normal(own_key, extent, jnp.float32)
    if shards:
        result = result * steps_of(own_key, extent, shards, -0.22, 0.18)
    return jnp.clip(result, -most, most).astype(dtype)


def setup_inputs(seed: int = 0) -> dict:
    key_of = jax.random.split(jax.random.key(seed), 16)
    return {
        "right_hand_sides": bell_draw(key_of[0], (RHS_COLUMNS, TOTAL), 1.0, 6.0, ((1, 128),), jnp.float32),
        "elimination_natural_index": draw_elimination_natural_index(jax.random.fold_in(key_of[15], 71), 0),
        "leaf_diagonal_inverse": draw_leaf_diagonal_inverse(jax.random.fold_in(key_of[15], 71), 0),
        "leaf_update_block": bell_draw(key_of[3], (DEVICES * LEAVES, LEAF, BORDER0), LEAF ** -0.5, 0.25, ((0, 128),)),
        "leaf_parent_rows": draw_leaf_parent_rows(jax.random.fold_in(key_of[15], 71), 0),
        "leaf_parent_node": draw_leaf_parent_node(jax.random.fold_in(key_of[15], 71), 0),
        "level1_diagonal_inverse": draw_level1_diagonal_inverse(jax.random.fold_in(key_of[15], 71), 0),
        "level1_update_block": bell_draw(key_of[7], (DEVICES * NODES1, SEP1, BORDER1), SEP1 ** -0.5, 0.1875, ((0, 128),)),
        "level1_parent_rows": draw_level1_parent_rows(jax.random.fold_in(key_of[15], 71), 0),
        "level1_parent_node": draw_level1_parent_node(jax.random.fold_in(key_of[15], 71), 0),
        "level2_diagonal_inverse": draw_level2_diagonal_inverse(jax.random.fold_in(key_of[15], 71), 0),
        "level2_update_block": bell_draw(key_of[11], (N_SUBTREE * NODES2, SEP2, BORDER2), SEP2 ** -0.5, 0.15625, ((0, 32), (1, 4))),
        "level2_parent_rows": draw_level2_parent_rows(jax.random.fold_in(key_of[15], 71), 0),
        "level2_parent_node": draw_level2_parent_node(jax.random.fold_in(key_of[15], 71), 0),
        "level3_diagonal_inverse": draw_level3_diagonal_inverse(jax.random.fold_in(key_of[15], 71), 0),
    }


def solve_nodes(rhs_nodes, inverse_nodes):
    rounded = rhs_nodes.astype(jnp.bfloat16)
    return lax.map(lambda pair: jnp.dot(pair[0], pair[1], preferred_element_type=jnp.float32), (rounded, inverse_nodes))


def spread_nodes(solved, update_nodes, row_ids, parent_ids, count, width):
    terms = lax.map(lambda pair: jnp.dot(pair[0].astype(jnp.bfloat16), pair[1], preferred_element_type=jnp.float32), (solved, update_nodes))
    segment_ids = (parent_ids[:, None] * width + row_ids).reshape(-1).astype(jnp.int32)
    flat_terms = jnp.transpose(terms, (0, 2, 1)).reshape(-1, RHS_COLUMNS)
    totals = jax.ops.segment_sum(flat_terms, segment_ids, num_segments=count * width)
    return jnp.transpose(totals.reshape(count, width, RHS_COLUMNS), (0, 2, 1))


def reference(right_hand_sides, elimination_natural_index, leaf_diagonal_inverse, leaf_update_block, leaf_parent_rows, leaf_parent_node, level1_diagonal_inverse, level1_update_block, level1_parent_rows, level1_parent_node, level2_diagonal_inverse, level2_update_block, level2_parent_rows, level2_parent_node, level3_diagonal_inverse):
    device_list = N_SUBTREE * N_FRONT
    front_list = N_FRONT
    ordered_rows = jnp.take(right_hand_sides, elimination_natural_index, axis=1).reshape(RHS_COLUMNS, N_SUBTREE, front_list, ROWS_PER_DEVICE)
    edge_zero = LEAVES * LEAF
    edge_one = edge_zero + NODES1 * SEP1
    edge_two = edge_one + NODES2 * SEP2 // front_list
    leaf_rhs = jnp.transpose(ordered_rows[..., :edge_zero].reshape(RHS_COLUMNS, device_list, LEAVES, LEAF), (1, 2, 0, 3)).reshape(device_list * LEAVES, RHS_COLUMNS, LEAF)
    level1_rhs = jnp.transpose(ordered_rows[..., edge_zero:edge_one].reshape(RHS_COLUMNS, device_list, NODES1, SEP1), (1, 2, 0, 3)).reshape(device_list * NODES1, RHS_COLUMNS, SEP1)
    level2_rhs = jnp.transpose(ordered_rows[..., edge_one:edge_two].reshape(RHS_COLUMNS, N_SUBTREE, front_list, NODES2, SEP2 // front_list), (1, 3, 0, 2, 4)).reshape(N_SUBTREE * NODES2, RHS_COLUMNS, SEP2)
    level3_rhs = jnp.transpose(ordered_rows[..., edge_two:].reshape(RHS_COLUMNS, N_SUBTREE, front_list, NODES3, SEP3 // front_list), (1, 3, 0, 2, 4)).reshape(N_SUBTREE * NODES3, RHS_COLUMNS, SEP3)
    leaf_sol = solve_nodes(leaf_rhs, leaf_diagonal_inverse)
    update_one = spread_nodes(leaf_sol, leaf_update_block, leaf_parent_rows, leaf_parent_node, device_list * NODES1, SEP1)
    level1_sol = solve_nodes(level1_rhs - update_one, level1_diagonal_inverse)
    update_two = spread_nodes(level1_sol, level1_update_block, level1_parent_rows, level1_parent_node, N_SUBTREE * NODES2, SEP2)
    level2_sol = solve_nodes(level2_rhs - update_two, level2_diagonal_inverse)
    update_three = spread_nodes(level2_sol, level2_update_block, level2_parent_rows, level2_parent_node, N_SUBTREE * NODES3, SEP3)
    level3_sol = solve_nodes(level3_rhs - update_three, level3_diagonal_inverse)
    leaf_back = jnp.transpose(leaf_sol.reshape(device_list, LEAVES, RHS_COLUMNS, LEAF), (2, 0, 1, 3)).reshape(RHS_COLUMNS, device_list, edge_zero)
    one_back = jnp.transpose(level1_sol.reshape(device_list, NODES1, RHS_COLUMNS, SEP1), (2, 0, 1, 3)).reshape(RHS_COLUMNS, device_list, NODES1 * SEP1)
    two_back = jnp.transpose(level2_sol.reshape(N_SUBTREE, NODES2, RHS_COLUMNS, front_list, SEP2 // front_list), (2, 0, 3, 1, 4)).reshape(RHS_COLUMNS, device_list, NODES2 * SEP2 // front_list)
    three_back = jnp.transpose(level3_sol.reshape(N_SUBTREE, NODES3, RHS_COLUMNS, front_list, SEP3 // front_list), (2, 0, 3, 1, 4)).reshape(RHS_COLUMNS, device_list, NODES3 * SEP3 // front_list)
    joined = jnp.concatenate([leaf_back, one_back, two_back, three_back], axis=2)
    return joined.reshape(RHS_COLUMNS, device_list * ROWS_PER_DEVICE)
```

```python
import jax
import jax.numpy as jnp
from jax import lax
from jax.experimental import pallas as pl
from jax.experimental.pallas import tpu as pltpu
from jax.sharding import Mesh, PartitionSpec as P

RHS = 64
LEAVES, LEAF, BORDER0 = 4, 512, 256
NODES1, SEP1, BORDER1 = 2, 1024, 512
NODES2, SEP2, BORDER2 = 4, 1536, 768
NODES3, SEP3 = 2, 2048
FRONT = 4
SHARE2, SHARE3 = SEP2 // FRONT, SEP3 // FRONT
PART1, PART2 = BORDER1 // FRONT, BORDER2 // FRONT
ROWS = 6656
DEVICES = 128
EACH = ROWS // DEVICES
HALF = EACH // 2
SLOT = 32
EDGE0 = LEAVES * LEAF
EDGE1 = EDGE0 + NODES1 * SEP1
EDGE2 = EDGE1 + NODES2 * SHARE2
META = 16

SUBTREE = ("z", "x1", "x0", "core")
ALL = SUBTREE + ("front",)

bf16, f32, i32 = jnp.bfloat16, jnp.float32, jnp.int32
VMEM = pl.BlockSpec(memory_space=pltpu.VMEM)
SMEM = pl.BlockSpec(memory_space=pltpu.SMEM)
HBM = pl.BlockSpec(memory_space=pl.ANY)


def params(mib):
    return pltpu.CompilerParams(vmem_limit_bytes=mib << 20)


def struct(shape, dtype):
    return jax.ShapeDtypeStruct(shape, dtype)


def mm(a, b):
    return jnp.dot(a, b, preferred_element_type=f32)


def mm_nt(a, b):
    return lax.dot_general(a, b, (((1,), (1,)), ((), ())), preferred_element_type=f32)


def place(targets, width):
    ids = lax.broadcasted_iota(i32, (width, targets.shape[1]), 0)
    return jnp.where(ids == targets, 1.0, 0.0).astype(bf16)


def digits(targets, flag):
    n = targets.shape[1]
    ids = lax.broadcasted_iota(i32, (META, n), 0)
    high = jnp.broadcast_to(targets >> 6, (META, n))
    low = jnp.broadcast_to(targets & 63, (META, n))
    rows = jnp.where(ids == 0, high, jnp.where(ids == 1, low, flag))
    return rows.astype(f32).astype(bf16)


def undigits(meta):
    m = meta.astype(f32).astype(i32)
    return m[0:1] * 64 + m[1:2], m[2:3]


def tall_kernel(wide_ref, tall_ref):
    wide = wide_ref[...]
    tall_ref[...] = jnp.concatenate([wide, wide], axis=0).T


def pick_kernel(asked_ref, tall_ref, out_ref, buf):
    low = lax.broadcasted_iota(i32, (1, 128), 1) < RHS

    def gather(d, carry):
        base = pl.multiple_of(d * SLOT, SLOT)
        buf[pl.ds(base + 24, 8), :] = jnp.zeros((8, 128), f32)
        for k in range(HALF):
            first = tall_ref[pl.ds(asked_ref[d, k], 1), :]
            second = tall_ref[pl.ds(asked_ref[d, k + HALF], 1), :]
            buf[pl.ds(base + k, 1), :] = jnp.where(low, first, second)
        return carry

    lax.fori_loop(0, DEVICES, gather, 0)

    def narrow(d, carry):
        base = pl.multiple_of(d * 8 * SLOT, 8 * SLOT)
        out_ref[pl.ds(base, 8 * SLOT), :] = buf[pl.ds(base, 8 * SLOT), :].astype(bf16)
        return carry

    lax.fori_loop(0, DEVICES // 8, narrow, 0)


def leaf_kernel(
    order_ref,
    parent_ref,
    where_ref,
    arrived_ref,
    rows_ref,
    inverse_hbm,
    update_hbm,
    out_hbm,
    send_ref,
    rhs1_ref,
    rhs2_ref,
    rhs3_ref,
    flat,
    turned,
    tall,
    inverse_ref,
    update_ref,
    sol_ref,
    kept_ref,
    kept_rows,
    sems,
):
    load_inverse = pltpu.make_async_copy(inverse_hbm, inverse_ref, sems.at[0])
    load_update = pltpu.make_async_copy(update_hbm, update_ref, sems.at[1])
    load_inverse.start()
    load_update.start()

    def widen(d, carry):
        base = pl.multiple_of(d * 8 * SLOT, 8 * SLOT)
        piece = arrived_ref[pl.ds(base, 8 * SLOT), :].astype(f32)
        flat[pl.ds(base, 8 * SLOT), :] = piece
        turned[pl.ds(base, 8 * SLOT), :] = pltpu.roll(piece, RHS, 1)
        return carry

    lax.fori_loop(0, DEVICES // 8, widen, 0)

    def scatter(d, carry):
        base = pl.multiple_of(d * SLOT, SLOT)
        for k in range(HALF):
            tall[pl.ds(order_ref[d, k], 1), :] = flat[pl.ds(base + k, 1), :]
            tall[pl.ds(order_ref[d, k + HALF], 1), :] = turned[pl.ds(base + k, 1), :]
        return carry

    lax.fori_loop(0, DEVICES, scatter, 0)
    core = where_ref[0]
    load_inverse.wait()
    load_update.wait()
    for n in range(LEAVES):
        lhs = tall[n * LEAF : (n + 1) * LEAF, :].T[:RHS].astype(bf16)
        sol = mm(lhs, inverse_ref[n])
        sol_ref[:, n * LEAF : (n + 1) * LEAF] = sol
        terms = mm(sol.astype(bf16), update_ref[n]).astype(bf16)
        node = parent_ref[n]
        slot = node & 1
        away = ((node >> 3) & 1) != core
        targets = rows_ref[n : n + 1, :]

        @pl.when(away)
        def _():
            send_ref[slot, 0:RHS, :] = terms
            send_ref[slot, RHS : RHS + META, :] = digits(targets, 0)

        @pl.when(jnp.logical_not(away))
        def _():
            kept_ref[slot] = terms
            kept_rows[slot] = jnp.broadcast_to(targets, (8, BORDER0))

    store = pltpu.make_async_copy(sol_ref, out_hbm.at[:, 0:EDGE0], sems.at[2])
    store.start()
    for q in range(NODES1):
        rhs = tall[EDGE0 + q * SEP1 : EDGE0 + (q + 1) * SEP1, :].T[:RHS]
        rhs1_ref[q] = rhs - mm_nt(kept_ref[q], place(kept_rows[q, 0:1, :], SEP1))
    rhs2_ref[...] = tall[EDGE1:EDGE2, :].T[:RHS]
    rhs3_ref[...] = tall[EDGE2:ROWS, :].T[:RHS]
    store.wait()


def level1_kernel(
    parent_ref,
    got_ref,
    rhs_ref,
    rows_ref,
    inverse_ref,
    update_ref,
    out_in,
    out_hbm,
    send_ref,
    sol_ref,
    sem,
):
    del out_in
    for n in range(NODES1):
        targets, _ = undigits(got_ref[n, RHS : RHS + META, :])
        rhs = rhs_ref[n] - mm_nt(got_ref[n, 0:RHS, :], place(targets, SEP1))
        sol = mm(rhs.astype(bf16), inverse_ref[n])
        sol_ref[:, n * SEP1 : (n + 1) * SEP1] = sol
        terms = mm(sol.astype(bf16), update_ref[n]).astype(bf16)
        node = parent_ref[n]
        slot = node & 3
        side = (node >> 3) & 1
        for f in range(FRONT):
            own = slice(f * PART1, (f + 1) * PART1)
            targets = rows_ref[n : n + 1, own] + (slot * SHARE2 - f * SHARE2)
            meta = digits(targets, side)
            for x in range(2):
                send_ref[x * FRONT + f, n, 0:RHS, :] = terms[:, own]
                send_ref[x * FRONT + f, n, RHS : RHS + META, :] = meta
    store = pltpu.make_async_copy(sol_ref, out_hbm.at[:, EDGE0:EDGE1], sem)
    store.start()
    store.wait()


def sum2_kernel(where_ref, got_ref, rhs_ref, out_ref):
    x0 = where_ref[1]
    total = rhs_ref[...]
    for e in range(2 * FRONT):
        lhs, targets = [], []
        for n in range(NODES1):
            lhs.append(got_ref[e, n, 0:RHS, :])
            target, side = undigits(got_ref[e, n, RHS : RHS + META, :])
            targets.append(jnp.where(side == x0, target, -1))
        total = total - mm_nt(
            jnp.concatenate(lhs, axis=1), place(jnp.concatenate(targets, axis=1), NODES2 * SHARE2)
        )
    out_ref[...] = total.astype(bf16)


def level2_kernel(
    parent_ref,
    rhs_ref,
    rows_ref,
    inverse_ref,
    update_ref,
    out_in,
    out_hbm,
    send_ref,
    sol_ref,
    terms_ref,
    terms_rows,
    sem,
):
    del out_in
    for c in range(NODES2):
        own = slice(c * SHARE2, (c + 1) * SHARE2)
        lhs = jnp.concatenate([rhs_ref[g, :, own] for g in range(FRONT)], axis=1)
        sol = mm(lhs, inverse_ref[c])
        sol_ref[:, own] = sol
        node = parent_ref[c]
        slot = ((node >> 3) & 1) * NODES3 + (node & 1)
        terms_ref[slot] = mm(sol.astype(bf16), update_ref[c])
        terms_rows[slot] = jnp.broadcast_to(rows_ref[c : c + 1, :], (8, BORDER2))
    store = pltpu.make_async_copy(sol_ref, out_hbm.at[:, EDGE1:EDGE2], sem)
    store.start()
    for x in range(2):
        for f in range(FRONT):
            ends, end_rows = [], []
            for q in range(NODES3):
                at = x * NODES3 + q
                terms = terms_ref[at, :, f * PART2 : (f + 1) * PART2]
                rows = terms_rows[at, 0:1, f * PART2 : (f + 1) * PART2] + (q - f) * SHARE3
                send_ref[x * FRONT + f, q, 0:RHS, :] = terms[:, :128].astype(bf16)
                send_ref[x * FRONT + f, q, RHS : RHS + META, :] = digits(rows[:, :128], 0)
                ends.append(terms[:, 128:])
                end_rows.append(rows[:, 128:])
            end = jnp.concatenate(ends, axis=1).astype(bf16)
            send_ref[x * FRONT + f, NODES3, 0:RHS, :] = end
            send_ref[x * FRONT + f, NODES3, RHS : RHS + META, :] = digits(
                jnp.concatenate(end_rows, axis=1), 0
            )
    store.wait()


def sum3_kernel(got_ref, rhs_ref, out_ref):
    total = rhs_ref[...]
    for x in range(2):
        parts, targets = [], []
        for b in range(NODES3 + 1):
            pieces = [got_ref[x * FRONT + g, b, 0:RHS, :].astype(f32) for g in range(FRONT)]
            parts.append((pieces[0] + pieces[1]) + (pieces[2] + pieces[3]))
            targets.append(undigits(got_ref[x * FRONT, b, RHS : RHS + META, :])[0])
        part = jnp.concatenate(parts, axis=1)
        high = part.astype(bf16)
        low = (part - high.astype(f32)).astype(bf16)
        both = mm_nt(
            jnp.concatenate([high, low], axis=0),
            place(jnp.concatenate(targets, axis=1), NODES3 * SHARE3),
        )
        total = total - (both[:RHS] + both[RHS:])
    out_ref[...] = total.astype(bf16)


def level3_kernel(rhs_ref, inverse_ref, out_in, out_hbm, sol_ref, sem):
    del out_in
    for c in range(NODES3):
        own = slice(c * SHARE3, (c + 1) * SHARE3)
        lhs = jnp.concatenate([rhs_ref[g, :, own] for g in range(FRONT)], axis=1)
        sol_ref[:, own] = mm(lhs, inverse_ref[c])
    store = pltpu.make_async_copy(sol_ref, out_hbm.at[:, EDGE2:ROWS], sem)
    store.start()
    store.wait()


def exchange(block, axes):
    return lax.all_to_all(block, axes, split_axis=0, concat_axis=0, tiled=True)


def per_device(
    right_hand_sides,
    elimination_natural_index,
    leaf_diagonal_inverse,
    leaf_update_block,
    leaf_parent_rows,
    leaf_parent_node,
    level1_diagonal_inverse,
    level1_update_block,
    level1_parent_rows,
    level1_parent_node,
    level2_diagonal_inverse,
    level2_update_block,
    level2_parent_rows,
    level2_parent_node,
    level3_diagonal_inverse,
):
    where = jnp.stack([lax.axis_index("core"), lax.axis_index("x0")]).astype(i32)
    by_source, order = lax.sort(
        (elimination_natural_index, lax.iota(i32, ROWS)), num_keys=1, is_stable=False
    )
    asked = exchange((by_source % ROWS).reshape(DEVICES, EACH), ALL)
    tall = pl.pallas_call(
        tall_kernel,
        grid=(13,),
        in_specs=[pl.BlockSpec((RHS, 512), lambda i: (0, i))],
        out_specs=pl.BlockSpec((512, 128), lambda i: (i, 0)),
        out_shape=struct((ROWS, 128), f32),
        name="tall",
    )(right_hand_sides)
    picked = pl.pallas_call(
        pick_kernel,
        in_specs=[SMEM, VMEM],
        out_specs=VMEM,
        out_shape=struct((DEVICES * SLOT, 128), bf16),
        scratch_shapes=[pltpu.VMEM((DEVICES * SLOT, 128), f32)],
        compiler_params=params(16),
        name="pick",
    )(asked, tall)
    arrived = exchange(picked.reshape(DEVICES, SLOT, 128), ALL).reshape(DEVICES * SLOT, 128)
    out, send0, rhs1, rhs2, rhs3 = pl.pallas_call(
        leaf_kernel,
        in_specs=[SMEM, SMEM, SMEM, VMEM, VMEM, HBM, HBM],
        out_specs=[HBM, VMEM, VMEM, VMEM, VMEM],
        out_shape=[
            struct((RHS, ROWS), f32),
            struct((NODES1, RHS + META, BORDER0), bf16),
            struct((NODES1, RHS, SEP1), f32),
            struct((RHS, NODES2 * SHARE2), f32),
            struct((RHS, NODES3 * SHARE3), f32),
        ],
        scratch_shapes=[
            pltpu.VMEM((DEVICES * SLOT, 128), f32),
            pltpu.VMEM((DEVICES * SLOT, 128), f32),
            pltpu.VMEM((ROWS, 128), f32),
            pltpu.VMEM((LEAVES, LEAF, LEAF), bf16),
            pltpu.VMEM((LEAVES, LEAF, BORDER0), bf16),
            pltpu.VMEM((RHS, EDGE0), f32),
            pltpu.VMEM((NODES1, RHS, BORDER0), bf16),
            pltpu.VMEM((NODES1, 8, BORDER0), i32),
            pltpu.SemaphoreType.DMA((3,)),
        ],
        compiler_params=params(28),
        name="leaf",
    )(
        order.reshape(DEVICES, EACH),
        leaf_parent_node,
        where,
        arrived,
        leaf_parent_rows,
        leaf_diagonal_inverse,
        leaf_update_block,
    )
    got0 = lax.ppermute(send0, "core", [(0, 1), (1, 0)])
    out, send1 = pl.pallas_call(
        level1_kernel,
        in_specs=[SMEM, VMEM, VMEM, VMEM, VMEM, VMEM, HBM],
        out_specs=[HBM, VMEM],
        out_shape=[
            struct((RHS, ROWS), f32),
            struct((2 * FRONT, NODES1, RHS + META, PART1), bf16),
        ],
        scratch_shapes=[pltpu.VMEM((RHS, NODES1 * SEP1), f32), pltpu.SemaphoreType.DMA],
        input_output_aliases={6: 0},
        compiler_params=params(24),
        name="level1",
    )(
        level1_parent_node,
        got0,
        rhs1,
        level1_parent_rows,
        level1_diagonal_inverse,
        level1_update_block,
        out,
    )
    got1 = exchange(send1, ("x0", "front"))
    side2 = pl.pallas_call(
        sum2_kernel,
        in_specs=[SMEM, VMEM, VMEM],
        out_specs=VMEM,
        out_shape=struct((RHS, NODES2 * SHARE2), bf16),
        compiler_params=params(24),
        name="sum2",
    )(where, got1, rhs2)
    all2 = lax.all_gather(side2, "front", axis=0, tiled=False)
    out, send2 = pl.pallas_call(
        level2_kernel,
        in_specs=[SMEM, VMEM, VMEM, VMEM, VMEM, HBM],
        out_specs=[HBM, VMEM],
        out_shape=[
            struct((RHS, ROWS), f32),
            struct((2 * FRONT, NODES3 + 1, RHS + META, 128), bf16),
        ],
        scratch_shapes=[
            pltpu.VMEM((RHS, NODES2 * SHARE2), f32),
            pltpu.VMEM((2 * NODES3, RHS, BORDER2), f32),
            pltpu.VMEM((2 * NODES3, 8, BORDER2), i32),
            pltpu.SemaphoreType.DMA,
        ],
        input_output_aliases={5: 0},
        compiler_params=params(24),
        name="level2",
    )(
        level2_parent_node,
        all2,
        level2_parent_rows,
        level2_diagonal_inverse,
        level2_update_block,
        out,
    )
    got2 = exchange(send2, ("x1", "front"))
    side3 = pl.pallas_call(
        sum3_kernel,
        in_specs=[VMEM, VMEM],
        out_specs=VMEM,
        out_shape=struct((RHS, NODES3 * SHARE3), bf16),
        compiler_params=params(24),
        name="sum3",
    )(got2, rhs3)
    all3 = lax.all_gather(side3, "front", axis=0, tiled=False)
    return pl.pallas_call(
        level3_kernel,
        in_specs=[VMEM, VMEM, HBM],
        out_specs=HBM,
        out_shape=struct((RHS, ROWS), f32),
        scratch_shapes=[pltpu.VMEM((RHS, NODES3 * SHARE3), f32), pltpu.SemaphoreType.DMA],
        input_output_aliases={2: 0},
        compiler_params=params(24),
        name="level3",
    )(all3, level3_diagonal_inverse, out)


def solution(mesh):
    fine = Mesh(mesh.devices.reshape(4, 2, 2, 2, 4), ALL)
    return jax.shard_map(
        per_device,
        mesh=fine,
        in_specs=(
            P(None, ALL),
            P(ALL),
            P(ALL, None, None),
            P(ALL, None, None),
            P(ALL, None),
            P(ALL),
            P(ALL, None, None),
            P(ALL, None, None),
            P(ALL, None),
            P(ALL),
            P(SUBTREE, None, "front"),
            P(SUBTREE, "front", None),
            P(SUBTREE, None),
            P(SUBTREE),
            P(SUBTREE, None, "front"),
        ),
        out_specs=P(None, ALL),
        check_vma=False,
    )
```

```python
import jax
import jax.numpy as jnp
from jax import lax
from jax.experimental import pallas as pl
from jax.experimental.pallas import tpu as pltpu
from jax.sharding import Mesh, PartitionSpec as P

RHS = 64
LEAVES, LEAF, BORDER0 = 4, 512, 256
NODES1, SEP1, BORDER1 = 2, 1024, 512
NODES2, SEP2, BORDER2 = 4, 1536, 768
NODES3, SEP3 = 2, 2048
FRONT = 4
SHARE2, SHARE3 = SEP2 // FRONT, SEP3 // FRONT
PART1, PART2 = BORDER1 // FRONT, BORDER2 // FRONT
ROWS = 6656
DEVICES = 128
EACH = ROWS // DEVICES
HALF = EACH // 2
SLOT = 32
EDGE0 = LEAVES * LEAF
EDGE1 = EDGE0 + NODES1 * SEP1
EDGE2 = EDGE1 + NODES2 * SHARE2
META = 8
CHUNKS = 4
LOW = 256

SUBTREE = ("z", "x1", "x0", "core")
ALL = SUBTREE + ("front",)

bf16, f32, i32 = jnp.bfloat16, jnp.float32, jnp.int32
VMEM = pl.BlockSpec(memory_space=pltpu.VMEM)
SMEM = pl.BlockSpec(memory_space=pltpu.SMEM)
HBM = pl.BlockSpec(memory_space=pltpu.HBM)


def params(mib):
    return pltpu.CompilerParams(vmem_limit_bytes=mib << 20)


def in_hbm(x):
    return pltpu.with_memory_space_constraint(x, pltpu.HBM)


def struct(shape, dtype):
    return jax.ShapeDtypeStruct(shape, dtype)


def mm(a, b):
    return jnp.dot(a, b, preferred_element_type=f32)


def mm_nt(a, b):
    return lax.dot_general(a, b, (((1,), (1,)), ((), ())), preferred_element_type=f32)


def place(terms, high, low, blocks):
    n = low.shape[1]
    ids = lax.broadcasted_iota(i32, (LOW, n), 0).astype(f32)
    picks = jnp.where(ids == low, 1.0, 0.0).astype(bf16)
    lhs = [jnp.where(high == h, t, 0.0).astype(bf16) for t in terms for h in range(blocks)]
    found = mm_nt(jnp.concatenate(lhs, axis=0), picks)
    out = []
    for h in range(blocks):
        parts = [
            found[(t * blocks + h) * RHS : (t * blocks + h + 1) * RHS] for t in range(len(terms))
        ]
        out.append(sum(parts[1:], parts[0]))
    return jnp.concatenate(out, axis=1)


def digits(targets, flag):
    n = targets.shape[1]
    ids = lax.broadcasted_iota(i32, (META, n), 0)
    high = jnp.broadcast_to(targets >> 8, (META, n))
    low = jnp.broadcast_to(targets & (LOW - 1), (META, n))
    rows = jnp.where(ids == 0, high, jnp.where(ids == 1, low, flag))
    return rows.astype(f32).astype(bf16)


def undigits(meta):
    m = meta.astype(f32)
    return m[0:1], m[1:2], m[2:3]


def tall_kernel(wide_ref, tall_ref):
    for b in range(ROWS // 512):
        wide = wide_ref[:, b * 512 : (b + 1) * 512]
        tall_ref[b * 512 : (b + 1) * 512, :] = jnp.concatenate([wide, wide], axis=0).T


def pick_kernel(asked_ref, tall_ref, out_hbm, buf, narrow, sems):
    low = lax.broadcasted_iota(i32, (1, 128), 1) < RHS
    step = DEVICES // CHUNKS
    stores = []
    for c in range(CHUNKS):

        def gather(d, carry):
            base = pl.multiple_of(d * SLOT, SLOT)
            buf[pl.ds(base + 24, 8), :] = jnp.zeros((8, 128), f32)
            for k in range(HALF):
                first = tall_ref[pl.ds(asked_ref[d, k], 1), :]
                second = tall_ref[pl.ds(asked_ref[d, k + HALF], 1), :]
                buf[pl.ds(base + k, 1), :] = jnp.where(low, first, second)
            return carry

        lax.fori_loop(c * step, (c + 1) * step, gather, 0)
        part = slice(c * step * SLOT, (c + 1) * step * SLOT)
        narrow[part, :] = buf[part, :].astype(bf16)
        store = pltpu.make_async_copy(narrow.at[part], out_hbm.at[part], sems.at[c])
        store.start()
        stores.append(store)
    for store in stores:
        store.wait()


def leaf_kernel(
    order_ref,
    parent_ref,
    where_ref,
    arrived_ref,
    rows_ref,
    inverse_hbm,
    update_hbm,
    inverse1_hbm,
    update1_hbm,
    out_hbm,
    send_ref,
    rhs1_ref,
    rhs2_ref,
    rhs3_ref,
    inverse1_ref,
    update1_ref,
    flat,
    turned,
    tall,
    inverse_ref,
    update_ref,
    sol_ref,
    kept_ref,
    kept_rows,
    sems,
):
    load_inverse = pltpu.make_async_copy(inverse_hbm, inverse_ref, sems.at[0])
    load_update = pltpu.make_async_copy(update_hbm, update_ref, sems.at[1])
    load_inverse1 = pltpu.make_async_copy(inverse1_hbm, inverse1_ref, sems.at[3])
    load_update1 = pltpu.make_async_copy(update1_hbm, update1_ref, sems.at[4])
    load_inverse.start()
    load_update.start()
    load_inverse1.start()
    load_update1.start()

    def widen(d, carry):
        base = pl.multiple_of(d * 8 * SLOT, 8 * SLOT)
        piece = arrived_ref[pl.ds(base, 8 * SLOT), :].astype(f32)
        flat[pl.ds(base, 8 * SLOT), :] = piece
        turned[pl.ds(base, 8 * SLOT), :] = pltpu.roll(piece, RHS, 1)
        return carry

    lax.fori_loop(0, DEVICES // 8, widen, 0)

    def scatter(d, carry):
        base = pl.multiple_of(d * SLOT, SLOT)
        for k in range(HALF):
            at = order_ref[d * EACH + k]
            other = order_ref[d * EACH + k + HALF]
            tall[pl.ds(at, 1), :] = flat[pl.ds(base + k, 1), :]
            tall[pl.ds(other, 1), :] = turned[pl.ds(base + k, 1), :]
        return carry

    lax.fori_loop(0, DEVICES, scatter, 0)
    core = where_ref[0]
    load_inverse.wait()
    load_update.wait()
    for n in range(LEAVES):
        lhs = tall[n * LEAF : (n + 1) * LEAF, :].T[:RHS].astype(bf16)
        sol = mm(lhs, inverse_ref[n])
        sol_ref[:, n * LEAF : (n + 1) * LEAF] = sol
        terms = mm(sol.astype(bf16), update_ref[n]).astype(bf16)
        node = parent_ref[n]
        slot = node & 1
        away = ((node >> 3) & 1) != core
        targets = rows_ref[n : n + 1, :]

        @pl.when(away)
        def _():
            send_ref[slot, 0:RHS, :] = terms
            send_ref[slot, RHS : RHS + META, :] = digits(targets, 0)

        @pl.when(jnp.logical_not(away))
        def _():
            kept_ref[slot] = terms
            kept_rows[slot] = jnp.broadcast_to(targets, (8, BORDER0))

    store = pltpu.make_async_copy(sol_ref, out_hbm.at[:, 0:EDGE0], sems.at[2])
    store.start()
    for q in range(NODES1):
        rhs = tall[EDGE0 + q * SEP1 : EDGE0 + (q + 1) * SEP1, :].T[:RHS]
        rows = kept_rows[q, 0:1, :]
        high, low = (rows >> 8).astype(f32), (rows & (LOW - 1)).astype(f32)
        rhs1_ref[q] = rhs - place([kept_ref[q].astype(f32)], high, low, SEP1 // LOW)
    rhs2_ref[...] = tall[EDGE1:EDGE2, :].T[:RHS]
    rhs3_ref[...] = tall[EDGE2:ROWS, :].T[:RHS]
    store.wait()
    load_inverse1.wait()
    load_update1.wait()


def level1_kernel(
    parent_ref,
    got_ref,
    rhs_ref,
    rows_ref,
    inverse_ref,
    update_ref,
    out_in,
    out_hbm,
    send_ref,
    sol_ref,
    sem,
):
    del out_in
    for n in range(NODES1):
        high, low, _ = undigits(got_ref[n, RHS : RHS + META, :])
        got = got_ref[n, 0:RHS, :].astype(f32)
        rhs = rhs_ref[n] - place([got], high, low, SEP1 // LOW)
        sol = mm(rhs.astype(bf16), inverse_ref[n])
        sol_ref[:, n * SEP1 : (n + 1) * SEP1] = sol
        terms = mm(sol.astype(bf16), update_ref[n]).astype(bf16)
        node = parent_ref[n]
        slot = node & 3
        side = (node >> 3) & 1
        for f in range(FRONT):
            own = slice(f * PART1, (f + 1) * PART1)
            targets = rows_ref[n : n + 1, own] + (slot * SHARE2 - f * SHARE2)
            meta = digits(targets, side)
            for x in range(2):
                send_ref[x * FRONT + f, n, 0:RHS, :] = terms[:, own]
                send_ref[x * FRONT + f, n, RHS : RHS + META, :] = meta
    store = pltpu.make_async_copy(sol_ref, out_hbm.at[:, EDGE0:EDGE1], sem)
    store.start()
    store.wait()


def sum2_kernel(where_ref, got_ref, rhs_ref, out_ref):
    x0 = where_ref[1].astype(f32)
    terms, highs, lows = [], [], []
    for e in range(2 * FRONT):
        for n in range(NODES1):
            terms.append(got_ref[e, n, 0:RHS, :].astype(f32))
            high, low, side = undigits(got_ref[e, n, RHS : RHS + META, :])
            highs.append(jnp.where(side == x0, high, -1.0))
            lows.append(low)
    total = place(
        [jnp.concatenate(terms, axis=1)],
        jnp.concatenate(highs, axis=1),
        jnp.concatenate(lows, axis=1),
        NODES2 * SHARE2 // LOW,
    )
    out_ref[...] = (rhs_ref[...] - total).astype(bf16)


def level2_kernel(
    parent_ref,
    rhs_ref,
    rows_ref,
    inverse_ref,
    update_ref,
    out_in,
    out_hbm,
    send_ref,
    sol_ref,
    terms_ref,
    terms_rows,
    sem,
):
    del out_in
    for c in range(NODES2):
        own = slice(c * SHARE2, (c + 1) * SHARE2)
        lhs = jnp.concatenate([rhs_ref[g, :, own] for g in range(FRONT)], axis=1)
        sol = mm(lhs, inverse_ref[c])
        sol_ref[:, own] = sol
        node = parent_ref[c]
        slot = ((node >> 3) & 1) * NODES3 + (node & 1)
        terms_ref[slot] = mm(sol.astype(bf16), update_ref[c])
        terms_rows[slot] = jnp.broadcast_to(rows_ref[c : c + 1, :], (8, BORDER2))
    store = pltpu.make_async_copy(sol_ref, out_hbm.at[:, EDGE1:EDGE2], sem)
    store.start()
    for x in range(2):
        for f in range(FRONT):
            ends, end_rows = [], []
            for q in range(NODES3):
                at = x * NODES3 + q
                terms = terms_ref[at, :, f * PART2 : (f + 1) * PART2]
                rows = terms_rows[at, 0:1, f * PART2 : (f + 1) * PART2] + (q - f) * SHARE3
                send_ref[x * FRONT + f, q, 0:RHS, :] = terms[:, :128].astype(bf16)
                send_ref[x * FRONT + f, q, RHS : RHS + META, :] = digits(rows[:, :128], 0)
                ends.append(terms[:, 128:])
                end_rows.append(rows[:, 128:])
            end = jnp.concatenate(ends, axis=1).astype(bf16)
            send_ref[x * FRONT + f, NODES3, 0:RHS, :] = end
            send_ref[x * FRONT + f, NODES3, RHS : RHS + META, :] = digits(
                jnp.concatenate(end_rows, axis=1), 0
            )
    store.wait()


def sum3_kernel(got_ref, rhs_ref, out_ref):
    parts, highs, lows = [], [], []
    for x in range(2):
        for b in range(NODES3 + 1):
            pieces = [got_ref[x * FRONT + g, b, 0:RHS, :].astype(f32) for g in range(FRONT)]
            parts.append((pieces[0] + pieces[1]) + (pieces[2] + pieces[3]))
            high, low, _ = undigits(got_ref[x * FRONT, b, RHS : RHS + META, :])
            highs.append(high)
            lows.append(low)
    part = jnp.concatenate(parts, axis=1)
    coarse = part.astype(bf16).astype(f32)
    total = place(
        [coarse, part - coarse],
        jnp.concatenate(highs, axis=1),
        jnp.concatenate(lows, axis=1),
        NODES3 * SHARE3 // LOW,
    )
    out_ref[...] = (rhs_ref[...] - total).astype(bf16)


def level3_kernel(rhs_ref, inverse_ref, out_in, out_hbm, sol_ref, sem):
    del out_in
    for c in range(NODES3):
        own = slice(c * SHARE3, (c + 1) * SHARE3)
        lhs = jnp.concatenate([rhs_ref[g, :, own] for g in range(FRONT)], axis=1)
        sol_ref[:, own] = mm(lhs, inverse_ref[c])
    store = pltpu.make_async_copy(sol_ref, out_hbm.at[:, EDGE2:ROWS], sem)
    store.start()
    store.wait()


def exchange(block, axes):
    return lax.all_to_all(block, axes, split_axis=0, concat_axis=0, tiled=True)


def per_device(
    right_hand_sides,
    elimination_natural_index,
    leaf_diagonal_inverse,
    leaf_update_block,
    leaf_parent_rows,
    leaf_parent_node,
    level1_diagonal_inverse,
    level1_update_block,
    level1_parent_rows,
    level1_parent_node,
    level2_diagonal_inverse,
    level2_update_block,
    level2_parent_rows,
    level2_parent_node,
    level3_diagonal_inverse,
):
    where = jnp.stack([lax.axis_index("core"), lax.axis_index("x0")]).astype(i32)
    by_source, order = lax.sort(
        (elimination_natural_index, lax.iota(i32, ROWS)), num_keys=1, is_stable=False
    )
    asked = exchange((by_source % ROWS).reshape(DEVICES, EACH), ALL)
    tall = pl.pallas_call(
        tall_kernel,
        in_specs=[VMEM],
        out_specs=VMEM,
        out_shape=struct((ROWS, 128), f32),
        compiler_params=params(8),
        name="tall",
    )(right_hand_sides)
    picked = pl.pallas_call(
        pick_kernel,
        in_specs=[SMEM, VMEM],
        out_specs=HBM,
        out_shape=struct((DEVICES * SLOT, 128), bf16),
        scratch_shapes=[
            pltpu.VMEM((DEVICES * SLOT, 128), f32),
            pltpu.VMEM((DEVICES * SLOT, 128), bf16),
            pltpu.SemaphoreType.DMA((CHUNKS,)),
        ],
        compiler_params=params(16),
        name="pick",
    )(asked, tall)
    arrived = exchange(picked.reshape(DEVICES, SLOT, 128), ALL).reshape(DEVICES * SLOT, 128)
    out, send0, rhs1, rhs2, rhs3, inverse1, update1 = pl.pallas_call(
        leaf_kernel,
        in_specs=[SMEM, SMEM, SMEM, VMEM, VMEM, HBM, HBM, HBM, HBM],
        out_specs=[HBM, VMEM, VMEM, VMEM, VMEM, VMEM, VMEM],
        out_shape=[
            struct((RHS, ROWS), f32),
            struct((NODES1, RHS + META, BORDER0), bf16),
            struct((NODES1, RHS, SEP1), f32),
            struct((RHS, NODES2 * SHARE2), f32),
            struct((RHS, NODES3 * SHARE3), f32),
            struct((NODES1, SEP1, SEP1), bf16),
            struct((NODES1, SEP1, BORDER1), bf16),
        ],
        scratch_shapes=[
            pltpu.VMEM((DEVICES * SLOT, 128), f32),
            pltpu.VMEM((DEVICES * SLOT, 128), f32),
            pltpu.VMEM((ROWS, 128), f32),
            pltpu.VMEM((LEAVES, LEAF, LEAF), bf16),
            pltpu.VMEM((LEAVES, LEAF, BORDER0), bf16),
            pltpu.VMEM((RHS, EDGE0), f32),
            pltpu.VMEM((NODES1, RHS, BORDER0), bf16),
            pltpu.VMEM((NODES1, 8, BORDER0), i32),
            pltpu.SemaphoreType.DMA((5,)),
        ],
        compiler_params=params(28),
        name="leaf",
    )(
        order,
        leaf_parent_node,
        where,
        arrived,
        leaf_parent_rows,
        in_hbm(leaf_diagonal_inverse),
        in_hbm(leaf_update_block),
        in_hbm(level1_diagonal_inverse),
        in_hbm(level1_update_block),
    )
    got0 = lax.ppermute(send0, "core", [(0, 1), (1, 0)])
    out, send1 = pl.pallas_call(
        level1_kernel,
        in_specs=[SMEM, VMEM, VMEM, VMEM, VMEM, VMEM, HBM],
        out_specs=[HBM, VMEM],
        out_shape=[
            struct((RHS, ROWS), f32),
            struct((2 * FRONT, NODES1, RHS + META, PART1), bf16),
        ],
        scratch_shapes=[pltpu.VMEM((RHS, NODES1 * SEP1), f32), pltpu.SemaphoreType.DMA],
        input_output_aliases={6: 0},
        compiler_params=params(24),
        name="level1",
    )(
        level1_parent_node,
        got0,
        rhs1,
        level1_parent_rows,
        inverse1,
        update1,
        out,
    )
    got1 = exchange(send1, ("x0", "front"))
    side2 = pl.pallas_call(
        sum2_kernel,
        in_specs=[SMEM, VMEM, VMEM],
        out_specs=VMEM,
        out_shape=struct((RHS, NODES2 * SHARE2), bf16),
        compiler_params=params(24),
        name="sum2",
    )(where, got1, rhs2)
    all2 = lax.all_gather(side2, "front", axis=0, tiled=False)
    out, send2 = pl.pallas_call(
        level2_kernel,
        in_specs=[SMEM, VMEM, VMEM, VMEM, VMEM, HBM],
        out_specs=[HBM, VMEM],
        out_shape=[
            struct((RHS, ROWS), f32),
            struct((2 * FRONT, NODES3 + 1, RHS + META, 128), bf16),
        ],
        scratch_shapes=[
            pltpu.VMEM((RHS, NODES2 * SHARE2), f32),
            pltpu.VMEM((2 * NODES3, RHS, BORDER2), f32),
            pltpu.VMEM((2 * NODES3, 8, BORDER2), i32),
            pltpu.SemaphoreType.DMA,
        ],
        input_output_aliases={5: 0},
        compiler_params=params(24),
        name="level2",
    )(
        level2_parent_node,
        all2,
        level2_parent_rows,
        level2_diagonal_inverse,
        level2_update_block,
        out,
    )
    got2 = exchange(send2, ("x1", "front"))
    side3 = pl.pallas_call(
        sum3_kernel,
        in_specs=[VMEM, VMEM],
        out_specs=VMEM,
        out_shape=struct((RHS, NODES3 * SHARE3), bf16),
        compiler_params=params(24),
        name="sum3",
    )(got2, rhs3)
    all3 = lax.all_gather(side3, "front", axis=0, tiled=False)
    return pl.pallas_call(
        level3_kernel,
        in_specs=[VMEM, VMEM, HBM],
        out_specs=HBM,
        out_shape=struct((RHS, ROWS), f32),
        scratch_shapes=[pltpu.VMEM((RHS, NODES3 * SHARE3), f32), pltpu.SemaphoreType.DMA],
        input_output_aliases={2: 0},
        compiler_params=params(24),
        name="level3",
    )(all3, level3_diagonal_inverse, out)


def solution(mesh):
    fine = Mesh(mesh.devices.reshape(4, 2, 2, 2, 4), ALL)
    return jax.shard_map(
        per_device,
        mesh=fine,
        in_specs=(
            P(None, ALL),
            P(ALL),
            P(ALL, None, None),
            P(ALL, None, None),
            P(ALL, None),
            P(ALL),
            P(ALL, None, None),
            P(ALL, None, None),
            P(ALL, None),
            P(ALL),
            P(SUBTREE, None, "front"),
            P(SUBTREE, "front", None),
            P(SUBTREE, None),
            P(SUBTREE),
            P(SUBTREE, None, "front"),
        ),
        out_specs=P(None, ALL),
        check_vma=False,
    )
```

```python
import jax
import jax.numpy as jnp
from jax import lax
from jax.experimental import pallas as pl
from jax.experimental.pallas import tpu as pltpu
from jax.sharding import Mesh, PartitionSpec as P

RHS = 64
LEAVES, LEAF, BORDER0 = 4, 512, 256
NODES1, SEP1, BORDER1 = 2, 1024, 512
NODES2, SEP2, BORDER2 = 4, 1536, 768
NODES3, SEP3 = 2, 2048
FRONT = 4
SHARE2, SHARE3 = SEP2 // FRONT, SEP3 // FRONT
PART1, PART2 = BORDER1 // FRONT, BORDER2 // FRONT
ROWS = 6656
DEVICES = 128
EACH = ROWS // DEVICES
HALF = EACH // 2
GROUP = 4
EDGE0 = LEAVES * LEAF
EDGE1 = EDGE0 + NODES1 * SEP1
EDGE2 = EDGE1 + NODES2 * SHARE2
META = 8
LOW = 256

SUBTREE = ("z", "x1", "x0", "core")
ALL = SUBTREE + ("front",)

bf16, f32, i32 = jnp.bfloat16, jnp.float32, jnp.int32
VMEM = pl.BlockSpec(memory_space=pltpu.VMEM)
SMEM = pl.BlockSpec(memory_space=pltpu.SMEM)
HBM = pl.BlockSpec(memory_space=pltpu.HBM)


def params(mib):
    return pltpu.CompilerParams(vmem_limit_bytes=mib << 20)


def in_hbm(x):
    return pltpu.with_memory_space_constraint(x, pltpu.HBM)


def struct(shape, dtype):
    return jax.ShapeDtypeStruct(shape, dtype)


def mm(a, b):
    return jnp.dot(a, b, preferred_element_type=f32)


def mm_nt(a, b):
    return lax.dot_general(a, b, (((1,), (1,)), ((), ())), preferred_element_type=f32)


def place(terms, high, low, blocks):
    n = low.shape[1]
    ids = lax.broadcasted_iota(i32, (LOW, n), 0).astype(f32)
    picks = jnp.where(ids == low, 1.0, 0.0).astype(bf16)
    lhs = [jnp.where(high == h, t, 0.0).astype(bf16) for t in terms for h in range(blocks)]
    found = mm_nt(jnp.concatenate(lhs, axis=0), picks)
    out = []
    for h in range(blocks):
        parts = [
            found[(t * blocks + h) * RHS : (t * blocks + h + 1) * RHS] for t in range(len(terms))
        ]
        out.append(sum(parts[1:], parts[0]))
    return jnp.concatenate(out, axis=1)


def digits(targets, flag):
    n = targets.shape[1]
    ids = lax.broadcasted_iota(i32, (META, n), 0)
    high = jnp.broadcast_to(targets >> 8, (META, n))
    low = jnp.broadcast_to(targets & (LOW - 1), (META, n))
    rows = jnp.where(ids == 0, high, jnp.where(ids == 1, low, flag))
    return rows.astype(f32).astype(bf16)


def undigits(meta):
    m = meta.astype(f32)
    return m[0:1], m[1:2], m[2:3]


def tall_kernel(wide_ref, tall_ref):
    for b in range(ROWS // 512):
        wide = wide_ref[:, b * 512 : (b + 1) * 512]
        tall_ref[b * 512 : (b + 1) * 512, :] = jnp.concatenate([wide, wide], axis=0).T


def pick_kernel(asked_ref, tall_ref, out_hbm, buf, narrow, sem):
    low = lax.broadcasted_iota(i32, (1, 128), 1) < RHS

    def gather(g, carry):
        base = pl.multiple_of(g * (GROUP * HALF), 8)
        for e in range(GROUP):
            d = g * GROUP + e
            for k in range(HALF):
                first = tall_ref[pl.ds(asked_ref[d, k], 1), :]
                second = tall_ref[pl.ds(asked_ref[d, k + HALF], 1), :]
                buf[pl.ds(base + (e * HALF + k), 1), :] = jnp.where(low, first, second)
        return carry

    lax.fori_loop(0, DEVICES // GROUP, gather, 0)
    narrow[...] = buf[...].astype(bf16)
    store = pltpu.make_async_copy(narrow, out_hbm, sem)
    store.start()
    store.wait()


def restore(order_ref, arrived_ref, flat, turned, tall_ref):
    piece = arrived_ref[...].astype(f32)
    flat[...] = piece
    turned[...] = pltpu.roll(piece, RHS, 1)

    def scatter(g, carry):
        base = pl.multiple_of(g * (GROUP * HALF), 8)
        for e in range(GROUP):
            at = (g * GROUP + e) * EACH
            for k in range(HALF):
                row = pl.ds(base + (e * HALF + k), 1)
                tall_ref[pl.ds(order_ref[at + k], 1), :] = flat[row, :]
                tall_ref[pl.ds(order_ref[at + k + HALF], 1), :] = turned[row, :]
        return carry

    lax.fori_loop(0, DEVICES // GROUP, scatter, 0)


def leaf_kernel(
    order_ref,
    parent_ref,
    where_ref,
    arrived_ref,
    rows_ref,
    inverse_hbm,
    update_hbm,
    inverse1_hbm,
    update1_hbm,
    out_hbm,
    send_ref,
    rhs1_ref,
    rhs2_ref,
    rhs3_ref,
    inverse1_ref,
    update1_ref,
    flat,
    turned,
    tall,
    inverse_ref,
    update_ref,
    sol_ref,
    kept_ref,
    kept_rows,
    sems,
):
    load_inverse = pltpu.make_async_copy(inverse_hbm, inverse_ref, sems.at[0])
    load_update = pltpu.make_async_copy(update_hbm, update_ref, sems.at[1])
    load_inverse1 = pltpu.make_async_copy(inverse1_hbm, inverse1_ref, sems.at[3])
    load_update1 = pltpu.make_async_copy(update1_hbm, update1_ref, sems.at[4])
    load_inverse.start()
    load_update.start()
    load_inverse1.start()
    load_update1.start()
    restore(order_ref, arrived_ref, flat, turned, tall)
    load_inverse.wait()
    load_update.wait()
    sols, terms = [], []
    for n in range(LEAVES):
        lhs = tall[n * LEAF : (n + 1) * LEAF, :].T[:RHS].astype(bf16)
        sols.append(mm(lhs, inverse_ref[n]))
    for n in range(LEAVES):
        sol_ref[:, n * LEAF : (n + 1) * LEAF] = sols[n]
        terms.append(mm(sols[n].astype(bf16), update_ref[n]).astype(bf16))
    rhs2_ref[...] = tall[EDGE1:EDGE2, :].T[:RHS]
    rhs3_ref[...] = tall[EDGE2:ROWS, :].T[:RHS]
    core = where_ref[0]
    for n in range(LEAVES):
        node = parent_ref[n]
        slot = node & 1
        away = ((node >> 3) & 1) != core
        targets = rows_ref[n : n + 1, :]

        @pl.when(away)
        def _():
            send_ref[slot, 0:RHS, :] = terms[n]
            send_ref[slot, RHS : RHS + META, :] = digits(targets, 0)

        @pl.when(jnp.logical_not(away))
        def _():
            kept_ref[slot] = terms[n]
            kept_rows[slot] = jnp.broadcast_to(targets, (8, BORDER0))

    store = pltpu.make_async_copy(sol_ref, out_hbm.at[:, 0:EDGE0], sems.at[2])
    store.start()
    for q in range(NODES1):
        rhs = tall[EDGE0 + q * SEP1 : EDGE0 + (q + 1) * SEP1, :].T[:RHS]
        rows = kept_rows[q, 0:1, :]
        high, low = (rows >> 8).astype(f32), (rows & (LOW - 1)).astype(f32)
        rhs1_ref[q] = rhs - place([kept_ref[q].astype(f32)], high, low, SEP1 // LOW)
    store.wait()
    load_inverse1.wait()
    load_update1.wait()


def level1_kernel(
    parent_ref,
    got_ref,
    rhs_ref,
    rows_ref,
    inverse_ref,
    update_ref,
    out_in,
    out_hbm,
    send_ref,
    sol_ref,
    sem,
):
    del out_in
    for n in range(NODES1):
        high, low, _ = undigits(got_ref[n, RHS : RHS + META, :])
        got = got_ref[n, 0:RHS, :].astype(f32)
        rhs = rhs_ref[n] - place([got], high, low, SEP1 // LOW)
        sol = mm(rhs.astype(bf16), inverse_ref[n])
        sol_ref[:, n * SEP1 : (n + 1) * SEP1] = sol
        terms = mm(sol.astype(bf16), update_ref[n]).astype(bf16)
        node = parent_ref[n]
        slot = node & 3
        side = (node >> 3) & 1
        for f in range(FRONT):
            own = slice(f * PART1, (f + 1) * PART1)
            targets = rows_ref[n : n + 1, own] + (slot * SHARE2 - f * SHARE2)
            meta = digits(targets, side)
            for x in range(2):
                send_ref[x * FRONT + f, n, 0:RHS, :] = terms[:, own]
                send_ref[x * FRONT + f, n, RHS : RHS + META, :] = meta
    store = pltpu.make_async_copy(sol_ref, out_hbm.at[:, EDGE0:EDGE1], sem)
    store.start()
    store.wait()


def sum2_kernel(where_ref, got_ref, rhs_ref, out_ref):
    x0 = where_ref[1].astype(f32)
    terms, highs, lows = [], [], []
    for e in range(2 * FRONT):
        for n in range(NODES1):
            terms.append(got_ref[e, n, 0:RHS, :].astype(f32))
            high, low, side = undigits(got_ref[e, n, RHS : RHS + META, :])
            highs.append(jnp.where(side == x0, high, -1.0))
            lows.append(low)
    total = place(
        [jnp.concatenate(terms, axis=1)],
        jnp.concatenate(highs, axis=1),
        jnp.concatenate(lows, axis=1),
        NODES2 * SHARE2 // LOW,
    )
    out_ref[...] = (rhs_ref[...] - total).astype(bf16)


def level2_kernel(
    parent_ref,
    rhs_ref,
    rows_ref,
    inverse_ref,
    update_ref,
    out_in,
    out_hbm,
    send_ref,
    sol_ref,
    terms_ref,
    terms_rows,
    sem,
):
    del out_in
    for c in range(NODES2):
        own = slice(c * SHARE2, (c + 1) * SHARE2)
        lhs = jnp.concatenate([rhs_ref[g, :, own] for g in range(FRONT)], axis=1)
        sol = mm(lhs, inverse_ref[c])
        sol_ref[:, own] = sol
        node = parent_ref[c]
        slot = ((node >> 3) & 1) * NODES3 + (node & 1)
        terms_ref[slot] = mm(sol.astype(bf16), update_ref[c])
        terms_rows[slot] = jnp.broadcast_to(rows_ref[c : c + 1, :], (8, BORDER2))
    store = pltpu.make_async_copy(sol_ref, out_hbm.at[:, EDGE1:EDGE2], sem)
    store.start()
    for x in range(2):
        for f in range(FRONT):
            ends, end_rows = [], []
            for q in range(NODES3):
                at = x * NODES3 + q
                terms = terms_ref[at, :, f * PART2 : (f + 1) * PART2]
                rows = terms_rows[at, 0:1, f * PART2 : (f + 1) * PART2] + (q - f) * SHARE3
                send_ref[x * FRONT + f, q, 0:RHS, :] = terms[:, :128].astype(bf16)
                send_ref[x * FRONT + f, q, RHS : RHS + META, :] = digits(rows[:, :128], 0)
                ends.append(terms[:, 128:])
                end_rows.append(rows[:, 128:])
            end = jnp.concatenate(ends, axis=1).astype(bf16)
            send_ref[x * FRONT + f, NODES3, 0:RHS, :] = end
            send_ref[x * FRONT + f, NODES3, RHS : RHS + META, :] = digits(
                jnp.concatenate(end_rows, axis=1), 0
            )
    store.wait()


def sum3_kernel(got_ref, rhs_ref, out_ref):
    parts, highs, lows = [], [], []
    for x in range(2):
        for b in range(NODES3 + 1):
            pieces = [got_ref[x * FRONT + g, b, 0:RHS, :].astype(f32) for g in range(FRONT)]
            parts.append((pieces[0] + pieces[1]) + (pieces[2] + pieces[3]))
            high, low, _ = undigits(got_ref[x * FRONT, b, RHS : RHS + META, :])
            highs.append(high)
            lows.append(low)
    part = jnp.concatenate(parts, axis=1)
    coarse = part.astype(bf16).astype(f32)
    total = place(
        [coarse, part - coarse],
        jnp.concatenate(highs, axis=1),
        jnp.concatenate(lows, axis=1),
        NODES3 * SHARE3 // LOW,
    )
    out_ref[...] = (rhs_ref[...] - total).astype(bf16)


def level3_kernel(rhs_ref, inverse_ref, out_in, out_hbm, sol_ref, sem):
    del out_in
    for c in range(NODES3):
        own = slice(c * SHARE3, (c + 1) * SHARE3)
        lhs = jnp.concatenate([rhs_ref[g, :, own] for g in range(FRONT)], axis=1)
        sol_ref[:, own] = mm(lhs, inverse_ref[c])
    store = pltpu.make_async_copy(sol_ref, out_hbm.at[:, EDGE2:ROWS], sem)
    store.start()
    store.wait()


def exchange(block, axes):
    return lax.all_to_all(block, axes, split_axis=0, concat_axis=0, tiled=True)


def per_device(
    right_hand_sides,
    elimination_natural_index,
    leaf_diagonal_inverse,
    leaf_update_block,
    leaf_parent_rows,
    leaf_parent_node,
    level1_diagonal_inverse,
    level1_update_block,
    level1_parent_rows,
    level1_parent_node,
    level2_diagonal_inverse,
    level2_update_block,
    level2_parent_rows,
    level2_parent_node,
    level3_diagonal_inverse,
):
    where = jnp.stack([lax.axis_index("core"), lax.axis_index("x0")]).astype(i32)
    by_source, order = lax.sort(
        (elimination_natural_index, lax.iota(i32, ROWS)), num_keys=1, is_stable=False
    )
    asked = exchange((by_source % ROWS).reshape(DEVICES, EACH), ALL)
    tall = pl.pallas_call(
        tall_kernel,
        in_specs=[VMEM],
        out_specs=VMEM,
        out_shape=struct((ROWS, 128), f32),
        compiler_params=params(8),
        name="tall",
    )(right_hand_sides)
    picked = pl.pallas_call(
        pick_kernel,
        in_specs=[SMEM, VMEM],
        out_specs=HBM,
        out_shape=pltpu.HBM((DEVICES * HALF, 128), bf16),
        scratch_shapes=[
            pltpu.VMEM((DEVICES * HALF, 128), f32),
            pltpu.VMEM((DEVICES * HALF, 128), bf16),
            pltpu.SemaphoreType.DMA,
        ],
        compiler_params=params(16),
        name="pick",
    )(asked, tall)
    arrived = exchange(picked.reshape(DEVICES, HALF // 2, 2, 128), ALL)
    out, send0, rhs1, rhs2, rhs3, inverse1, update1 = pl.pallas_call(
        leaf_kernel,
        in_specs=[SMEM, SMEM, SMEM, VMEM, VMEM, HBM, HBM, HBM, HBM],
        out_specs=[HBM, VMEM, VMEM, VMEM, VMEM, VMEM, VMEM],
        out_shape=[
            struct((RHS, ROWS), f32),
            struct((NODES1, RHS + META, BORDER0), bf16),
            struct((NODES1, RHS, SEP1), f32),
            struct((RHS, NODES2 * SHARE2), f32),
            struct((RHS, NODES3 * SHARE3), f32),
            struct((NODES1, SEP1, SEP1), bf16),
            struct((NODES1, SEP1, BORDER1), bf16),
        ],
        scratch_shapes=[
            pltpu.VMEM((DEVICES * HALF, 128), f32),
            pltpu.VMEM((DEVICES * HALF, 128), f32),
            pltpu.VMEM((ROWS, 128), f32),
            pltpu.VMEM((LEAVES, LEAF, LEAF), bf16),
            pltpu.VMEM((LEAVES, LEAF, BORDER0), bf16),
            pltpu.VMEM((RHS, EDGE0), f32),
            pltpu.VMEM((NODES1, RHS, BORDER0), bf16),
            pltpu.VMEM((NODES1, 8, BORDER0), i32),
            pltpu.SemaphoreType.DMA((5,)),
        ],
        compiler_params=params(24),
        name="leaf",
    )(
        order,
        leaf_parent_node,
        where,
        arrived.reshape(DEVICES * HALF, 128),
        leaf_parent_rows,
        in_hbm(leaf_diagonal_inverse),
        in_hbm(leaf_update_block),
        in_hbm(level1_diagonal_inverse),
        in_hbm(level1_update_block),
    )
    got0 = lax.ppermute(send0, "core", [(0, 1), (1, 0)])
    out, send1 = pl.pallas_call(
        level1_kernel,
        in_specs=[SMEM, VMEM, VMEM, VMEM, VMEM, VMEM, HBM],
        out_specs=[HBM, VMEM],
        out_shape=[
            struct((RHS, ROWS), f32),
            struct((2 * FRONT, NODES1, RHS + META, PART1), bf16),
        ],
        scratch_shapes=[pltpu.VMEM((RHS, NODES1 * SEP1), f32), pltpu.SemaphoreType.DMA],
        input_output_aliases={6: 0},
        compiler_params=params(24),
        name="level1",
    )(
        level1_parent_node,
        got0,
        rhs1,
        level1_parent_rows,
        inverse1,
        update1,
        out,
    )
    got1 = exchange(send1, ("x0", "front"))
    side2 = pl.pallas_call(
        sum2_kernel,
        in_specs=[SMEM, VMEM, VMEM],
        out_specs=VMEM,
        out_shape=struct((RHS, NODES2 * SHARE2), bf16),
        compiler_params=params(24),
        name="sum2",
    )(where, got1, rhs2)
    all2 = lax.all_gather(side2, "front", axis=0, tiled=False)
    out, send2 = pl.pallas_call(
        level2_kernel,
        in_specs=[SMEM, VMEM, VMEM, VMEM, VMEM, HBM],
        out_specs=[HBM, VMEM],
        out_shape=[
            struct((RHS, ROWS), f32),
            struct((2 * FRONT, NODES3 + 1, RHS + META, 128), bf16),
        ],
        scratch_shapes=[
            pltpu.VMEM((RHS, NODES2 * SHARE2), f32),
            pltpu.VMEM((2 * NODES3, RHS, BORDER2), f32),
            pltpu.VMEM((2 * NODES3, 8, BORDER2), i32),
            pltpu.SemaphoreType.DMA,
        ],
        input_output_aliases={5: 0},
        compiler_params=params(24),
        name="level2",
    )(
        level2_parent_node,
        all2,
        level2_parent_rows,
        level2_diagonal_inverse,
        level2_update_block,
        out,
    )
    got2 = exchange(send2, ("x1", "front"))
    side3 = pl.pallas_call(
        sum3_kernel,
        in_specs=[VMEM, VMEM],
        out_specs=VMEM,
        out_shape=struct((RHS, NODES3 * SHARE3), bf16),
        compiler_params=params(24),
        name="sum3",
    )(got2, rhs3)
    all3 = lax.all_gather(side3, "front", axis=0, tiled=False)
    return pl.pallas_call(
        level3_kernel,
        in_specs=[VMEM, VMEM, HBM],
        out_specs=HBM,
        out_shape=struct((RHS, ROWS), f32),
        scratch_shapes=[pltpu.VMEM((RHS, NODES3 * SHARE3), f32), pltpu.SemaphoreType.DMA],
        input_output_aliases={2: 0},
        compiler_params=params(24),
        name="level3",
    )(all3, level3_diagonal_inverse, out)


def solution(mesh):
    fine = Mesh(mesh.devices.reshape(4, 2, 2, 2, 4), ALL)
    return jax.shard_map(
        per_device,
        mesh=fine,
        in_specs=(
            P(None, ALL),
            P(ALL),
            P(ALL, None, None),
            P(ALL, None, None),
            P(ALL, None),
            P(ALL),
            P(ALL, None, None),
            P(ALL, None, None),
            P(ALL, None),
            P(ALL),
            P(SUBTREE, None, "front"),
            P(SUBTREE, "front", None),
            P(SUBTREE, None),
            P(SUBTREE),
            P(SUBTREE, None, "front"),
        ),
        out_specs=P(None, ALL),
        check_vma=False,
    )
```

```python
import jax
import jax.numpy as jnp
from jax import lax
from jax.experimental import pallas as pl
from jax.experimental.pallas import tpu as pltpu
from jax.sharding import Mesh, PartitionSpec as P

RHS = 64
LEAVES, LEAF, BORDER0 = 4, 512, 256
NODES1, SEP1, BORDER1 = 2, 1024, 512
NODES2, SEP2, BORDER2 = 4, 1536, 768
NODES3, SEP3 = 2, 2048
FRONT = 4
SHARE2, SHARE3 = SEP2 // FRONT, SEP3 // FRONT
PART1, PART2 = BORDER1 // FRONT, BORDER2 // FRONT
ROWS = 6656
DEVICES = 128
EACH = ROWS // DEVICES
HALF = EACH // 2
LANES = 128
BLOCKS = ROWS // LANES
PAIRS = DEVICES * HALF
GROUP = 4
EDGE0 = LEAVES * LEAF
EDGE1 = EDGE0 + NODES1 * SEP1
EDGE2 = EDGE1 + NODES2 * SHARE2
META = 8
LOW = 256

SUBTREE = ("z", "x1", "x0", "core")
ALL = SUBTREE + ("front",)

bf16, f32, i32 = jnp.bfloat16, jnp.float32, jnp.int32
VMEM = pl.BlockSpec(memory_space=pltpu.VMEM)
SMEM = pl.BlockSpec(memory_space=pltpu.SMEM)
HBM = pl.BlockSpec(memory_space=pltpu.HBM)


def params(mib):
    return pltpu.CompilerParams(vmem_limit_bytes=mib << 20)


def in_hbm(x):
    return pltpu.with_memory_space_constraint(x, pltpu.HBM)


def struct(shape, dtype):
    return jax.ShapeDtypeStruct(shape, dtype)


def mm(a, b):
    return jnp.dot(a, b, preferred_element_type=f32)


def mm_nt(a, b):
    return lax.dot_general(a, b, (((1,), (1,)), ((), ())), preferred_element_type=f32)


def place(terms, high, low, blocks):
    n = low.shape[1]
    ids = lax.broadcasted_iota(i32, (LOW, n), 0).astype(f32)
    picks = jnp.where(ids == low, 1.0, 0.0).astype(bf16)
    lhs = [jnp.where(high == h, t, 0.0).astype(bf16) for t in terms for h in range(blocks)]
    found = mm_nt(jnp.concatenate(lhs, axis=0), picks)
    out = []
    for h in range(blocks):
        parts = [
            found[(t * blocks + h) * RHS : (t * blocks + h + 1) * RHS] for t in range(len(terms))
        ]
        out.append(sum(parts[1:], parts[0]))
    return jnp.concatenate(out, axis=1)


def digits(targets, flag):
    n = targets.shape[1]
    ids = lax.broadcasted_iota(i32, (META, n), 0)
    high = jnp.broadcast_to(targets >> 8, (META, n))
    low = jnp.broadcast_to(targets & (LOW - 1), (META, n))
    rows = jnp.where(ids == 0, high, jnp.where(ids == 1, low, flag))
    return rows.astype(f32).astype(bf16)


def undigits(meta):
    m = meta.astype(f32)
    return m[0:1], m[1:2], m[2:3]


def tall_kernel(wide_ref, tall_ref):
    for b in range(ROWS // 512):
        wide = wide_ref[:, b * 512 : (b + 1) * 512]
        tall_ref[b * 512 : (b + 1) * 512, :] = jnp.concatenate([wide, wide], axis=0).T


def pick_kernel(asked_ref, tall_ref, out_hbm, buf, narrow, sem):
    low = lax.broadcasted_iota(i32, (1, 128), 1) < RHS

    def gather(g, carry):
        base = pl.multiple_of(g * (GROUP * HALF), 8)
        for e in range(GROUP):
            d = g * GROUP + e
            for k in range(HALF):
                first = tall_ref[pl.ds(asked_ref[d, k], 1), :]
                second = tall_ref[pl.ds(asked_ref[d, k + HALF], 1), :]
                buf[pl.ds(base + (e * HALF + k), 1), :] = jnp.where(low, first, second)
        return carry

    lax.fori_loop(0, DEVICES // GROUP, gather, 0)
    narrow[...] = buf[...].astype(bf16)
    store = pltpu.make_async_copy(narrow, out_hbm, sem)
    store.start()
    store.wait()


def rank_kernel(index_ref, asked_ref, slot_ref):
    index = index_ref[...].astype(f32)
    source = jnp.floor((index + 0.5) * (1.0 / ROWS))
    local = index - source * ROWS
    high = jnp.floor(local * (1.0 / LANES))
    low = local - high * LANES
    rows = lax.broadcasted_iota(i32, (LANES, 2 * LANES), 0)
    columns = lax.broadcasted_iota(i32, (LANES, 2 * LANES), 1)
    before = jnp.where((rows < columns) | (columns >= LANES), 1.0, 0.0).astype(bf16)
    devices = lax.broadcasted_iota(i32, (DEVICES, LANES), 0).astype(f32)
    ranks = lax.broadcasted_iota(i32, (64, LANES), 0).astype(f32)
    seen = jnp.zeros((DEVICES, LANES), f32)
    asked = jnp.zeros((DEVICES, LANES), f32)
    for b in range(BLOCKS):
        row = slice(b, b + 1)
        mine = jnp.where(devices == source[row], 1.0, 0.0)
        mine16 = mine.astype(bf16)
        counts = mm(mine16, before)
        rank = jnp.sum(mine * (seen + counts[:, :LANES]), axis=0, keepdims=True)
        seen = seen + counts[:, LANES:]
        at = ranks == rank
        values = [jnp.where(at, high[row], 0.0), jnp.where(at, low[row], 0.0)]
        asked = asked + mm_nt(mine16, jnp.concatenate(values, axis=0).astype(bf16))
        slot = source[row] * HALF + jnp.where(rank < HALF, rank, rank + (PAIRS - HALF))
        slot_ref[row, :] = slot.astype(i32)
    asked_ref[...] = (asked * LANES + pltpu.roll(asked, 64, 1)).astype(i32)


def restore(slot_ref, arrived_ref, both, tall_ref):
    piece = arrived_ref[...].astype(f32)
    both[0:PAIRS, :] = piece
    both[PAIRS : 2 * PAIRS, :] = pltpu.roll(piece, RHS, 1)

    def gather(r, carry):
        base = pl.multiple_of(r * LANES, LANES)
        for k in range(LANES):
            tall_ref[pl.ds(base + k, 1), :] = both[pl.ds(slot_ref[r, k], 1), :]
        return carry

    lax.fori_loop(0, BLOCKS, gather, 0)


def leaf_kernel(
    slot_ref,
    parent_ref,
    where_ref,
    arrived_ref,
    rows_ref,
    inverse_hbm,
    update_hbm,
    inverse1_hbm,
    update1_hbm,
    out_hbm,
    send_ref,
    rhs1_ref,
    rhs2_ref,
    rhs3_ref,
    inverse1_ref,
    update1_ref,
    both,
    tall,
    inverse_ref,
    update_ref,
    sol_ref,
    kept_ref,
    kept_rows,
    sems,
):
    load_inverse = pltpu.make_async_copy(inverse_hbm, inverse_ref, sems.at[0])
    load_update = pltpu.make_async_copy(update_hbm, update_ref, sems.at[1])
    load_inverse1 = pltpu.make_async_copy(inverse1_hbm, inverse1_ref, sems.at[3])
    load_update1 = pltpu.make_async_copy(update1_hbm, update1_ref, sems.at[4])
    load_inverse.start()
    load_update.start()
    load_inverse1.start()
    load_update1.start()
    restore(slot_ref, arrived_ref, both, tall)
    load_inverse.wait()
    load_update.wait()
    sols, terms = [], []
    for n in range(LEAVES):
        lhs = tall[n * LEAF : (n + 1) * LEAF, :].T[:RHS].astype(bf16)
        sols.append(mm(lhs, inverse_ref[n]))
    for n in range(LEAVES):
        sol_ref[:, n * LEAF : (n + 1) * LEAF] = sols[n]
        terms.append(mm(sols[n].astype(bf16), update_ref[n]).astype(bf16))
    rhs2_ref[...] = tall[EDGE1:EDGE2, :].T[:RHS]
    rhs3_ref[...] = tall[EDGE2:ROWS, :].T[:RHS]
    core = where_ref[0]
    for n in range(LEAVES):
        node = parent_ref[n]
        slot = node & 1
        away = ((node >> 3) & 1) != core
        targets = rows_ref[n : n + 1, :]

        @pl.when(away)
        def _():
            send_ref[slot, 0:RHS, :] = terms[n]
            send_ref[slot, RHS : RHS + META, :] = digits(targets, 0)

        @pl.when(jnp.logical_not(away))
        def _():
            kept_ref[slot] = terms[n]
            kept_rows[slot] = jnp.broadcast_to(targets, (8, BORDER0))

    store = pltpu.make_async_copy(sol_ref, out_hbm.at[:, 0:EDGE0], sems.at[2])
    store.start()
    for q in range(NODES1):
        rhs = tall[EDGE0 + q * SEP1 : EDGE0 + (q + 1) * SEP1, :].T[:RHS]
        rows = kept_rows[q, 0:1, :]
        high, low = (rows >> 8).astype(f32), (rows & (LOW - 1)).astype(f32)
        rhs1_ref[q] = rhs - place([kept_ref[q].astype(f32)], high, low, SEP1 // LOW)
    store.wait()
    load_inverse1.wait()
    load_update1.wait()


def level1_kernel(
    parent_ref,
    got_ref,
    rhs_ref,
    rows_ref,
    inverse_ref,
    update_ref,
    out_in,
    out_hbm,
    send_ref,
    sol_ref,
    sem,
):
    del out_in
    for n in range(NODES1):
        high, low, _ = undigits(got_ref[n, RHS : RHS + META, :])
        got = got_ref[n, 0:RHS, :].astype(f32)
        rhs = rhs_ref[n] - place([got], high, low, SEP1 // LOW)
        sol = mm(rhs.astype(bf16), inverse_ref[n])
        sol_ref[:, n * SEP1 : (n + 1) * SEP1] = sol
        terms = mm(sol.astype(bf16), update_ref[n]).astype(bf16)
        node = parent_ref[n]
        slot = node & 3
        side = (node >> 3) & 1
        for f in range(FRONT):
            own = slice(f * PART1, (f + 1) * PART1)
            targets = rows_ref[n : n + 1, own] + (slot * SHARE2 - f * SHARE2)
            meta = digits(targets, side)
            for x in range(2):
                send_ref[x * FRONT + f, n, 0:RHS, :] = terms[:, own]
                send_ref[x * FRONT + f, n, RHS : RHS + META, :] = meta
    store = pltpu.make_async_copy(sol_ref, out_hbm.at[:, EDGE0:EDGE1], sem)
    store.start()
    store.wait()


def sum2_kernel(where_ref, got_ref, rhs_ref, out_ref):
    x0 = where_ref[1].astype(f32)
    terms, highs, lows = [], [], []
    for e in range(2 * FRONT):
        for n in range(NODES1):
            terms.append(got_ref[e, n, 0:RHS, :].astype(f32))
            high, low, side = undigits(got_ref[e, n, RHS : RHS + META, :])
            highs.append(jnp.where(side == x0, high, -1.0))
            lows.append(low)
    total = place(
        [jnp.concatenate(terms, axis=1)],
        jnp.concatenate(highs, axis=1),
        jnp.concatenate(lows, axis=1),
        NODES2 * SHARE2 // LOW,
    )
    out_ref[...] = (rhs_ref[...] - total).astype(bf16)


def level2_kernel(
    parent_ref,
    rhs_ref,
    rows_ref,
    inverse_ref,
    update_ref,
    out_in,
    out_hbm,
    send_ref,
    sol_ref,
    terms_ref,
    terms_rows,
    sem,
):
    del out_in
    for c in range(NODES2):
        own = slice(c * SHARE2, (c + 1) * SHARE2)
        lhs = jnp.concatenate([rhs_ref[g, :, own] for g in range(FRONT)], axis=1)
        sol = mm(lhs, inverse_ref[c])
        sol_ref[:, own] = sol
        node = parent_ref[c]
        slot = ((node >> 3) & 1) * NODES3 + (node & 1)
        terms_ref[slot] = mm(sol.astype(bf16), update_ref[c])
        terms_rows[slot] = jnp.broadcast_to(rows_ref[c : c + 1, :], (8, BORDER2))
    store = pltpu.make_async_copy(sol_ref, out_hbm.at[:, EDGE1:EDGE2], sem)
    store.start()
    for x in range(2):
        for f in range(FRONT):
            ends, end_rows = [], []
            for q in range(NODES3):
                at = x * NODES3 + q
                terms = terms_ref[at, :, f * PART2 : (f + 1) * PART2]
                rows = terms_rows[at, 0:1, f * PART2 : (f + 1) * PART2] + (q - f) * SHARE3
                send_ref[x * FRONT + f, q, 0:RHS, :] = terms[:, :128].astype(bf16)
                send_ref[x * FRONT + f, q, RHS : RHS + META, :] = digits(rows[:, :128], 0)
                ends.append(terms[:, 128:])
                end_rows.append(rows[:, 128:])
            end = jnp.concatenate(ends, axis=1).astype(bf16)
            send_ref[x * FRONT + f, NODES3, 0:RHS, :] = end
            send_ref[x * FRONT + f, NODES3, RHS : RHS + META, :] = digits(
                jnp.concatenate(end_rows, axis=1), 0
            )
    store.wait()


def sum3_kernel(got_ref, rhs_ref, out_ref):
    parts, highs, lows = [], [], []
    for x in range(2):
        for b in range(NODES3 + 1):
            pieces = [got_ref[x * FRONT + g, b, 0:RHS, :].astype(f32) for g in range(FRONT)]
            parts.append((pieces[0] + pieces[1]) + (pieces[2] + pieces[3]))
            high, low, _ = undigits(got_ref[x * FRONT, b, RHS : RHS + META, :])
            highs.append(high)
            lows.append(low)
    part = jnp.concatenate(parts, axis=1)
    coarse = part.astype(bf16).astype(f32)
    total = place(
        [coarse, part - coarse],
        jnp.concatenate(highs, axis=1),
        jnp.concatenate(lows, axis=1),
        NODES3 * SHARE3 // LOW,
    )
    out_ref[...] = (rhs_ref[...] - total).astype(bf16)


def level3_kernel(rhs_ref, inverse_ref, out_in, out_hbm, sol_ref, sem):
    del out_in
    for c in range(NODES3):
        own = slice(c * SHARE3, (c + 1) * SHARE3)
        lhs = jnp.concatenate([rhs_ref[g, :, own] for g in range(FRONT)], axis=1)
        sol_ref[:, own] = mm(lhs, inverse_ref[c])
    store = pltpu.make_async_copy(sol_ref, out_hbm.at[:, EDGE2:ROWS], sem)
    store.start()
    store.wait()


def exchange(block, axes):
    return lax.all_to_all(block, axes, split_axis=0, concat_axis=0, tiled=True)


def per_device(
    right_hand_sides,
    elimination_natural_index,
    leaf_diagonal_inverse,
    leaf_update_block,
    leaf_parent_rows,
    leaf_parent_node,
    level1_diagonal_inverse,
    level1_update_block,
    level1_parent_rows,
    level1_parent_node,
    level2_diagonal_inverse,
    level2_update_block,
    level2_parent_rows,
    level2_parent_node,
    level3_diagonal_inverse,
):
    where = jnp.stack([lax.axis_index("core"), lax.axis_index("x0")]).astype(i32)
    requests, slot = pl.pallas_call(
        rank_kernel,
        in_specs=[VMEM],
        out_specs=[VMEM, VMEM],
        out_shape=[struct((DEVICES, LANES), i32), struct((BLOCKS, LANES), i32)],
        compiler_params=params(6),
        name="rank",
    )(elimination_natural_index.reshape(BLOCKS, LANES))
    asked = exchange(requests.reshape(DEVICES, 1, LANES), ALL).reshape(DEVICES, LANES)
    tall = pl.pallas_call(
        tall_kernel,
        in_specs=[VMEM],
        out_specs=VMEM,
        out_shape=struct((ROWS, 128), f32),
        compiler_params=params(8),
        name="tall",
    )(right_hand_sides)
    picked = pl.pallas_call(
        pick_kernel,
        in_specs=[SMEM, VMEM],
        out_specs=HBM,
        out_shape=pltpu.HBM((DEVICES * HALF, 128), bf16),
        scratch_shapes=[
            pltpu.VMEM((DEVICES * HALF, 128), f32),
            pltpu.VMEM((DEVICES * HALF, 128), bf16),
            pltpu.SemaphoreType.DMA,
        ],
        compiler_params=params(16),
        name="pick",
    )(asked, tall)
    arrived = exchange(picked.reshape(DEVICES, HALF // 2, 2, 128), ALL)
    out, send0, rhs1, rhs2, rhs3, inverse1, update1 = pl.pallas_call(
        leaf_kernel,
        in_specs=[SMEM, SMEM, SMEM, VMEM, VMEM, HBM, HBM, HBM, HBM],
        out_specs=[HBM, VMEM, VMEM, VMEM, VMEM, VMEM, VMEM],
        out_shape=[
            struct((RHS, ROWS), f32),
            struct((NODES1, RHS + META, BORDER0), bf16),
            struct((NODES1, RHS, SEP1), f32),
            struct((RHS, NODES2 * SHARE2), f32),
            struct((RHS, NODES3 * SHARE3), f32),
            struct((NODES1, SEP1, SEP1), bf16),
            struct((NODES1, SEP1, BORDER1), bf16),
        ],
        scratch_shapes=[
            pltpu.VMEM((2 * PAIRS, 128), f32),
            pltpu.VMEM((ROWS, 128), f32),
            pltpu.VMEM((LEAVES, LEAF, LEAF), bf16),
            pltpu.VMEM((LEAVES, LEAF, BORDER0), bf16),
            pltpu.VMEM((RHS, EDGE0), f32),
            pltpu.VMEM((NODES1, RHS, BORDER0), bf16),
            pltpu.VMEM((NODES1, 8, BORDER0), i32),
            pltpu.SemaphoreType.DMA((5,)),
        ],
        compiler_params=params(24),
        name="leaf",
    )(
        slot,
        leaf_parent_node,
        where,
        arrived.reshape(DEVICES * HALF, 128),
        leaf_parent_rows,
        in_hbm(leaf_diagonal_inverse),
        in_hbm(leaf_update_block),
        in_hbm(level1_diagonal_inverse),
        in_hbm(level1_update_block),
    )
    got0 = lax.ppermute(send0, "core", [(0, 1), (1, 0)])
    out, send1 = pl.pallas_call(
        level1_kernel,
        in_specs=[SMEM, VMEM, VMEM, VMEM, VMEM, VMEM, HBM],
        out_specs=[HBM, VMEM],
        out_shape=[
            struct((RHS, ROWS), f32),
            struct((2 * FRONT, NODES1, RHS + META, PART1), bf16),
        ],
        scratch_shapes=[pltpu.VMEM((RHS, NODES1 * SEP1), f32), pltpu.SemaphoreType.DMA],
        input_output_aliases={6: 0},
        compiler_params=params(24),
        name="level1",
    )(
        level1_parent_node,
        got0,
        rhs1,
        level1_parent_rows,
        inverse1,
        update1,
        out,
    )
    got1 = exchange(send1, ("x0", "front"))
    side2 = pl.pallas_call(
        sum2_kernel,
        in_specs=[SMEM, VMEM, VMEM],
        out_specs=VMEM,
        out_shape=struct((RHS, NODES2 * SHARE2), bf16),
        compiler_params=params(24),
        name="sum2",
    )(where, got1, rhs2)
    all2 = lax.all_gather(side2, "front", axis=0, tiled=False)
    out, send2 = pl.pallas_call(
        level2_kernel,
        in_specs=[SMEM, VMEM, VMEM, VMEM, VMEM, HBM],
        out_specs=[HBM, VMEM],
        out_shape=[
            struct((RHS, ROWS), f32),
            struct((2 * FRONT, NODES3 + 1, RHS + META, 128), bf16),
        ],
        scratch_shapes=[
            pltpu.VMEM((RHS, NODES2 * SHARE2), f32),
            pltpu.VMEM((2 * NODES3, RHS, BORDER2), f32),
            pltpu.VMEM((2 * NODES3, 8, BORDER2), i32),
            pltpu.SemaphoreType.DMA,
        ],
        input_output_aliases={5: 0},
        compiler_params=params(24),
        name="level2",
    )(
        level2_parent_node,
        all2,
        level2_parent_rows,
        level2_diagonal_inverse,
        level2_update_block,
        out,
    )
    got2 = exchange(send2, ("x1", "front"))
    side3 = pl.pallas_call(
        sum3_kernel,
        in_specs=[VMEM, VMEM],
        out_specs=VMEM,
        out_shape=struct((RHS, NODES3 * SHARE3), bf16),
        compiler_params=params(24),
        name="sum3",
    )(got2, rhs3)
    all3 = lax.all_gather(side3, "front", axis=0, tiled=False)
    return pl.pallas_call(
        level3_kernel,
        in_specs=[VMEM, VMEM, HBM],
        out_specs=HBM,
        out_shape=struct((RHS, ROWS), f32),
        scratch_shapes=[pltpu.VMEM((RHS, NODES3 * SHARE3), f32), pltpu.SemaphoreType.DMA],
        input_output_aliases={2: 0},
        compiler_params=params(24),
        name="level3",
    )(all3, level3_diagonal_inverse, out)


def solution(mesh):
    fine = Mesh(mesh.devices.reshape(4, 2, 2, 2, 4), ALL)
    return jax.shard_map(
        per_device,
        mesh=fine,
        in_specs=(
            P(None, ALL),
            P(ALL),
            P(ALL, None, None),
            P(ALL, None, None),
            P(ALL, None),
            P(ALL),
            P(ALL, None, None),
            P(ALL, None, None),
            P(ALL, None),
            P(ALL),
            P(SUBTREE, None, "front"),
            P(SUBTREE, "front", None),
            P(SUBTREE, None),
            P(SUBTREE),
            P(SUBTREE, None, "front"),
        ),
        out_specs=P(None, ALL),
        check_vma=False,
    )
```

```python
import jax
import jax.numpy as jnp
from jax import lax
from jax.experimental import pallas as pl
from jax.experimental.pallas import tpu as pltpu
from jax.sharding import Mesh, PartitionSpec as P

RHS = 64
LEAVES, LEAF, BORDER0 = 4, 512, 256
NODES1, SEP1, BORDER1 = 2, 1024, 512
NODES2, SEP2, BORDER2 = 4, 1536, 768
NODES3, SEP3 = 2, 2048
FRONT = 4
SHARE2, SHARE3 = SEP2 // FRONT, SEP3 // FRONT
PART1, PART2 = BORDER1 // FRONT, BORDER2 // FRONT
ROWS = 6656
DEVICES = 128
EACH = ROWS // DEVICES
HALF = EACH // 2
LANES = 128
BLOCKS = ROWS // LANES
PAIRS = DEVICES * HALF
GROUP = 4
CHUNKS = 4
EDGE0 = LEAVES * LEAF
EDGE1 = EDGE0 + NODES1 * SEP1
EDGE2 = EDGE1 + NODES2 * SHARE2
META = 8
LOW = 256

SUBTREE = ("z", "x1", "x0", "core")
ALL = SUBTREE + ("front",)

bf16, f32, i32 = jnp.bfloat16, jnp.float32, jnp.int32
VMEM = pl.BlockSpec(memory_space=pltpu.VMEM)
SMEM = pl.BlockSpec(memory_space=pltpu.SMEM)
HBM = pl.BlockSpec(memory_space=pltpu.HBM)


def params(mib):
    return pltpu.CompilerParams(vmem_limit_bytes=mib << 20)


def in_hbm(x):
    return pltpu.with_memory_space_constraint(x, pltpu.HBM)


def struct(shape, dtype):
    return jax.ShapeDtypeStruct(shape, dtype)


def mm(a, b):
    return jnp.dot(a, b, preferred_element_type=f32)


def mm_nt(a, b):
    return lax.dot_general(a, b, (((1,), (1,)), ((), ())), preferred_element_type=f32)


def place(terms, high, low, blocks):
    n = low.shape[1]
    ids = lax.broadcasted_iota(i32, (LOW, n), 0).astype(f32)
    picks = jnp.where(ids == low, 1.0, 0.0).astype(bf16)
    lhs = [jnp.where(high == h, t, 0.0).astype(bf16) for t in terms for h in range(blocks)]
    found = mm_nt(jnp.concatenate(lhs, axis=0), picks)
    out = []
    for h in range(blocks):
        parts = [
            found[(t * blocks + h) * RHS : (t * blocks + h + 1) * RHS] for t in range(len(terms))
        ]
        out.append(sum(parts[1:], parts[0]))
    return jnp.concatenate(out, axis=1)


def digits(targets, flag):
    n = targets.shape[1]
    ids = lax.broadcasted_iota(i32, (META, n), 0)
    high = jnp.broadcast_to(targets >> 8, (META, n))
    low = jnp.broadcast_to(targets & (LOW - 1), (META, n))
    rows = jnp.where(ids == 0, high, jnp.where(ids == 1, low, flag))
    return rows.astype(f32).astype(bf16)


def undigits(meta):
    m = meta.astype(f32)
    return m[0:1], m[1:2], m[2:3]


def tall_kernel(wide_hbm, tall_ref, wide_ref, sems):
    loads = []
    for b in range(ROWS // 512):
        part = slice(b * 512, (b + 1) * 512)
        loads.append(
            pltpu.make_async_copy(wide_hbm.at[:, part], wide_ref.at[:, part], sems.at[b])
        )
        loads[b].start()
    for b in range(ROWS // 512):
        part = slice(b * 512, (b + 1) * 512)
        loads[b].wait()
        wide = wide_ref[:, part]
        tall_ref[part, :] = jnp.concatenate([wide, wide], axis=0).T


def pick_kernel(asked_ref, tall_ref, out_hbm, buf, narrow, asked, sems, sem):
    low = lax.broadcasted_iota(i32, (1, 128), 1) < RHS
    step = DEVICES // CHUNKS
    loads = []
    for c in range(CHUNKS):
        part = slice(c * step, (c + 1) * step)
        loads.append(pltpu.make_async_copy(asked_ref.at[part], asked.at[part], sems.at[c]))
        loads[c].start()

    def gather(g, carry):
        base = pl.multiple_of(g * (GROUP * HALF), 8)
        for e in range(GROUP):
            d = g * GROUP + e
            for k in range(HALF):
                first = tall_ref[pl.ds(asked[d, k], 1), :]
                second = tall_ref[pl.ds(asked[d, k + HALF], 1), :]
                buf[pl.ds(base + (e * HALF + k), 1), :] = jnp.where(low, first, second)
        return carry

    for c in range(CHUNKS):
        loads[c].wait()
        lax.fori_loop(c * step // GROUP, (c + 1) * step // GROUP, gather, 0)
    narrow[...] = buf[...].astype(bf16)
    store = pltpu.make_async_copy(narrow, out_hbm, sem)
    store.start()
    store.wait()


def rank_kernel(index_ref, asked_ref, slot_ref):
    index = index_ref[...].astype(f32)
    source = jnp.floor((index + 0.5) * (1.0 / ROWS))
    local = index - source * ROWS
    high = jnp.floor(local * (1.0 / LANES))
    low = local - high * LANES
    rows = lax.broadcasted_iota(i32, (LANES, 2 * LANES), 0)
    columns = lax.broadcasted_iota(i32, (LANES, 2 * LANES), 1)
    before = jnp.where((rows < columns) | (columns >= LANES), 1.0, 0.0).astype(bf16)
    devices = lax.broadcasted_iota(i32, (DEVICES, LANES), 0).astype(f32)
    ranks = lax.broadcasted_iota(i32, (64, LANES), 0).astype(f32)
    seen = jnp.zeros((DEVICES, LANES), f32)
    asked = jnp.zeros((DEVICES, LANES), f32)
    for b in range(BLOCKS):
        row = slice(b, b + 1)
        mine = jnp.where(devices == source[row], 1.0, 0.0)
        mine16 = mine.astype(bf16)
        counts = mm(mine16, before)
        rank = jnp.sum(mine * (seen + counts[:, :LANES]), axis=0, keepdims=True)
        seen = seen + counts[:, LANES:]
        at = ranks == rank
        values = [jnp.where(at, high[row], 0.0), jnp.where(at, low[row], 0.0)]
        asked = asked + mm_nt(mine16, jnp.concatenate(values, axis=0).astype(bf16))
        slot = source[row] * HALF + jnp.where(rank < HALF, rank, rank + (PAIRS - HALF))
        slot_ref[row, :] = slot.astype(i32)
    asked_ref[...] = (asked * LANES + pltpu.roll(asked, 64, 1)).astype(i32)


def restore(slot_ref, arrived_ref, both, tall_ref, slots, sem):
    load = pltpu.make_async_copy(slot_ref, slots, sem)
    load.start()
    piece = arrived_ref[...].astype(f32)
    both[0:PAIRS, :] = piece
    both[PAIRS : 2 * PAIRS, :] = pltpu.roll(piece, RHS, 1)
    load.wait()

    def gather(r, carry):
        base = pl.multiple_of(r * LANES, LANES)
        for k in range(LANES):
            tall_ref[pl.ds(base + k, 1), :] = both[pl.ds(slots[r, k], 1), :]
        return carry

    lax.fori_loop(0, BLOCKS, gather, 0)


def leaf_kernel(
    slot_ref,
    parent_ref,
    where_ref,
    arrived_ref,
    rows_ref,
    inverse_hbm,
    update_hbm,
    inverse1_hbm,
    update1_hbm,
    out_hbm,
    send_ref,
    rhs1_ref,
    rhs2_ref,
    rhs3_ref,
    inverse1_ref,
    update1_ref,
    both,
    tall,
    slots,
    inverse_ref,
    update_ref,
    sol_ref,
    kept_ref,
    kept_rows,
    sems,
):
    load_inverse = pltpu.make_async_copy(inverse_hbm, inverse_ref, sems.at[0])
    load_update = pltpu.make_async_copy(update_hbm, update_ref, sems.at[1])
    load_inverse1 = pltpu.make_async_copy(inverse1_hbm, inverse1_ref, sems.at[3])
    load_update1 = pltpu.make_async_copy(update1_hbm, update1_ref, sems.at[4])
    load_inverse.start()
    load_update.start()
    load_inverse1.start()
    load_update1.start()
    restore(slot_ref, arrived_ref, both, tall, slots, sems.at[5])
    load_inverse.wait()
    load_update.wait()
    sols, terms = [], []
    for n in range(LEAVES):
        lhs = tall[n * LEAF : (n + 1) * LEAF, :].T[:RHS].astype(bf16)
        sols.append(mm(lhs, inverse_ref[n]))
    for n in range(LEAVES):
        sol_ref[:, n * LEAF : (n + 1) * LEAF] = sols[n]
        terms.append(mm(sols[n].astype(bf16), update_ref[n]).astype(bf16))
    rhs2_ref[...] = tall[EDGE1:EDGE2, :].T[:RHS]
    rhs3_ref[...] = tall[EDGE2:ROWS, :].T[:RHS]
    core = where_ref[0]
    for n in range(LEAVES):
        node = parent_ref[n]
        slot = node & 1
        away = ((node >> 3) & 1) != core
        targets = rows_ref[n : n + 1, :]

        @pl.when(away)
        def _():
            send_ref[slot, 0:RHS, :] = terms[n]
            send_ref[slot, RHS : RHS + META, :] = digits(targets, 0)

        @pl.when(jnp.logical_not(away))
        def _():
            kept_ref[slot] = terms[n]
            kept_rows[slot] = jnp.broadcast_to(targets, (8, BORDER0))

    store = pltpu.make_async_copy(sol_ref, out_hbm.at[:, 0:EDGE0], sems.at[2])
    store.start()
    for q in range(NODES1):
        rhs = tall[EDGE0 + q * SEP1 : EDGE0 + (q + 1) * SEP1, :].T[:RHS]
        rows = kept_rows[q, 0:1, :]
        high, low = (rows >> 8).astype(f32), (rows & (LOW - 1)).astype(f32)
        rhs1_ref[q] = rhs - place([kept_ref[q].astype(f32)], high, low, SEP1 // LOW)
    store.wait()
    load_inverse1.wait()
    load_update1.wait()


def level1_kernel(
    parent_ref,
    got_ref,
    rhs_ref,
    rows_ref,
    inverse_ref,
    update_ref,
    out_in,
    out_hbm,
    send_ref,
    sol_ref,
    sem,
):
    del out_in
    for n in range(NODES1):
        high, low, _ = undigits(got_ref[n, RHS : RHS + META, :])
        got = got_ref[n, 0:RHS, :].astype(f32)
        rhs = rhs_ref[n] - place([got], high, low, SEP1 // LOW)
        sol = mm(rhs.astype(bf16), inverse_ref[n])
        sol_ref[:, n * SEP1 : (n + 1) * SEP1] = sol
        terms = mm(sol.astype(bf16), update_ref[n]).astype(bf16)
        node = parent_ref[n]
        slot = node & 3
        side = (node >> 3) & 1
        for f in range(FRONT):
            own = slice(f * PART1, (f + 1) * PART1)
            targets = rows_ref[n : n + 1, own] + (slot * SHARE2 - f * SHARE2)
            meta = digits(targets, side)
            for x in range(2):
                send_ref[x * FRONT + f, n, 0:RHS, :] = terms[:, own]
                send_ref[x * FRONT + f, n, RHS : RHS + META, :] = meta
    store = pltpu.make_async_copy(sol_ref, out_hbm.at[:, EDGE0:EDGE1], sem)
    store.start()
    store.wait()


def sum2_kernel(where_ref, got_ref, rhs_ref, out_ref):
    x0 = where_ref[1].astype(f32)
    terms, highs, lows = [], [], []
    for e in range(2 * FRONT):
        for n in range(NODES1):
            terms.append(got_ref[e, n, 0:RHS, :].astype(f32))
            high, low, side = undigits(got_ref[e, n, RHS : RHS + META, :])
            highs.append(jnp.where(side == x0, high, -1.0))
            lows.append(low)
    total = place(
        [jnp.concatenate(terms, axis=1)],
        jnp.concatenate(highs, axis=1),
        jnp.concatenate(lows, axis=1),
        NODES2 * SHARE2 // LOW,
    )
    out_ref[...] = (rhs_ref[...] - total).astype(bf16)


def level2_kernel(
    parent_ref,
    rhs_ref,
    rows_ref,
    inverse_ref,
    update_ref,
    out_in,
    out_hbm,
    send_ref,
    sol_ref,
    terms_ref,
    terms_rows,
    sem,
):
    del out_in
    for c in range(NODES2):
        own = slice(c * SHARE2, (c + 1) * SHARE2)
        lhs = jnp.concatenate([rhs_ref[g, :, own] for g in range(FRONT)], axis=1)
        sol = mm(lhs, inverse_ref[c])
        sol_ref[:, own] = sol
        node = parent_ref[c]
        slot = ((node >> 3) & 1) * NODES3 + (node & 1)
        terms_ref[slot] = mm(sol.astype(bf16), update_ref[c])
        terms_rows[slot] = jnp.broadcast_to(rows_ref[c : c + 1, :], (8, BORDER2))
    store = pltpu.make_async_copy(sol_ref, out_hbm.at[:, EDGE1:EDGE2], sem)
    store.start()
    for x in range(2):
        for f in range(FRONT):
            ends, end_rows = [], []
            for q in range(NODES3):
                at = x * NODES3 + q
                terms = terms_ref[at, :, f * PART2 : (f + 1) * PART2]
                rows = terms_rows[at, 0:1, f * PART2 : (f + 1) * PART2] + (q - f) * SHARE3
                send_ref[x * FRONT + f, q, 0:RHS, :] = terms[:, :128].astype(bf16)
                send_ref[x * FRONT + f, q, RHS : RHS + META, :] = digits(rows[:, :128], 0)
                ends.append(terms[:, 128:])
                end_rows.append(rows[:, 128:])
            end = jnp.concatenate(ends, axis=1).astype(bf16)
            send_ref[x * FRONT + f, NODES3, 0:RHS, :] = end
            send_ref[x * FRONT + f, NODES3, RHS : RHS + META, :] = digits(
                jnp.concatenate(end_rows, axis=1), 0
            )
    store.wait()


def sum3_kernel(got_ref, rhs_ref, out_ref):
    parts, highs, lows = [], [], []
    for x in range(2):
        for b in range(NODES3 + 1):
            pieces = [got_ref[x * FRONT + g, b, 0:RHS, :].astype(f32) for g in range(FRONT)]
            parts.append((pieces[0] + pieces[1]) + (pieces[2] + pieces[3]))
            high, low, _ = undigits(got_ref[x * FRONT, b, RHS : RHS + META, :])
            highs.append(high)
            lows.append(low)
    part = jnp.concatenate(parts, axis=1)
    coarse = part.astype(bf16).astype(f32)
    total = place(
        [coarse, part - coarse],
        jnp.concatenate(highs, axis=1),
        jnp.concatenate(lows, axis=1),
        NODES3 * SHARE3 // LOW,
    )
    out_ref[...] = (rhs_ref[...] - total).astype(bf16)


def level3_kernel(
    where_ref, own_ref, first_ref, second_ref, third_ref, inverse_ref, out_in, out_hbm, sol_ref, sem
):
    del out_in
    front = where_ref[2]
    for c in range(NODES3):
        own = slice(c * SHARE3, (c + 1) * SHARE3)
        sol = jnp.zeros((RHS, SHARE3), f32)
        for k, piece in enumerate((own_ref, first_ref, second_ref, third_ref)):
            at = pl.multiple_of(((front + FRONT - k) & (FRONT - 1)) * SHARE3, SHARE3)
            sol = sol + mm(piece[:, own], inverse_ref[c, pl.ds(at, SHARE3), :])
        sol_ref[:, own] = sol
    store = pltpu.make_async_copy(sol_ref, out_hbm.at[:, EDGE2:ROWS], sem)
    store.start()
    store.wait()


def exchange(block, axes):
    return lax.all_to_all(block, axes, split_axis=0, concat_axis=0, tiled=True)


def per_device(
    right_hand_sides,
    elimination_natural_index,
    leaf_diagonal_inverse,
    leaf_update_block,
    leaf_parent_rows,
    leaf_parent_node,
    level1_diagonal_inverse,
    level1_update_block,
    level1_parent_rows,
    level1_parent_node,
    level2_diagonal_inverse,
    level2_update_block,
    level2_parent_rows,
    level2_parent_node,
    level3_diagonal_inverse,
):
    where = jnp.stack([lax.axis_index(a) for a in ("core", "x0", "front")]).astype(i32)
    requests, slot = pl.pallas_call(
        rank_kernel,
        in_specs=[VMEM],
        out_specs=[VMEM, VMEM],
        out_shape=[struct((DEVICES, LANES), i32), struct((BLOCKS, LANES), i32)],
        compiler_params=params(6),
        name="rank",
    )(elimination_natural_index.reshape(BLOCKS, LANES))
    asked = exchange(requests.reshape(DEVICES, 1, LANES), ALL).reshape(DEVICES, LANES)
    tall = pl.pallas_call(
        tall_kernel,
        in_specs=[HBM],
        out_specs=VMEM,
        out_shape=struct((ROWS, 128), f32),
        scratch_shapes=[
            pltpu.VMEM((RHS, ROWS), f32),
            pltpu.SemaphoreType.DMA((ROWS // 512,)),
        ],
        compiler_params=params(8),
        name="tall",
    )(in_hbm(right_hand_sides))
    picked = pl.pallas_call(
        pick_kernel,
        in_specs=[VMEM, VMEM],
        out_specs=HBM,
        out_shape=pltpu.HBM((DEVICES * HALF, 128), bf16),
        scratch_shapes=[
            pltpu.VMEM((DEVICES * HALF, 128), f32),
            pltpu.VMEM((DEVICES * HALF, 128), bf16),
            pltpu.SMEM((DEVICES, LANES), i32),
            pltpu.SemaphoreType.DMA((CHUNKS,)),
            pltpu.SemaphoreType.DMA,
        ],
        compiler_params=params(16),
        name="pick",
    )(asked, tall)
    arrived = exchange(picked.reshape(DEVICES, HALF // 2, 2, 128), ALL)
    out, send0, rhs1, rhs2, rhs3, inverse1, update1 = pl.pallas_call(
        leaf_kernel,
        in_specs=[VMEM, SMEM, SMEM, VMEM, VMEM, HBM, HBM, HBM, HBM],
        out_specs=[HBM, VMEM, VMEM, VMEM, VMEM, VMEM, VMEM],
        out_shape=[
            struct((RHS, ROWS), f32),
            struct((NODES1, RHS + META, BORDER0), bf16),
            struct((NODES1, RHS, SEP1), f32),
            struct((RHS, NODES2 * SHARE2), f32),
            struct((RHS, NODES3 * SHARE3), f32),
            struct((NODES1, SEP1, SEP1), bf16),
            struct((NODES1, SEP1, BORDER1), bf16),
        ],
        scratch_shapes=[
            pltpu.VMEM((2 * PAIRS, 128), f32),
            pltpu.VMEM((ROWS, 128), f32),
            pltpu.SMEM((BLOCKS, LANES), i32),
            pltpu.VMEM((LEAVES, LEAF, LEAF), bf16),
            pltpu.VMEM((LEAVES, LEAF, BORDER0), bf16),
            pltpu.VMEM((RHS, EDGE0), f32),
            pltpu.VMEM((NODES1, RHS, BORDER0), bf16),
            pltpu.VMEM((NODES1, 8, BORDER0), i32),
            pltpu.SemaphoreType.DMA((6,)),
        ],
        compiler_params=params(24),
        name="leaf",
    )(
        slot,
        leaf_parent_node,
        where,
        arrived.reshape(DEVICES * HALF, 128),
        leaf_parent_rows,
        in_hbm(leaf_diagonal_inverse),
        in_hbm(leaf_update_block),
        in_hbm(level1_diagonal_inverse),
        in_hbm(level1_update_block),
    )
    got0 = lax.ppermute(send0, "core", [(0, 1), (1, 0)])
    out, send1 = pl.pallas_call(
        level1_kernel,
        in_specs=[SMEM, VMEM, VMEM, VMEM, VMEM, VMEM, HBM],
        out_specs=[HBM, VMEM],
        out_shape=[
            struct((RHS, ROWS), f32),
            struct((2 * FRONT, NODES1, RHS + META, PART1), bf16),
        ],
        scratch_shapes=[pltpu.VMEM((RHS, NODES1 * SEP1), f32), pltpu.SemaphoreType.DMA],
        input_output_aliases={6: 0},
        compiler_params=params(24),
        name="level1",
    )(
        level1_parent_node,
        got0,
        rhs1,
        level1_parent_rows,
        inverse1,
        update1,
        out,
    )
    got1 = exchange(send1, ("x0", "front"))
    side2 = pl.pallas_call(
        sum2_kernel,
        in_specs=[SMEM, VMEM, VMEM],
        out_specs=VMEM,
        out_shape=struct((RHS, NODES2 * SHARE2), bf16),
        compiler_params=params(24),
        name="sum2",
    )(where, got1, rhs2)
    all2 = lax.all_gather(side2, "front", axis=0, tiled=False)
    out, send2 = pl.pallas_call(
        level2_kernel,
        in_specs=[SMEM, VMEM, VMEM, VMEM, VMEM, HBM],
        out_specs=[HBM, VMEM],
        out_shape=[
            struct((RHS, ROWS), f32),
            struct((2 * FRONT, NODES3 + 1, RHS + META, 128), bf16),
        ],
        scratch_shapes=[
            pltpu.VMEM((RHS, NODES2 * SHARE2), f32),
            pltpu.VMEM((2 * NODES3, RHS, BORDER2), f32),
            pltpu.VMEM((2 * NODES3, 8, BORDER2), i32),
            pltpu.SemaphoreType.DMA,
        ],
        input_output_aliases={5: 0},
        compiler_params=params(24),
        name="level2",
    )(
        level2_parent_node,
        all2,
        level2_parent_rows,
        level2_diagonal_inverse,
        level2_update_block,
        out,
    )
    got2 = exchange(send2, ("x1", "front"))
    side3 = pl.pallas_call(
        sum3_kernel,
        in_specs=[VMEM, VMEM],
        out_specs=VMEM,
        out_shape=struct((RHS, NODES3 * SHARE3), bf16),
        compiler_params=params(24),
        name="sum3",
    )(got2, rhs3)
    pieces = [
        lax.ppermute(side3, "front", [(f, (f + k) % FRONT) for f in range(FRONT)])
        for k in range(1, FRONT)
    ]
    return pl.pallas_call(
        level3_kernel,
        in_specs=[SMEM, VMEM, VMEM, VMEM, VMEM, VMEM, HBM],
        out_specs=HBM,
        out_shape=struct((RHS, ROWS), f32),
        scratch_shapes=[pltpu.VMEM((RHS, NODES3 * SHARE3), f32), pltpu.SemaphoreType.DMA],
        input_output_aliases={6: 0},
        compiler_params=params(24),
        name="level3",
    )(where, side3, *pieces, level3_diagonal_inverse, out)


def solution(mesh):
    fine = Mesh(mesh.devices.reshape(4, 2, 2, 2, 4), ALL)
    return jax.shard_map(
        per_device,
        mesh=fine,
        in_specs=(
            P(None, ALL),
            P(ALL),
            P(ALL, None, None),
            P(ALL, None, None),
            P(ALL, None),
            P(ALL),
            P(ALL, None, None),
            P(ALL, None, None),
            P(ALL, None),
            P(ALL),
            P(SUBTREE, None, "front"),
            P(SUBTREE, "front", None),
            P(SUBTREE, None),
            P(SUBTREE),
            P(SUBTREE, None, "front"),
        ),
        out_specs=P(None, ALL),
        check_vma=False,
    )
```

```python
import functools

import jax
import jax.numpy as jnp
from jax import lax
from jax.experimental import pallas as pl
from jax.experimental.pallas import tpu as pltpu
from jax.sharding import Mesh, PartitionSpec as P

RHS = 64
LEAVES, LEAF, BORDER0 = 4, 512, 256
NODES1, SEP1, BORDER1 = 2, 1024, 512
NODES2, SEP2, BORDER2 = 4, 1536, 768
NODES3, SEP3 = 2, 2048
FRONT = 4
SHARE2, SHARE3 = SEP2 // FRONT, SEP3 // FRONT
PART1, PART2 = BORDER1 // FRONT, BORDER2 // FRONT
ROWS = 6656
DEVICES = 128
EACH = ROWS // DEVICES
HALF = EACH // 2
LANES = 128
BLOCKS = ROWS // LANES
PAIRS = DEVICES * HALF
GROUP = 4
CHUNKS = 4
EDGE0 = LEAVES * LEAF
EDGE1 = EDGE0 + NODES1 * SEP1
EDGE2 = EDGE1 + NODES2 * SHARE2
META = 8
LOW = 256

SUBTREE = ("z", "x1", "x0", "core")
ALL = SUBTREE + ("front",)

bf16, f32, i32 = jnp.bfloat16, jnp.float32, jnp.int32
VMEM = pl.BlockSpec(memory_space=pltpu.VMEM)
SMEM = pl.BlockSpec(memory_space=pltpu.SMEM)
HBM = pl.BlockSpec(memory_space=pltpu.HBM)


def params(mib):
    return pltpu.CompilerParams(vmem_limit_bytes=mib << 20)


def in_hbm(x):
    return pltpu.with_memory_space_constraint(x, pltpu.HBM)


def struct(shape, dtype):
    return jax.ShapeDtypeStruct(shape, dtype)


def mm(a, b):
    return jnp.dot(a, b, preferred_element_type=f32)


def mm_nt(a, b):
    return lax.dot_general(a, b, (((1,), (1,)), ((), ())), preferred_element_type=f32)


def place(terms, high, low, blocks):
    n = low.shape[1]
    ids = lax.broadcasted_iota(i32, (LOW, n), 0).astype(f32)
    picks = jnp.where(ids == low, 1.0, 0.0).astype(bf16)
    lhs = [jnp.where(high == h, t, 0.0).astype(bf16) for t in terms for h in range(blocks)]
    found = mm_nt(jnp.concatenate(lhs, axis=0), picks)
    out = []
    for h in range(blocks):
        parts = [
            found[(t * blocks + h) * RHS : (t * blocks + h + 1) * RHS] for t in range(len(terms))
        ]
        out.append(sum(parts[1:], parts[0]))
    return jnp.concatenate(out, axis=1)


def digits(targets, flag):
    n = targets.shape[1]
    ids = lax.broadcasted_iota(i32, (META, n), 0)
    high = jnp.broadcast_to(targets >> 8, (META, n))
    low = jnp.broadcast_to(targets & (LOW - 1), (META, n))
    rows = jnp.where(ids == 0, high, jnp.where(ids == 1, low, flag))
    return rows.astype(f32).astype(bf16)


def undigits(meta):
    m = meta.astype(f32)
    return m[0:1], m[1:2], m[2:3]


def tall_kernel(wide_ref, tall_ref):
    for b in range(ROWS // 512):
        wide = wide_ref[:, b * 512 : (b + 1) * 512]
        tall_ref[b * 512 : (b + 1) * 512, :] = jnp.concatenate([wide, wide], axis=0).T


def pick_kernel(asked_ref, tall_ref, out_hbm, buf, narrow, asked, sems, sem):
    low = lax.broadcasted_iota(i32, (1, 128), 1) < RHS
    step = DEVICES // CHUNKS
    loads = []
    for c in range(CHUNKS):
        part = slice(c * step, (c + 1) * step)
        loads.append(pltpu.make_async_copy(asked_ref.at[part], asked.at[part], sems.at[c]))
        loads[c].start()

    def gather(g, carry):
        base = pl.multiple_of(g * (GROUP * HALF), 8)
        for e in range(GROUP):
            d = g * GROUP + e
            for k in range(HALF):
                first = tall_ref[pl.ds(asked[d, k], 1), :]
                second = tall_ref[pl.ds(asked[d, k + HALF], 1), :]
                buf[pl.ds(base + (e * HALF + k), 1), :] = jnp.where(low, first, second)
        return carry

    for c in range(CHUNKS):
        loads[c].wait()
        lax.fori_loop(c * step // GROUP, (c + 1) * step // GROUP, gather, 0)
    narrow[...] = buf[...].astype(bf16)
    store = pltpu.make_async_copy(narrow, out_hbm, sem)
    store.start()
    store.wait()


def rank_kernel(index_ref, asked_ref, slot_ref):
    index = index_ref[...].astype(f32)
    source = jnp.floor((index + 0.5) * (1.0 / ROWS))
    local = index - source * ROWS
    high = jnp.floor(local * (1.0 / LANES))
    low = local - high * LANES
    rows = lax.broadcasted_iota(i32, (LANES, 2 * LANES), 0)
    columns = lax.broadcasted_iota(i32, (LANES, 2 * LANES), 1)
    before = jnp.where((rows < columns) | (columns >= LANES), 1.0, 0.0).astype(bf16)
    devices = lax.broadcasted_iota(i32, (DEVICES, LANES), 0).astype(f32)
    ranks = lax.broadcasted_iota(i32, (64, LANES), 0).astype(f32)
    seen = jnp.zeros((DEVICES, LANES), f32)
    mines, picks = [], []
    for b in range(BLOCKS):
        row = slice(b, b + 1)
        mine = jnp.where(devices == source[row], 1.0, 0.0)
        mine16 = mine.astype(bf16)
        counts = mm(mine16, before)
        rank = jnp.sum(mine * (seen + counts[:, :LANES]), axis=0, keepdims=True)
        seen = seen + counts[:, LANES:]
        at = ranks == rank
        values = [jnp.where(at, high[row], 0.0), jnp.where(at, low[row], 0.0)]
        mines.append(mine16)
        picks.append(jnp.concatenate(values, axis=0).astype(bf16))
        slot = source[row] * HALF + jnp.where(rank < HALF, rank, rank + (PAIRS - HALF))
        slot_ref[row, :] = slot.astype(i32)
    asked = mm_nt(jnp.concatenate(mines, axis=1), jnp.concatenate(picks, axis=1))
    asked_ref[...] = (asked * LANES + pltpu.roll(asked, 64, 1)).astype(i32)


def restore(first, last, slot_ref, both_ref, tall_ref):
    def gather(r, carry):
        base = pl.multiple_of((r - first // LANES) * LANES, LANES)
        for k in range(LANES):
            tall_ref[pl.ds(base + k, 1), :] = both_ref[pl.ds(slot_ref[r, k], 1), :]
        return carry

    lax.fori_loop(first // LANES, last // LANES, gather, 0)


def rhs_kernel(first, last, slot_ref, both_ref, after_ref, rhs_ref, tall):
    del after_ref
    restore(first, last, slot_ref, both_ref, tall)
    rhs_ref[...] = tall[...].T[:RHS]


def late_rhs(first, last, slot, both, after):
    return pl.pallas_call(
        functools.partial(rhs_kernel, first, last),
        in_specs=[SMEM, VMEM, VMEM],
        out_specs=VMEM,
        out_shape=struct((RHS, last - first), f32),
        scratch_shapes=[pltpu.VMEM((last - first, 128), f32)],
        compiler_params=params(4),
        name="rhs",
    )(slot, both, after)


def leaf_kernel(
    slot_ref,
    parent_ref,
    where_ref,
    arrived_ref,
    rows_ref,
    inverse_hbm,
    update_hbm,
    inverse1_hbm,
    update1_hbm,
    out_hbm,
    send_ref,
    rhs1_ref,
    both,
    inverse1_ref,
    update1_ref,
    tall,
    inverse_ref,
    update_ref,
    sol_ref,
    kept_ref,
    kept_rows,
    sems,
):
    load_inverse = pltpu.make_async_copy(inverse_hbm, inverse_ref, sems.at[0])
    load_update = pltpu.make_async_copy(update_hbm, update_ref, sems.at[1])
    load_inverse1 = pltpu.make_async_copy(inverse1_hbm, inverse1_ref, sems.at[3])
    load_update1 = pltpu.make_async_copy(update1_hbm, update1_ref, sems.at[4])
    load_inverse.start()
    load_update.start()
    load_inverse1.start()
    load_update1.start()
    piece = arrived_ref[...].astype(f32)
    both[0:PAIRS, :] = piece
    both[PAIRS : 2 * PAIRS, :] = pltpu.roll(piece, RHS, 1)
    restore(0, EDGE1, slot_ref, both, tall)
    load_inverse.wait()
    load_update.wait()
    sols, terms = [], []
    for n in range(LEAVES):
        lhs = tall[n * LEAF : (n + 1) * LEAF, :].T[:RHS].astype(bf16)
        sols.append(mm(lhs, inverse_ref[n]))
    for n in range(LEAVES):
        sol_ref[:, n * LEAF : (n + 1) * LEAF] = sols[n]
        terms.append(mm(sols[n].astype(bf16), update_ref[n]).astype(bf16))
    core = where_ref[0]
    for n in range(LEAVES):
        node = parent_ref[n]
        slot = node & 1
        away = ((node >> 3) & 1) != core
        targets = rows_ref[n : n + 1, :]

        @pl.when(away)
        def _():
            send_ref[slot, 0:RHS, :] = terms[n]
            send_ref[slot, RHS : RHS + META, :] = digits(targets, 0)

        @pl.when(jnp.logical_not(away))
        def _():
            kept_ref[slot] = terms[n]
            kept_rows[slot] = jnp.broadcast_to(targets, (8, BORDER0))

    store = pltpu.make_async_copy(sol_ref, out_hbm.at[:, 0:EDGE0], sems.at[2])
    store.start()
    for q in range(NODES1):
        rhs = tall[EDGE0 + q * SEP1 : EDGE0 + (q + 1) * SEP1, :].T[:RHS]
        rows = kept_rows[q, 0:1, :]
        high, low = (rows >> 8).astype(f32), (rows & (LOW - 1)).astype(f32)
        rhs1_ref[q] = rhs - place([kept_ref[q].astype(f32)], high, low, SEP1 // LOW)
    store.wait()
    load_inverse1.wait()
    load_update1.wait()


def level1_kernel(
    parent_ref,
    got_ref,
    rhs_ref,
    rows_ref,
    inverse_ref,
    update_ref,
    after_ref,
    out_in,
    out_hbm,
    send_ref,
    sol_ref,
    sem,
):
    del out_in, after_ref
    for n in range(NODES1):
        high, low, _ = undigits(got_ref[n, RHS : RHS + META, :])
        got = got_ref[n, 0:RHS, :].astype(f32)
        rhs = rhs_ref[n] - place([got], high, low, SEP1 // LOW)
        sol = mm(rhs.astype(bf16), inverse_ref[n])
        sol_ref[:, n * SEP1 : (n + 1) * SEP1] = sol
        terms = mm(sol.astype(bf16), update_ref[n]).astype(bf16)
        node = parent_ref[n]
        slot = node & 3
        side = (node >> 3) & 1
        for f in range(FRONT):
            own = slice(f * PART1, (f + 1) * PART1)
            targets = rows_ref[n : n + 1, own] + (slot * SHARE2 - f * SHARE2)
            meta = digits(targets, side)
            for x in range(2):
                send_ref[x * FRONT + f, n, 0:RHS, :] = terms[:, own]
                send_ref[x * FRONT + f, n, RHS : RHS + META, :] = meta
    store = pltpu.make_async_copy(sol_ref, out_hbm.at[:, EDGE0:EDGE1], sem)
    store.start()
    store.wait()


def sum2_kernel(where_ref, got_ref, rhs_ref, out_ref):
    x0 = where_ref[1].astype(f32)
    terms, highs, lows = [], [], []
    for e in range(2 * FRONT):
        for n in range(NODES1):
            terms.append(got_ref[e, n, 0:RHS, :].astype(f32))
            high, low, side = undigits(got_ref[e, n, RHS : RHS + META, :])
            highs.append(jnp.where(side == x0, high, -1.0))
            lows.append(low)
    total = place(
        [jnp.concatenate(terms, axis=1)],
        jnp.concatenate(highs, axis=1),
        jnp.concatenate(lows, axis=1),
        NODES2 * SHARE2 // LOW,
    )
    out_ref[...] = (rhs_ref[...] - total).astype(bf16)


def gathered(front, pieces, rhs_ref):
    for k, piece in enumerate(pieces):
        rhs_ref[(front + FRONT - k) & (FRONT - 1)] = piece[...]


def level2_kernel(
    where_ref,
    parent_ref,
    own_ref,
    first_ref,
    second_ref,
    third_ref,
    rows_ref,
    inverse_ref,
    update_ref,
    after_ref,
    out_in,
    out_hbm,
    send_ref,
    sol_ref,
    terms_ref,
    terms_rows,
    rhs_ref,
    sem,
):
    del out_in, after_ref
    gathered(where_ref[2], (own_ref, first_ref, second_ref, third_ref), rhs_ref)
    for c in range(NODES2):
        own = slice(c * SHARE2, (c + 1) * SHARE2)
        lhs = jnp.concatenate([rhs_ref[g, :, own] for g in range(FRONT)], axis=1)
        sol = mm(lhs, inverse_ref[c])
        sol_ref[:, own] = sol
        node = parent_ref[c]
        slot = ((node >> 3) & 1) * NODES3 + (node & 1)
        terms_ref[slot] = mm(sol.astype(bf16), update_ref[c])
        terms_rows[slot] = jnp.broadcast_to(rows_ref[c : c + 1, :], (8, BORDER2))
    store = pltpu.make_async_copy(sol_ref, out_hbm.at[:, EDGE1:EDGE2], sem)
    store.start()
    for x in range(2):
        for f in range(FRONT):
            ends, end_rows = [], []
            for q in range(NODES3):
                at = x * NODES3 + q
                terms = terms_ref[at, :, f * PART2 : (f + 1) * PART2]
                rows = terms_rows[at, 0:1, f * PART2 : (f + 1) * PART2] + (q - f) * SHARE3
                send_ref[x * FRONT + f, q, 0:RHS, :] = terms[:, :128].astype(bf16)
                send_ref[x * FRONT + f, q, RHS : RHS + META, :] = digits(rows[:, :128], 0)
                ends.append(terms[:, 128:])
                end_rows.append(rows[:, 128:])
            end = jnp.concatenate(ends, axis=1).astype(bf16)
            send_ref[x * FRONT + f, NODES3, 0:RHS, :] = end
            send_ref[x * FRONT + f, NODES3, RHS : RHS + META, :] = digits(
                jnp.concatenate(end_rows, axis=1), 0
            )
    store.wait()


def sum3_kernel(got_ref, rhs_ref, out_ref):
    parts, highs, lows = [], [], []
    for x in range(2):
        for b in range(NODES3 + 1):
            pieces = [got_ref[x * FRONT + g, b, 0:RHS, :].astype(f32) for g in range(FRONT)]
            parts.append((pieces[0] + pieces[1]) + (pieces[2] + pieces[3]))
            high, low, _ = undigits(got_ref[x * FRONT, b, RHS : RHS + META, :])
            highs.append(high)
            lows.append(low)
    part = jnp.concatenate(parts, axis=1)
    coarse = part.astype(bf16).astype(f32)
    total = place(
        [coarse, part - coarse],
        jnp.concatenate(highs, axis=1),
        jnp.concatenate(lows, axis=1),
        NODES3 * SHARE3 // LOW,
    )
    out_ref[...] = (rhs_ref[...] - total).astype(bf16)


def level3_kernel(
    where_ref,
    own_ref,
    first_ref,
    second_ref,
    third_ref,
    inverse_ref,
    out_in,
    out_hbm,
    sol_ref,
    rhs_ref,
    sem,
):
    del out_in
    gathered(where_ref[2], (own_ref, first_ref, second_ref, third_ref), rhs_ref)
    for c in range(NODES3):
        own = slice(c * SHARE3, (c + 1) * SHARE3)
        lhs = jnp.concatenate([rhs_ref[g, :, own] for g in range(FRONT)], axis=1)
        sol_ref[:, own] = mm(lhs, inverse_ref[c])
    store = pltpu.make_async_copy(sol_ref, out_hbm.at[:, EDGE2:ROWS], sem)
    store.start()
    store.wait()


def front_pieces(side):
    return [
        lax.ppermute(side, "front", [(f, (f + k) % FRONT) for f in range(FRONT)])
        for k in range(1, FRONT)
    ]


def exchange(block, axes):
    return lax.all_to_all(block, axes, split_axis=0, concat_axis=0, tiled=True)


def per_device(
    right_hand_sides,
    elimination_natural_index,
    leaf_diagonal_inverse,
    leaf_update_block,
    leaf_parent_rows,
    leaf_parent_node,
    level1_diagonal_inverse,
    level1_update_block,
    level1_parent_rows,
    level1_parent_node,
    level2_diagonal_inverse,
    level2_update_block,
    level2_parent_rows,
    level2_parent_node,
    level3_diagonal_inverse,
):
    where = jnp.stack([lax.axis_index(a) for a in ("core", "x0", "front")]).astype(i32)
    requests, slot = pl.pallas_call(
        rank_kernel,
        in_specs=[VMEM],
        out_specs=[VMEM, VMEM],
        out_shape=[struct((DEVICES, LANES), i32), struct((BLOCKS, LANES), i32)],
        compiler_params=params(6),
        name="rank",
    )(elimination_natural_index.reshape(BLOCKS, LANES))
    asked = exchange(requests.reshape(DEVICES, 1, LANES), ALL).reshape(DEVICES, LANES)
    tall = pl.pallas_call(
        tall_kernel,
        in_specs=[VMEM],
        out_specs=VMEM,
        out_shape=struct((ROWS, 128), f32),
        compiler_params=params(8),
        name="tall",
    )(right_hand_sides)
    picked = pl.pallas_call(
        pick_kernel,
        in_specs=[VMEM, VMEM],
        out_specs=HBM,
        out_shape=pltpu.HBM((DEVICES * HALF, 128), bf16),
        scratch_shapes=[
            pltpu.VMEM((DEVICES * HALF, 128), f32),
            pltpu.VMEM((DEVICES * HALF, 128), bf16),
            pltpu.SMEM((DEVICES, LANES), i32),
            pltpu.SemaphoreType.DMA((CHUNKS,)),
            pltpu.SemaphoreType.DMA,
        ],
        compiler_params=params(16),
        name="pick",
    )(asked, tall)
    arrived = exchange(picked.reshape(DEVICES, HALF // 2, 2, 128), ALL)
    out, send0, rhs1, both, inverse1, update1 = pl.pallas_call(
        leaf_kernel,
        in_specs=[SMEM, SMEM, SMEM, VMEM, VMEM, HBM, HBM, HBM, HBM],
        out_specs=[HBM, VMEM, VMEM, VMEM, VMEM, VMEM],
        out_shape=[
            struct((RHS, ROWS), f32),
            struct((NODES1, RHS + META, BORDER0), bf16),
            struct((NODES1, RHS, SEP1), f32),
            struct((2 * PAIRS, 128), f32),
            struct((NODES1, SEP1, SEP1), bf16),
            struct((NODES1, SEP1, BORDER1), bf16),
        ],
        scratch_shapes=[
            pltpu.VMEM((EDGE1, 128), f32),
            pltpu.VMEM((LEAVES, LEAF, LEAF), bf16),
            pltpu.VMEM((LEAVES, LEAF, BORDER0), bf16),
            pltpu.VMEM((RHS, EDGE0), f32),
            pltpu.VMEM((NODES1, RHS, BORDER0), bf16),
            pltpu.VMEM((NODES1, 8, BORDER0), i32),
            pltpu.SemaphoreType.DMA((5,)),
        ],
        compiler_params=params(24),
        name="leaf",
    )(
        slot,
        leaf_parent_node,
        where,
        arrived.reshape(DEVICES * HALF, 128),
        leaf_parent_rows,
        in_hbm(leaf_diagonal_inverse),
        in_hbm(leaf_update_block),
        in_hbm(level1_diagonal_inverse),
        in_hbm(level1_update_block),
    )
    got0 = lax.ppermute(send0, "core", [(0, 1), (1, 0)])
    rhs2 = late_rhs(EDGE1, EDGE2, slot, both, send0)
    out, send1 = pl.pallas_call(
        level1_kernel,
        in_specs=[SMEM] + [VMEM] * 6 + [HBM],
        out_specs=[HBM, VMEM],
        out_shape=[
            struct((RHS, ROWS), f32),
            struct((2 * FRONT, NODES1, RHS + META, PART1), bf16),
        ],
        scratch_shapes=[pltpu.VMEM((RHS, NODES1 * SEP1), f32), pltpu.SemaphoreType.DMA],
        input_output_aliases={7: 0},
        compiler_params=params(24),
        name="level1",
    )(
        level1_parent_node,
        got0,
        rhs1,
        level1_parent_rows,
        inverse1,
        update1,
        rhs2,
        out,
    )
    got1 = exchange(send1, ("x0", "front"))
    side2 = pl.pallas_call(
        sum2_kernel,
        in_specs=[SMEM, VMEM, VMEM],
        out_specs=VMEM,
        out_shape=struct((RHS, NODES2 * SHARE2), bf16),
        compiler_params=params(24),
        name="sum2",
    )(where, got1, rhs2)
    pieces = front_pieces(side2)
    rhs3 = late_rhs(EDGE2, ROWS, slot, both, side2)
    out, send2 = pl.pallas_call(
        level2_kernel,
        in_specs=[SMEM, SMEM] + [VMEM] * 8 + [HBM],
        out_specs=[HBM, VMEM],
        out_shape=[
            struct((RHS, ROWS), f32),
            struct((2 * FRONT, NODES3 + 1, RHS + META, 128), bf16),
        ],
        scratch_shapes=[
            pltpu.VMEM((RHS, NODES2 * SHARE2), f32),
            pltpu.VMEM((2 * NODES3, RHS, BORDER2), f32),
            pltpu.VMEM((2 * NODES3, 8, BORDER2), i32),
            pltpu.VMEM((FRONT, RHS, NODES2 * SHARE2), bf16),
            pltpu.SemaphoreType.DMA,
        ],
        input_output_aliases={10: 0},
        compiler_params=params(24),
        name="level2",
    )(
        where,
        level2_parent_node,
        side2,
        *pieces,
        level2_parent_rows,
        level2_diagonal_inverse,
        level2_update_block,
        rhs3,
        out,
    )
    got2 = exchange(send2, ("x1", "front"))
    side3 = pl.pallas_call(
        sum3_kernel,
        in_specs=[VMEM, VMEM],
        out_specs=VMEM,
        out_shape=struct((RHS, NODES3 * SHARE3), bf16),
        compiler_params=params(24),
        name="sum3",
    )(got2, rhs3)
    pieces = front_pieces(side3)
    return pl.pallas_call(
        level3_kernel,
        in_specs=[SMEM, VMEM, VMEM, VMEM, VMEM, VMEM, HBM],
        out_specs=HBM,
        out_shape=struct((RHS, ROWS), f32),
        scratch_shapes=[
            pltpu.VMEM((RHS, NODES3 * SHARE3), f32),
            pltpu.VMEM((FRONT, RHS, NODES3 * SHARE3), bf16),
            pltpu.SemaphoreType.DMA,
        ],
        input_output_aliases={6: 0},
        compiler_params=params(24),
        name="level3",
    )(where, side3, *pieces, level3_diagonal_inverse, out)


def solution(mesh):
    fine = Mesh(mesh.devices.reshape(4, 2, 2, 2, 4), ALL)
    return jax.shard_map(
        per_device,
        mesh=fine,
        in_specs=(
            P(None, ALL),
            P(ALL),
            P(ALL, None, None),
            P(ALL, None, None),
            P(ALL, None),
            P(ALL),
            P(ALL, None, None),
            P(ALL, None, None),
            P(ALL, None),
            P(ALL),
            P(SUBTREE, None, "front"),
            P(SUBTREE, "front", None),
            P(SUBTREE, None),
            P(SUBTREE),
            P(SUBTREE, None, "front"),
        ),
        out_specs=P(None, ALL),
        check_vma=False,
    )
```

```python
import functools

import jax
import jax.numpy as jnp
from jax import lax
from jax.experimental import pallas as pl
from jax.experimental.pallas import tpu as pltpu
from jax.sharding import Mesh, PartitionSpec as P

RHS = 64
LEAVES, LEAF, BORDER0 = 4, 512, 256
NODES1, SEP1, BORDER1 = 2, 1024, 512
NODES2, SEP2, BORDER2 = 4, 1536, 768
NODES3, SEP3 = 2, 2048
FRONT = 4
SHARE2, SHARE3 = SEP2 // FRONT, SEP3 // FRONT
PART1, PART2 = BORDER1 // FRONT, BORDER2 // FRONT
ROWS = 6656
DEVICES = 128
EACH = ROWS // DEVICES
HALF = EACH // 2
LANES = 128
BLOCKS = ROWS // LANES
PAIRS = DEVICES * HALF
GROUP = 4
CHUNKS = 4
EDGE0 = LEAVES * LEAF
EDGE1 = EDGE0 + NODES1 * SEP1
EDGE2 = EDGE1 + NODES2 * SHARE2
META = 8
LOW = 256

SUBTREE = ("z", "x1", "x0", "core")
ALL = SUBTREE + ("front",)

bf16, f32, i32 = jnp.bfloat16, jnp.float32, jnp.int32
VMEM = pl.BlockSpec(memory_space=pltpu.VMEM)
SMEM = pl.BlockSpec(memory_space=pltpu.SMEM)
HBM = pl.BlockSpec(memory_space=pltpu.HBM)


def params(mib):
    return pltpu.CompilerParams(vmem_limit_bytes=mib << 20)


def in_hbm(x):
    return pltpu.with_memory_space_constraint(x, pltpu.HBM)


def struct(shape, dtype):
    return jax.ShapeDtypeStruct(shape, dtype)


def mm(a, b):
    return jnp.dot(a, b, preferred_element_type=f32)


def mm_nt(a, b):
    return lax.dot_general(a, b, (((1,), (1,)), ((), ())), preferred_element_type=f32)


def place(terms, high, low, blocks):
    n = low.shape[1]
    ids = lax.broadcasted_iota(i32, (LOW, n), 0).astype(f32)
    picks = jnp.where(ids == low, 1.0, 0.0).astype(bf16)
    lhs = [jnp.where(high == h, t, 0.0).astype(bf16) for t in terms for h in range(blocks)]
    found = mm_nt(jnp.concatenate(lhs, axis=0), picks)
    out = []
    for h in range(blocks):
        parts = [
            found[(t * blocks + h) * RHS : (t * blocks + h + 1) * RHS] for t in range(len(terms))
        ]
        out.append(sum(parts[1:], parts[0]))
    return jnp.concatenate(out, axis=1)


def digits(targets, flag):
    n = targets.shape[1]
    ids = lax.broadcasted_iota(i32, (META, n), 0)
    high = jnp.broadcast_to(targets >> 8, (META, n))
    low = jnp.broadcast_to(targets & (LOW - 1), (META, n))
    rows = jnp.where(ids == 0, high, jnp.where(ids == 1, low, flag))
    return rows.astype(f32).astype(bf16)


def undigits(meta):
    m = meta.astype(f32)
    return m[0:1], m[1:2], m[2:3]


def tall_kernel(wide_ref, tall_ref):
    for b in range(ROWS // 512):
        wide = wide_ref[:, b * 512 : (b + 1) * 512]
        tall_ref[b * 512 : (b + 1) * 512, :] = jnp.concatenate([wide, wide], axis=0).T


def pick_kernel(asked_ref, tall_ref, out_hbm, buf, narrow, asked, sems):
    low = lax.broadcasted_iota(i32, (1, 128), 1) < RHS
    step = DEVICES // CHUNKS
    loads, stores = [], []
    for c in range(CHUNKS):
        part = slice(c * step, (c + 1) * step)
        loads.append(pltpu.make_async_copy(asked_ref.at[part], asked.at[part], sems.at[c]))
        loads[c].start()

    def gather(g, carry):
        base = pl.multiple_of(g * (GROUP * HALF), 8)
        for e in range(GROUP):
            d = g * GROUP + e
            for k in range(HALF):
                first = tall_ref[pl.ds(asked[d, k], 1), :]
                second = tall_ref[pl.ds(asked[d, k + HALF], 1), :]
                buf[pl.ds(base + (e * HALF + k), 1), :] = jnp.where(low, first, second)
        return carry

    for c in range(CHUNKS):
        loads[c].wait()
        lax.fori_loop(c * step // GROUP, (c + 1) * step // GROUP, gather, 0)
        part = slice(c * step * HALF, (c + 1) * step * HALF)
        narrow[part, :] = buf[part, :].astype(bf16)
        stores.append(
            pltpu.make_async_copy(narrow.at[part], out_hbm.at[part], sems.at[CHUNKS + c])
        )
        stores[c].start()
    for store in stores:
        store.wait()


def rank_kernel(index_ref, asked_ref, slot_ref):
    index = index_ref[...].astype(f32)
    source = jnp.floor((index + 0.5) * (1.0 / ROWS))
    local = index - source * ROWS
    high = jnp.floor(local * (1.0 / LANES))
    low = local - high * LANES
    rows = lax.broadcasted_iota(i32, (LANES, 2 * LANES), 0)
    columns = lax.broadcasted_iota(i32, (LANES, 2 * LANES), 1)
    before = jnp.where((rows < columns) | (columns >= LANES), 1.0, 0.0).astype(bf16)
    devices = lax.broadcasted_iota(i32, (DEVICES, LANES), 0).astype(f32)
    ranks = lax.broadcasted_iota(i32, (64, LANES), 0).astype(f32)
    seen = jnp.zeros((DEVICES, LANES), f32)
    mines, picks = [], []
    for b in range(BLOCKS):
        row = slice(b, b + 1)
        mine = jnp.where(devices == source[row], 1.0, 0.0)
        mine16 = mine.astype(bf16)
        counts = mm(mine16, before)
        rank = jnp.sum(mine * (seen + counts[:, :LANES]), axis=0, keepdims=True)
        seen = seen + counts[:, LANES:]
        at = ranks == rank
        values = [jnp.where(at, high[row], 0.0), jnp.where(at, low[row], 0.0)]
        mines.append(mine16)
        picks.append(jnp.concatenate(values, axis=0).astype(bf16))
        slot = source[row] * HALF + jnp.where(rank < HALF, rank, rank + (PAIRS - HALF))
        slot_ref[row, :] = slot.astype(i32)
    asked = mm_nt(jnp.concatenate(mines, axis=1), jnp.concatenate(picks, axis=1))
    asked_ref[...] = (asked * LANES + pltpu.roll(asked, 64, 1)).astype(i32)


def restore(first, last, slot_ref, both_ref, tall_ref):
    def gather(r, carry):
        base = pl.multiple_of((r - first // LANES) * LANES, LANES)
        for k in range(LANES):
            tall_ref[pl.ds(base + k, 1), :] = both_ref[pl.ds(slot_ref[r, k], 1), :]
        return carry

    lax.fori_loop(first // LANES, last // LANES, gather, 0)


def rhs_kernel(first, last, slot_ref, both_ref, after_ref, rhs_ref, tall):
    del after_ref
    restore(first, last, slot_ref, both_ref, tall)
    rhs_ref[...] = tall[...].T[:RHS]


def late_rhs(first, last, slot, both, after):
    return pl.pallas_call(
        functools.partial(rhs_kernel, first, last),
        in_specs=[SMEM, VMEM, VMEM],
        out_specs=VMEM,
        out_shape=struct((RHS, last - first), f32),
        scratch_shapes=[pltpu.VMEM((last - first, 128), f32)],
        compiler_params=params(4),
        name="rhs",
    )(slot, both, after)


def leaf_kernel(
    slot_ref,
    parent_ref,
    arrived_ref,
    rows_ref,
    inverse_hbm,
    update_hbm,
    inverse1_hbm,
    update1_hbm,
    out_hbm,
    send_ref,
    rhs1_ref,
    both,
    inverse1_ref,
    update1_ref,
    tall,
    inverse_ref,
    update_ref,
    sol_ref,
    kept_ref,
    kept_rows,
    sems,
):
    load_inverse = pltpu.make_async_copy(inverse_hbm, inverse_ref, sems.at[0])
    load_update = pltpu.make_async_copy(update_hbm, update_ref, sems.at[1])
    load_inverse1 = pltpu.make_async_copy(inverse1_hbm, inverse1_ref, sems.at[3])
    load_update1 = pltpu.make_async_copy(update1_hbm, update1_ref, sems.at[4])
    load_inverse.start()
    load_update.start()
    load_inverse1.start()
    load_update1.start()
    piece = arrived_ref[...].astype(f32)
    both[0:PAIRS, :] = piece
    both[PAIRS : 2 * PAIRS, :] = pltpu.roll(piece, RHS, 1)
    restore(0, EDGE1, slot_ref, both, tall)
    load_inverse.wait()
    load_update.wait()
    sols, terms = [], []
    for n in range(LEAVES):
        lhs = tall[n * LEAF : (n + 1) * LEAF, :].T[:RHS].astype(bf16)
        sols.append(mm(lhs, inverse_ref[n]))
    for n in range(LEAVES):
        sol_ref[:, n * LEAF : (n + 1) * LEAF] = sols[n]
        terms.append(mm(sols[n].astype(bf16), update_ref[n]).astype(bf16))
    store = pltpu.make_async_copy(sol_ref, out_hbm.at[:, 0:EDGE0], sems.at[2])
    store.start()
    core = lax.axis_index("core")
    for n in range(LEAVES):
        node = parent_ref[n]
        slot = node & 1
        away = ((node >> 3) & 1) != core
        targets = rows_ref[n : n + 1, :]

        @pl.when(away)
        def _():
            send_ref[slot, 0:RHS, :] = terms[n]
            send_ref[slot, RHS : RHS + META, :] = digits(targets, 0)

        @pl.when(jnp.logical_not(away))
        def _():
            kept_ref[slot] = terms[n]
            kept_rows[slot] = jnp.broadcast_to(targets, (8, BORDER0))

    for q in range(NODES1):
        rhs = tall[EDGE0 + q * SEP1 : EDGE0 + (q + 1) * SEP1, :].T[:RHS]
        rows = kept_rows[q, 0:1, :]
        high, low = (rows >> 8).astype(f32), (rows & (LOW - 1)).astype(f32)
        rhs1_ref[q] = rhs - place([kept_ref[q].astype(f32)], high, low, SEP1 // LOW)
    store.wait()
    load_inverse1.wait()
    load_update1.wait()


def level1_kernel(
    parent_vmem,
    got_ref,
    rhs_ref,
    rows_ref,
    inverse_ref,
    update_ref,
    after_ref,
    out_in,
    out_hbm,
    send_ref,
    sol_ref,
    parent_ref,
    sems,
):
    del out_in, after_ref
    load = pltpu.make_async_copy(parent_vmem, parent_ref, sems.at[NODES1])
    load.start()
    stores = []
    for n in range(NODES1):
        high, low, _ = undigits(got_ref[n, RHS : RHS + META, :])
        got = got_ref[n, 0:RHS, :].astype(f32)
        rhs = rhs_ref[n] - place([got], high, low, SEP1 // LOW)
        sol = mm(rhs.astype(bf16), inverse_ref[n])
        own = slice(n * SEP1, (n + 1) * SEP1)
        sol_ref[:, own] = sol
        part = slice(EDGE0 + n * SEP1, EDGE0 + (n + 1) * SEP1)
        stores.append(
            pltpu.make_async_copy(sol_ref.at[:, own], out_hbm.at[:, part], sems.at[n])
        )
        stores[n].start()
        terms = mm(sol.astype(bf16), update_ref[n]).astype(bf16)
        if n == 0:
            load.wait()
        node = parent_ref[n]
        slot = node & 3
        side = (node >> 3) & 1
        for f in range(FRONT):
            own = slice(f * PART1, (f + 1) * PART1)
            targets = rows_ref[n : n + 1, own] + (slot * SHARE2 - f * SHARE2)
            meta = digits(targets, side)
            for x in range(2):
                send_ref[x * FRONT + f, n, 0:RHS, :] = terms[:, own]
                send_ref[x * FRONT + f, n, RHS : RHS + META, :] = meta
    for store in stores:
        store.wait()


def sum2_kernel(got_ref, rhs_ref, out_ref):
    x0 = lax.axis_index("x0").astype(f32)
    terms, highs, lows = [], [], []
    for e in range(2 * FRONT):
        for n in range(NODES1):
            terms.append(got_ref[e, n, 0:RHS, :].astype(f32))
            high, low, side = undigits(got_ref[e, n, RHS : RHS + META, :])
            highs.append(jnp.where(side == x0, high, -1.0))
            lows.append(low)
    total = place(
        [jnp.concatenate(terms, axis=1)],
        jnp.concatenate(highs, axis=1),
        jnp.concatenate(lows, axis=1),
        NODES2 * SHARE2 // LOW,
    )
    out_ref[...] = (rhs_ref[...] - total).astype(bf16)


def gathered(pieces, rhs_ref):
    front = lax.axis_index("front")
    for k, piece in enumerate(pieces):
        rhs_ref[(front + FRONT - k) & (FRONT - 1)] = piece[...]


def level2_kernel(
    parent_vmem,
    own_ref,
    first_ref,
    second_ref,
    third_ref,
    rows_ref,
    inverse_ref,
    update_ref,
    after_ref,
    out_in,
    out_hbm,
    send_ref,
    sol_ref,
    terms_ref,
    terms_rows,
    rhs_ref,
    parent_ref,
    sems,
):
    del out_in, after_ref
    load = pltpu.make_async_copy(parent_vmem, parent_ref, sems.at[1])
    load.start()
    gathered((own_ref, first_ref, second_ref, third_ref), rhs_ref)
    for c in range(NODES2):
        own = slice(c * SHARE2, (c + 1) * SHARE2)
        lhs = jnp.concatenate([rhs_ref[g, :, own] for g in range(FRONT)], axis=1)
        sol = mm(lhs, inverse_ref[c])
        sol_ref[:, own] = sol
        if c == 0:
            load.wait()
        node = parent_ref[c]
        slot = ((node >> 3) & 1) * NODES3 + (node & 1)
        terms_ref[slot] = mm(sol.astype(bf16), update_ref[c])
        terms_rows[slot] = jnp.broadcast_to(rows_ref[c : c + 1, :], (8, BORDER2))
    store = pltpu.make_async_copy(sol_ref, out_hbm.at[:, EDGE1:EDGE2], sems.at[0])
    store.start()
    for x in range(2):
        for f in range(FRONT):
            ends, end_rows = [], []
            for q in range(NODES3):
                at = x * NODES3 + q
                terms = terms_ref[at, :, f * PART2 : (f + 1) * PART2]
                rows = terms_rows[at, 0:1, f * PART2 : (f + 1) * PART2] + (q - f) * SHARE3
                send_ref[x * FRONT + f, q, 0:RHS, :] = terms[:, :128].astype(bf16)
                send_ref[x * FRONT + f, q, RHS : RHS + META, :] = digits(rows[:, :128], 0)
                ends.append(terms[:, 128:])
                end_rows.append(rows[:, 128:])
            end = jnp.concatenate(ends, axis=1).astype(bf16)
            send_ref[x * FRONT + f, NODES3, 0:RHS, :] = end
            send_ref[x * FRONT + f, NODES3, RHS : RHS + META, :] = digits(
                jnp.concatenate(end_rows, axis=1), 0
            )
    store.wait()


def sum3_kernel(got_ref, rhs_ref, out_ref):
    parts, highs, lows = [], [], []
    for x in range(2):
        for b in range(NODES3 + 1):
            pieces = [got_ref[x * FRONT + g, b, 0:RHS, :].astype(f32) for g in range(FRONT)]
            parts.append((pieces[0] + pieces[1]) + (pieces[2] + pieces[3]))
            high, low, _ = undigits(got_ref[x * FRONT, b, RHS : RHS + META, :])
            highs.append(high)
            lows.append(low)
    part = jnp.concatenate(parts, axis=1)
    coarse = part.astype(bf16).astype(f32)
    total = place(
        [coarse, part - coarse],
        jnp.concatenate(highs, axis=1),
        jnp.concatenate(lows, axis=1),
        NODES3 * SHARE3 // LOW,
    )
    out_ref[...] = (rhs_ref[...] - total).astype(bf16)


def level3_kernel(
    own_ref,
    first_ref,
    second_ref,
    third_ref,
    inverse_ref,
    out_in,
    out_hbm,
    sol_ref,
    rhs_ref,
    sems,
):
    del out_in
    gathered((own_ref, first_ref, second_ref, third_ref), rhs_ref)
    stores = []
    for c in range(NODES3):
        own = slice(c * SHARE3, (c + 1) * SHARE3)
        lhs = jnp.concatenate([rhs_ref[g, :, own] for g in range(FRONT)], axis=1)
        sol_ref[:, own] = mm(lhs, inverse_ref[c])
        part = slice(EDGE2 + c * SHARE3, EDGE2 + (c + 1) * SHARE3)
        stores.append(
            pltpu.make_async_copy(sol_ref.at[:, own], out_hbm.at[:, part], sems.at[c])
        )
        stores[c].start()
    for store in stores:
        store.wait()


def front_pieces(side):
    return [
        lax.ppermute(side, "front", [(f, (f + k) % FRONT) for f in range(FRONT)])
        for k in range(1, FRONT)
    ]


def exchange(block, axes):
    return lax.all_to_all(block, axes, split_axis=0, concat_axis=0, tiled=True)


def per_device(
    right_hand_sides,
    elimination_natural_index,
    leaf_diagonal_inverse,
    leaf_update_block,
    leaf_parent_rows,
    leaf_parent_node,
    level1_diagonal_inverse,
    level1_update_block,
    level1_parent_rows,
    level1_parent_node,
    level2_diagonal_inverse,
    level2_update_block,
    level2_parent_rows,
    level2_parent_node,
    level3_diagonal_inverse,
):
    requests, slot = pl.pallas_call(
        rank_kernel,
        in_specs=[VMEM],
        out_specs=[VMEM, VMEM],
        out_shape=[struct((DEVICES, LANES), i32), struct((BLOCKS, LANES), i32)],
        compiler_params=params(6),
        name="rank",
    )(elimination_natural_index.reshape(BLOCKS, LANES))
    asked = exchange(requests.reshape(DEVICES, 1, LANES), ALL).reshape(DEVICES, LANES)
    tall = pl.pallas_call(
        tall_kernel,
        in_specs=[VMEM],
        out_specs=VMEM,
        out_shape=struct((ROWS, 128), f32),
        compiler_params=params(8),
        name="tall",
    )(right_hand_sides)
    picked = pl.pallas_call(
        pick_kernel,
        in_specs=[VMEM, VMEM],
        out_specs=HBM,
        out_shape=pltpu.HBM((DEVICES * HALF, 128), bf16),
        scratch_shapes=[
            pltpu.VMEM((DEVICES * HALF, 128), f32),
            pltpu.VMEM((DEVICES * HALF, 128), bf16),
            pltpu.SMEM((DEVICES, LANES), i32),
            pltpu.SemaphoreType.DMA((2 * CHUNKS,)),
        ],
        compiler_params=params(16),
        name="pick",
    )(asked, tall)
    arrived = exchange(picked.reshape(DEVICES, HALF // 2, 2, 128), ALL)
    out, send0, rhs1, both, inverse1, update1 = pl.pallas_call(
        leaf_kernel,
        in_specs=[SMEM, SMEM, VMEM, VMEM, HBM, HBM, HBM, HBM],
        out_specs=[HBM, VMEM, VMEM, VMEM, VMEM, VMEM],
        out_shape=[
            struct((RHS, ROWS), f32),
            struct((NODES1, RHS + META, BORDER0), bf16),
            struct((NODES1, RHS, SEP1), f32),
            struct((2 * PAIRS, 128), f32),
            struct((NODES1, SEP1, SEP1), bf16),
            struct((NODES1, SEP1, BORDER1), bf16),
        ],
        scratch_shapes=[
            pltpu.VMEM((EDGE1, 128), f32),
            pltpu.VMEM((LEAVES, LEAF, LEAF), bf16),
            pltpu.VMEM((LEAVES, LEAF, BORDER0), bf16),
            pltpu.VMEM((RHS, EDGE0), f32),
            pltpu.VMEM((NODES1, RHS, BORDER0), bf16),
            pltpu.VMEM((NODES1, 8, BORDER0), i32),
            pltpu.SemaphoreType.DMA((5,)),
        ],
        compiler_params=params(24),
        name="leaf",
    )(
        slot,
        leaf_parent_node,
        arrived.reshape(DEVICES * HALF, 128),
        leaf_parent_rows,
        in_hbm(leaf_diagonal_inverse),
        in_hbm(leaf_update_block),
        in_hbm(level1_diagonal_inverse),
        in_hbm(level1_update_block),
    )
    got0 = lax.ppermute(send0, "core", [(0, 1), (1, 0)])
    rhs2 = late_rhs(EDGE1, EDGE2, slot, both, send0)
    out, send1 = pl.pallas_call(
        level1_kernel,
        in_specs=[VMEM] * 7 + [HBM],
        out_specs=[HBM, VMEM],
        out_shape=[
            struct((RHS, ROWS), f32),
            struct((2 * FRONT, NODES1, RHS + META, PART1), bf16),
        ],
        scratch_shapes=[
            pltpu.VMEM((RHS, NODES1 * SEP1), f32),
            pltpu.SMEM((NODES1,), i32),
            pltpu.SemaphoreType.DMA((NODES1 + 1,)),
        ],
        input_output_aliases={7: 0},
        compiler_params=params(24),
        name="level1",
    )(
        level1_parent_node,
        got0,
        rhs1,
        level1_parent_rows,
        inverse1,
        update1,
        rhs2,
        out,
    )
    got1 = exchange(send1, ("x0", "front"))
    side2 = pl.pallas_call(
        sum2_kernel,
        in_specs=[VMEM, VMEM],
        out_specs=VMEM,
        out_shape=struct((RHS, NODES2 * SHARE2), bf16),
        compiler_params=params(24),
        name="sum2",
    )(got1, rhs2)
    pieces = front_pieces(side2)
    rhs3 = late_rhs(EDGE2, ROWS, slot, both, side2)
    out, send2 = pl.pallas_call(
        level2_kernel,
        in_specs=[VMEM] * 9 + [HBM],
        out_specs=[HBM, VMEM],
        out_shape=[
            struct((RHS, ROWS), f32),
            struct((2 * FRONT, NODES3 + 1, RHS + META, 128), bf16),
        ],
        scratch_shapes=[
            pltpu.VMEM((RHS, NODES2 * SHARE2), f32),
            pltpu.VMEM((2 * NODES3, RHS, BORDER2), f32),
            pltpu.VMEM((2 * NODES3, 8, BORDER2), i32),
            pltpu.VMEM((FRONT, RHS, NODES2 * SHARE2), bf16),
            pltpu.SMEM((NODES2,), i32),
            pltpu.SemaphoreType.DMA((2,)),
        ],
        input_output_aliases={9: 0},
        compiler_params=params(24),
        name="level2",
    )(
        level2_parent_node,
        side2,
        *pieces,
        level2_parent_rows,
        level2_diagonal_inverse,
        level2_update_block,
        rhs3,
        out,
    )
    got2 = exchange(send2, ("x1", "front"))
    side3 = pl.pallas_call(
        sum3_kernel,
        in_specs=[VMEM, VMEM],
        out_specs=VMEM,
        out_shape=struct((RHS, NODES3 * SHARE3), bf16),
        compiler_params=params(24),
        name="sum3",
    )(got2, rhs3)
    pieces = front_pieces(side3)
    return pl.pallas_call(
        level3_kernel,
        in_specs=[VMEM] * 5 + [HBM],
        out_specs=HBM,
        out_shape=struct((RHS, ROWS), f32),
        scratch_shapes=[
            pltpu.VMEM((RHS, NODES3 * SHARE3), f32),
            pltpu.VMEM((FRONT, RHS, NODES3 * SHARE3), bf16),
            pltpu.SemaphoreType.DMA((NODES3,)),
        ],
        input_output_aliases={5: 0},
        compiler_params=params(24),
        name="level3",
    )(side3, *pieces, level3_diagonal_inverse, out)


def solution(mesh):
    fine = Mesh(mesh.devices.reshape(4, 2, 2, 2, 4), ALL)
    return jax.shard_map(
        per_device,
        mesh=fine,
        in_specs=(
            P(None, ALL),
            P(ALL),
            P(ALL, None, None),
            P(ALL, None, None),
            P(ALL, None),
            P(ALL),
            P(ALL, None, None),
            P(ALL, None, None),
            P(ALL, None),
            P(ALL),
            P(SUBTREE, None, "front"),
            P(SUBTREE, "front", None),
            P(SUBTREE, None),
            P(SUBTREE),
            P(SUBTREE, None, "front"),
        ),
        out_specs=P(None, ALL),
        check_vma=False,
    )
```

```python
import functools

import jax
import jax.numpy as jnp
from jax import lax
from jax.experimental import pallas as pl
from jax.experimental.pallas import tpu as pltpu
from jax.sharding import Mesh, PartitionSpec as P

RHS = 64
LEAVES, LEAF, BORDER0 = 4, 512, 256
NODES1, SEP1, BORDER1 = 2, 1024, 512
NODES2, SEP2, BORDER2 = 4, 1536, 768
NODES3, SEP3 = 2, 2048
FRONT = 4
SHARE2, SHARE3 = SEP2 // FRONT, SEP3 // FRONT
PART1, PART2 = BORDER1 // FRONT, BORDER2 // FRONT
ROWS = 6656
DEVICES = 128
EACH = ROWS // DEVICES
HALF = EACH // 2
LANES = 128
BLOCKS = ROWS // LANES
PAIRS = DEVICES * HALF
GROUP = 4
CHUNKS = 4
EDGE0 = LEAVES * LEAF
EDGE1 = EDGE0 + NODES1 * SEP1
EDGE2 = EDGE1 + NODES2 * SHARE2
META = 8
LOW = 256

SUBTREE = ("z", "x1", "x0", "core")
ALL = SUBTREE + ("front",)

bf16, f32, i32 = jnp.bfloat16, jnp.float32, jnp.int32
VMEM = pl.BlockSpec(memory_space=pltpu.VMEM)
SMEM = pl.BlockSpec(memory_space=pltpu.SMEM)
HBM = pl.BlockSpec(memory_space=pltpu.HBM)


def params(mib):
    return pltpu.CompilerParams(vmem_limit_bytes=mib << 20)


def in_hbm(x):
    return pltpu.with_memory_space_constraint(x, pltpu.HBM)


def struct(shape, dtype):
    return jax.ShapeDtypeStruct(shape, dtype)


def mm(a, b):
    return jnp.dot(a, b, preferred_element_type=f32)


def mm_nt(a, b):
    return lax.dot_general(a, b, (((1,), (1,)), ((), ())), preferred_element_type=f32)


def place(terms, high, low, blocks):
    n = low.shape[1]
    ids = lax.broadcasted_iota(i32, (LOW, n), 0).astype(f32)
    picks = jnp.where(ids == low, 1.0, 0.0).astype(bf16)
    lhs = [jnp.where(high == h, t, 0.0).astype(bf16) for t in terms for h in range(blocks)]
    found = mm_nt(jnp.concatenate(lhs, axis=0), picks)
    out = []
    for h in range(blocks):
        parts = [
            found[(t * blocks + h) * RHS : (t * blocks + h + 1) * RHS] for t in range(len(terms))
        ]
        out.append(sum(parts[1:], parts[0]))
    return jnp.concatenate(out, axis=1)


def digits(targets, flag):
    n = targets.shape[1]
    ids = lax.broadcasted_iota(i32, (META, n), 0)
    high = jnp.broadcast_to(targets >> 8, (META, n))
    low = jnp.broadcast_to(targets & (LOW - 1), (META, n))
    rows = jnp.where(ids == 0, high, jnp.where(ids == 1, low, flag))
    return rows.astype(f32).astype(bf16)


def undigits(meta):
    m = meta.astype(f32)
    return m[0:1], m[1:2], m[2:3]


def tall_kernel(wide_ref, tall_ref):
    for b in range(ROWS // 512):
        wide = wide_ref[:, b * 512 : (b + 1) * 512]
        tall_ref[b * 512 : (b + 1) * 512, :] = jnp.concatenate([wide, wide], axis=0).T


def pick_kernel(asked_ref, tall_ref, out_hbm, buf, narrow, asked, sems):
    low = lax.broadcasted_iota(i32, (1, 128), 1) < RHS
    step = DEVICES // CHUNKS
    loads, stores = [], []
    for c in range(CHUNKS):
        part = slice(c * step, (c + 1) * step)
        loads.append(pltpu.make_async_copy(asked_ref.at[part], asked.at[part], sems.at[c]))
        loads[c].start()

    def gather(g, carry):
        base = pl.multiple_of(g * (GROUP * HALF), 8)
        for e in range(GROUP):
            d = g * GROUP + e
            for k in range(HALF):
                first = tall_ref[pl.ds(asked[d, k], 1), :]
                second = tall_ref[pl.ds(asked[d, k + HALF], 1), :]
                buf[pl.ds(base + (e * HALF + k), 1), :] = jnp.where(low, first, second)
        return carry

    for c in range(CHUNKS):
        loads[c].wait()
        lax.fori_loop(c * step // GROUP, (c + 1) * step // GROUP, gather, 0)
        part = slice(c * step * HALF, (c + 1) * step * HALF)
        narrow[part, :] = buf[part, :].astype(bf16)
        stores.append(
            pltpu.make_async_copy(narrow.at[part], out_hbm.at[part], sems.at[CHUNKS + c])
        )
        stores[c].start()
    for store in stores:
        store.wait()


def rank_kernel(index_ref, asked_ref, slot_ref):
    index = index_ref[...].astype(f32)
    source = jnp.floor((index + 0.5) * (1.0 / ROWS))
    local = index - source * ROWS
    high = jnp.floor(local * (1.0 / LANES))
    low = local - high * LANES
    rows = lax.broadcasted_iota(i32, (LANES, 2 * LANES), 0)
    columns = lax.broadcasted_iota(i32, (LANES, 2 * LANES), 1)
    before = jnp.where((rows < columns) | (columns >= LANES), 1.0, 0.0).astype(bf16)
    devices = lax.broadcasted_iota(i32, (DEVICES, LANES), 0).astype(f32)
    ranks = lax.broadcasted_iota(i32, (64, LANES), 0).astype(f32)
    seen = jnp.zeros((DEVICES, LANES), f32)
    mines, picks = [], []
    for b in range(BLOCKS):
        row = slice(b, b + 1)
        mine = jnp.where(devices == source[row], 1.0, 0.0)
        mine16 = mine.astype(bf16)
        counts = mm(mine16, before)
        rank = jnp.sum(mine * (seen + counts[:, :LANES]), axis=0, keepdims=True)
        seen = seen + counts[:, LANES:]
        at = ranks == rank
        values = [jnp.where(at, high[row], 0.0), jnp.where(at, low[row], 0.0)]
        mines.append(mine16)
        picks.append(jnp.concatenate(values, axis=0).astype(bf16))
        slot = source[row] * HALF + jnp.where(rank < HALF, rank, rank + (PAIRS - HALF))
        slot_ref[row, :] = slot.astype(i32)
    asked = mm_nt(jnp.concatenate(mines, axis=1), jnp.concatenate(picks, axis=1))
    asked_ref[...] = (asked * LANES + pltpu.roll(asked, 64, 1)).astype(i32)


def restore(first, last, slot_ref, both_ref, tall_ref):
    def gather(r, carry):
        base = pl.multiple_of((r - first // LANES) * LANES, LANES)
        for k in range(LANES):
            tall_ref[pl.ds(base + k, 1), :] = both_ref[pl.ds(slot_ref[r, k], 1), :]
        return carry

    lax.fori_loop(first // LANES, last // LANES, gather, 0)


def rhs_kernel(first, last, slot_ref, both_ref, after_ref, rhs_ref, tall):
    del after_ref
    restore(first, last, slot_ref, both_ref, tall)
    rhs_ref[...] = tall[...].T[:RHS]


def late_rhs(first, last, slot, both, after):
    return pl.pallas_call(
        functools.partial(rhs_kernel, first, last),
        in_specs=[SMEM, VMEM, VMEM],
        out_specs=VMEM,
        out_shape=struct((RHS, last - first), f32),
        scratch_shapes=[pltpu.VMEM((last - first, 128), f32)],
        compiler_params=params(4),
        name="rhs",
    )(slot, both, after)


def leaf_kernel(
    slot_ref,
    parent_ref,
    arrived_ref,
    rows_ref,
    inverse_hbm,
    update_hbm,
    inverse1_hbm,
    update1_hbm,
    out_hbm,
    send_ref,
    rhs1_ref,
    both,
    inverse1_ref,
    update1_ref,
    tall,
    inverse_ref,
    update_ref,
    sol_ref,
    kept_ref,
    kept_rows,
    sems,
):
    load_inverse = pltpu.make_async_copy(inverse_hbm, inverse_ref, sems.at[0])
    load_update = pltpu.make_async_copy(update_hbm, update_ref, sems.at[1])
    load_inverse1 = pltpu.make_async_copy(inverse1_hbm, inverse1_ref, sems.at[3])
    load_update1 = pltpu.make_async_copy(update1_hbm, update1_ref, sems.at[4])
    load_inverse.start()
    load_update.start()
    load_inverse1.start()
    load_update1.start()
    piece = arrived_ref[...].astype(f32)
    both[0:PAIRS, :] = piece
    both[PAIRS : 2 * PAIRS, :] = pltpu.roll(piece, RHS, 1)
    restore(0, EDGE1, slot_ref, both, tall)
    load_inverse.wait()
    load_update.wait()
    sols, terms = [], []
    for n in range(LEAVES):
        lhs = tall[n * LEAF : (n + 1) * LEAF, :].T[:RHS].astype(bf16)
        sols.append(mm(lhs, inverse_ref[n]))
    for n in range(LEAVES):
        sol_ref[:, n * LEAF : (n + 1) * LEAF] = sols[n]
        terms.append(mm(sols[n].astype(bf16), update_ref[n]).astype(bf16))
    store = pltpu.make_async_copy(sol_ref, out_hbm.at[:, 0:EDGE0], sems.at[2])
    store.start()
    core = lax.axis_index("core")
    for n in range(LEAVES):
        node = parent_ref[n]
        slot = node & 1
        away = ((node >> 3) & 1) != core
        targets = rows_ref[n : n + 1, :]

        @pl.when(away)
        def _():
            send_ref[slot, 0:RHS, :] = terms[n]
            send_ref[slot, RHS : RHS + META, :] = digits(targets, 0)

        @pl.when(jnp.logical_not(away))
        def _():
            kept_ref[slot] = terms[n]
            kept_rows[slot] = jnp.broadcast_to(targets, (8, BORDER0))

    for q in range(NODES1):
        rhs = tall[EDGE0 + q * SEP1 : EDGE0 + (q + 1) * SEP1, :].T[:RHS]
        rows = kept_rows[q, 0:1, :]
        high, low = (rows >> 8).astype(f32), (rows & (LOW - 1)).astype(f32)
        rhs1_ref[q] = rhs - place([kept_ref[q].astype(f32)], high, low, SEP1 // LOW)
    store.wait()
    load_inverse1.wait()
    load_update1.wait()


def level1_kernel(
    parent_vmem,
    got_ref,
    rhs_ref,
    rows_ref,
    inverse_ref,
    update_ref,
    after_ref,
    out_in,
    out_hbm,
    send_ref,
    sol_ref,
    parent_ref,
    sems,
):
    del out_in, after_ref
    load = pltpu.make_async_copy(parent_vmem, parent_ref, sems.at[NODES1])
    load.start()
    stores = []
    for n in range(NODES1):
        high, low, _ = undigits(got_ref[n, RHS : RHS + META, :])
        got = got_ref[n, 0:RHS, :].astype(f32)
        rhs = rhs_ref[n] - place([got], high, low, SEP1 // LOW)
        sol = mm(rhs.astype(bf16), inverse_ref[n])
        own = slice(n * SEP1, (n + 1) * SEP1)
        sol_ref[:, own] = sol
        part = slice(EDGE0 + n * SEP1, EDGE0 + (n + 1) * SEP1)
        stores.append(
            pltpu.make_async_copy(sol_ref.at[:, own], out_hbm.at[:, part], sems.at[n])
        )
        stores[n].start()
        terms = mm(sol.astype(bf16), update_ref[n]).astype(bf16)
        if n == 0:
            load.wait()
        node = parent_ref[n]
        slot = node & 3
        side = (node >> 3) & 1
        for f in range(FRONT):
            own = slice(f * PART1, (f + 1) * PART1)
            targets = rows_ref[n : n + 1, own] + (slot * SHARE2 - f * SHARE2)
            meta = digits(targets, side)
            for x in range(2):
                send_ref[x * FRONT + f, n, 0:RHS, :] = terms[:, own]
                send_ref[x * FRONT + f, n, RHS : RHS + META, :] = meta
    for store in stores:
        store.wait()


def sum2_kernel(got_ref, rhs_ref, out_ref):
    x0 = lax.axis_index("x0").astype(f32)
    terms, highs, lows = [], [], []
    for e in range(2 * FRONT):
        for n in range(NODES1):
            terms.append(got_ref[e, n, 0:RHS, :].astype(f32))
            high, low, side = undigits(got_ref[e, n, RHS : RHS + META, :])
            highs.append(jnp.where(side == x0, high, -1.0))
            lows.append(low)
    total = place(
        [jnp.concatenate(terms, axis=1)],
        jnp.concatenate(highs, axis=1),
        jnp.concatenate(lows, axis=1),
        NODES2 * SHARE2 // LOW,
    )
    out_ref[...] = (rhs_ref[...] - total).astype(bf16)


def ahead(k, share):
    front = lax.axis_index("front")
    return pl.ds(pl.multiple_of(((front + FRONT - k) & (FRONT - 1)) * share, share), share)


def part_kernel(own_ref, third_ref, second_ref, inverse_ref, part_ref):
    nodes, share = inverse_ref.shape[0], inverse_ref.shape[2]
    for c in range(nodes):
        own = slice(c * share, (c + 1) * share)
        total = mm(own_ref[:, own], inverse_ref[c, ahead(0, share), :])
        total = total + mm(third_ref[:, own], inverse_ref[c, ahead(3, share), :])
        part_ref[:, own] = total + mm(second_ref[:, own], inverse_ref[c, ahead(2, share), :])


def three_pieces(side, pieces, inverse):
    return pl.pallas_call(
        part_kernel,
        in_specs=[VMEM] * 4,
        out_specs=VMEM,
        out_shape=struct(side.shape, f32),
        compiler_params=params(6),
        name="part",
    )(side, pieces[2], pieces[1], inverse)


def level2_kernel(
    parent_vmem,
    part_ref,
    first_ref,
    rows_ref,
    inverse_ref,
    update_ref,
    after_ref,
    out_in,
    out_hbm,
    send_ref,
    sol_ref,
    terms_ref,
    terms_rows,
    parent_ref,
    sems,
):
    del out_in, after_ref
    load = pltpu.make_async_copy(parent_vmem, parent_ref, sems.at[1])
    load.start()
    for c in range(NODES2):
        own = slice(c * SHARE2, (c + 1) * SHARE2)
        sol = part_ref[:, own] + mm(first_ref[:, own], inverse_ref[c, ahead(1, SHARE2), :])
        sol_ref[:, own] = sol
        if c == 0:
            load.wait()
        node = parent_ref[c]
        slot = ((node >> 3) & 1) * NODES3 + (node & 1)
        terms_ref[slot] = mm(sol.astype(bf16), update_ref[c])
        terms_rows[slot] = jnp.broadcast_to(rows_ref[c : c + 1, :], (8, BORDER2))
    store = pltpu.make_async_copy(sol_ref, out_hbm.at[:, EDGE1:EDGE2], sems.at[0])
    store.start()
    for x in range(2):
        for f in range(FRONT):
            ends, end_rows = [], []
            for q in range(NODES3):
                at = x * NODES3 + q
                terms = terms_ref[at, :, f * PART2 : (f + 1) * PART2]
                rows = terms_rows[at, 0:1, f * PART2 : (f + 1) * PART2] + (q - f) * SHARE3
                send_ref[x * FRONT + f, q, 0:RHS, :] = terms[:, :128].astype(bf16)
                send_ref[x * FRONT + f, q, RHS : RHS + META, :] = digits(rows[:, :128], 0)
                ends.append(terms[:, 128:])
                end_rows.append(rows[:, 128:])
            end = jnp.concatenate(ends, axis=1).astype(bf16)
            send_ref[x * FRONT + f, NODES3, 0:RHS, :] = end
            send_ref[x * FRONT + f, NODES3, RHS : RHS + META, :] = digits(
                jnp.concatenate(end_rows, axis=1), 0
            )
    store.wait()


def sum3_kernel(got_ref, rhs_ref, out_ref):
    parts, highs, lows = [], [], []
    for x in range(2):
        for b in range(NODES3 + 1):
            pieces = [got_ref[x * FRONT + g, b, 0:RHS, :].astype(f32) for g in range(FRONT)]
            parts.append((pieces[0] + pieces[1]) + (pieces[2] + pieces[3]))
            high, low, _ = undigits(got_ref[x * FRONT, b, RHS : RHS + META, :])
            highs.append(high)
            lows.append(low)
    part = jnp.concatenate(parts, axis=1)
    coarse = part.astype(bf16).astype(f32)
    total = place(
        [coarse, part - coarse],
        jnp.concatenate(highs, axis=1),
        jnp.concatenate(lows, axis=1),
        NODES3 * SHARE3 // LOW,
    )
    out_ref[...] = (rhs_ref[...] - total).astype(bf16)


def level3_kernel(
    part_ref,
    first_ref,
    inverse_ref,
    out_in,
    out_hbm,
    sol_ref,
    sems,
):
    del out_in
    stores = []
    for c in range(NODES3):
        own = slice(c * SHARE3, (c + 1) * SHARE3)
        last = mm(first_ref[:, own], inverse_ref[c, ahead(1, SHARE3), :])
        sol_ref[:, own] = part_ref[:, own] + last
        part = slice(EDGE2 + c * SHARE3, EDGE2 + (c + 1) * SHARE3)
        stores.append(
            pltpu.make_async_copy(sol_ref.at[:, own], out_hbm.at[:, part], sems.at[c])
        )
        stores[c].start()
    for store in stores:
        store.wait()


def front_pieces(side):
    return [
        lax.ppermute(side, "front", [(f, (f + k) % FRONT) for f in range(FRONT)])
        for k in range(1, FRONT)
    ]


def exchange(block, axes):
    return lax.all_to_all(block, axes, split_axis=0, concat_axis=0, tiled=True)


def per_device(
    right_hand_sides,
    elimination_natural_index,
    leaf_diagonal_inverse,
    leaf_update_block,
    leaf_parent_rows,
    leaf_parent_node,
    level1_diagonal_inverse,
    level1_update_block,
    level1_parent_rows,
    level1_parent_node,
    level2_diagonal_inverse,
    level2_update_block,
    level2_parent_rows,
    level2_parent_node,
    level3_diagonal_inverse,
):
    requests, slot = pl.pallas_call(
        rank_kernel,
        in_specs=[VMEM],
        out_specs=[VMEM, VMEM],
        out_shape=[struct((DEVICES, LANES), i32), struct((BLOCKS, LANES), i32)],
        compiler_params=params(6),
        name="rank",
    )(elimination_natural_index.reshape(BLOCKS, LANES))
    asked = exchange(requests.reshape(DEVICES, 1, LANES), ALL).reshape(DEVICES, LANES)
    tall = pl.pallas_call(
        tall_kernel,
        in_specs=[VMEM],
        out_specs=VMEM,
        out_shape=struct((ROWS, 128), f32),
        compiler_params=params(8),
        name="tall",
    )(right_hand_sides)
    picked = pl.pallas_call(
        pick_kernel,
        in_specs=[VMEM, VMEM],
        out_specs=HBM,
        out_shape=pltpu.HBM((DEVICES * HALF, 128), bf16),
        scratch_shapes=[
            pltpu.VMEM((DEVICES * HALF, 128), f32),
            pltpu.VMEM((DEVICES * HALF, 128), bf16),
            pltpu.SMEM((DEVICES, LANES), i32),
            pltpu.SemaphoreType.DMA((2 * CHUNKS,)),
        ],
        compiler_params=params(16),
        name="pick",
    )(asked, tall)
    arrived = exchange(picked.reshape(DEVICES, HALF // 2, 2, 128), ALL)
    out, send0, rhs1, both, inverse1, update1 = pl.pallas_call(
        leaf_kernel,
        in_specs=[SMEM, SMEM, VMEM, VMEM, HBM, HBM, HBM, HBM],
        out_specs=[HBM, VMEM, VMEM, VMEM, VMEM, VMEM],
        out_shape=[
            struct((RHS, ROWS), f32),
            struct((NODES1, RHS + META, BORDER0), bf16),
            struct((NODES1, RHS, SEP1), f32),
            struct((2 * PAIRS, 128), f32),
            struct((NODES1, SEP1, SEP1), bf16),
            struct((NODES1, SEP1, BORDER1), bf16),
        ],
        scratch_shapes=[
            pltpu.VMEM((EDGE1, 128), f32),
            pltpu.VMEM((LEAVES, LEAF, LEAF), bf16),
            pltpu.VMEM((LEAVES, LEAF, BORDER0), bf16),
            pltpu.VMEM((RHS, EDGE0), f32),
            pltpu.VMEM((NODES1, RHS, BORDER0), bf16),
            pltpu.VMEM((NODES1, 8, BORDER0), i32),
            pltpu.SemaphoreType.DMA((5,)),
        ],
        compiler_params=params(24),
        name="leaf",
    )(
        slot,
        leaf_parent_node,
        arrived.reshape(DEVICES * HALF, 128),
        leaf_parent_rows,
        in_hbm(leaf_diagonal_inverse),
        in_hbm(leaf_update_block),
        in_hbm(level1_diagonal_inverse),
        in_hbm(level1_update_block),
    )
    got0 = lax.ppermute(send0, "core", [(0, 1), (1, 0)])
    rhs2 = late_rhs(EDGE1, EDGE2, slot, both, send0)
    out, send1 = pl.pallas_call(
        level1_kernel,
        in_specs=[VMEM] * 7 + [HBM],
        out_specs=[HBM, VMEM],
        out_shape=[
            struct((RHS, ROWS), f32),
            struct((2 * FRONT, NODES1, RHS + META, PART1), bf16),
        ],
        scratch_shapes=[
            pltpu.VMEM((RHS, NODES1 * SEP1), f32),
            pltpu.SMEM((NODES1,), i32),
            pltpu.SemaphoreType.DMA((NODES1 + 1,)),
        ],
        input_output_aliases={7: 0},
        compiler_params=params(24),
        name="level1",
    )(
        level1_parent_node,
        got0,
        rhs1,
        level1_parent_rows,
        inverse1,
        update1,
        rhs2,
        out,
    )
    got1 = exchange(send1, ("x0", "front"))
    side2 = pl.pallas_call(
        sum2_kernel,
        in_specs=[VMEM, VMEM],
        out_specs=VMEM,
        out_shape=struct((RHS, NODES2 * SHARE2), bf16),
        compiler_params=params(24),
        name="sum2",
    )(got1, rhs2)
    pieces = front_pieces(side2)
    rhs3 = late_rhs(EDGE2, ROWS, slot, both, side2)
    out, send2 = pl.pallas_call(
        level2_kernel,
        in_specs=[VMEM] * 7 + [HBM],
        out_specs=[HBM, VMEM],
        out_shape=[
            struct((RHS, ROWS), f32),
            struct((2 * FRONT, NODES3 + 1, RHS + META, 128), bf16),
        ],
        scratch_shapes=[
            pltpu.VMEM((RHS, NODES2 * SHARE2), f32),
            pltpu.VMEM((2 * NODES3, RHS, BORDER2), f32),
            pltpu.VMEM((2 * NODES3, 8, BORDER2), i32),
            pltpu.SMEM((NODES2,), i32),
            pltpu.SemaphoreType.DMA((2,)),
        ],
        input_output_aliases={7: 0},
        compiler_params=params(24),
        name="level2",
    )(
        level2_parent_node,
        three_pieces(side2, pieces, level2_diagonal_inverse),
        pieces[0],
        level2_parent_rows,
        level2_diagonal_inverse,
        level2_update_block,
        rhs3,
        out,
    )
    got2 = exchange(send2, ("x1", "front"))
    side3 = pl.pallas_call(
        sum3_kernel,
        in_specs=[VMEM, VMEM],
        out_specs=VMEM,
        out_shape=struct((RHS, NODES3 * SHARE3), bf16),
        compiler_params=params(24),
        name="sum3",
    )(got2, rhs3)
    pieces = front_pieces(side3)
    return pl.pallas_call(
        level3_kernel,
        in_specs=[VMEM] * 3 + [HBM],
        out_specs=HBM,
        out_shape=struct((RHS, ROWS), f32),
        scratch_shapes=[
            pltpu.VMEM((RHS, NODES3 * SHARE3), f32),
            pltpu.SemaphoreType.DMA((NODES3,)),
        ],
        input_output_aliases={3: 0},
        compiler_params=params(24),
        name="level3",
    )(
        three_pieces(side3, pieces, level3_diagonal_inverse),
        pieces[0],
        level3_diagonal_inverse,
        out,
    )


def solution(mesh):
    fine = Mesh(mesh.devices.reshape(4, 2, 2, 2, 4), ALL)
    return jax.shard_map(
        per_device,
        mesh=fine,
        in_specs=(
            P(None, ALL),
            P(ALL),
            P(ALL, None, None),
            P(ALL, None, None),
            P(ALL, None),
            P(ALL),
            P(ALL, None, None),
            P(ALL, None, None),
            P(ALL, None),
            P(ALL),
            P(SUBTREE, None, "front"),
            P(SUBTREE, "front", None),
            P(SUBTREE, None),
            P(SUBTREE),
            P(SUBTREE, None, "front"),
        ),
        out_specs=P(None, ALL),
        check_vma=False,
    )
```

```python
import functools

import jax
import jax.numpy as jnp
from jax import lax
from jax.experimental import pallas as pl
from jax.experimental.pallas import tpu as pltpu
from jax.sharding import Mesh, PartitionSpec as P

RHS = 64
LEAVES, LEAF, BORDER0 = 4, 512, 256
NODES1, SEP1, BORDER1 = 2, 1024, 512
NODES2, SEP2, BORDER2 = 4, 1536, 768
NODES3, SEP3 = 2, 2048
FRONT = 4
SHARE2, SHARE3 = SEP2 // FRONT, SEP3 // FRONT
PART1, PART2 = BORDER1 // FRONT, BORDER2 // FRONT
ROWS = 6656
DEVICES = 128
EACH = ROWS // DEVICES
HALF = EACH // 2
LANES = 128
BLOCKS = ROWS // LANES
PAIRS = DEVICES * HALF
GROUP = 4
CHUNKS = 4
EDGE0 = LEAVES * LEAF
EDGE1 = EDGE0 + NODES1 * SEP1
EDGE2 = EDGE1 + NODES2 * SHARE2
META = 8
LOW = 256

SUBTREE = ("z", "x1", "x0", "core")
ALL = SUBTREE + ("front",)

bf16, f32, i32 = jnp.bfloat16, jnp.float32, jnp.int32
VMEM = pl.BlockSpec(memory_space=pltpu.VMEM)
SMEM = pl.BlockSpec(memory_space=pltpu.SMEM)
HBM = pl.BlockSpec(memory_space=pltpu.HBM)


def params(mib):
    return pltpu.CompilerParams(vmem_limit_bytes=mib << 20)


def in_hbm(x):
    return pltpu.with_memory_space_constraint(x, pltpu.HBM)


def struct(shape, dtype):
    return jax.ShapeDtypeStruct(shape, dtype)


def mm(a, b):
    return jnp.dot(a, b, preferred_element_type=f32)


def mm_nt(a, b):
    return lax.dot_general(a, b, (((1,), (1,)), ((), ())), preferred_element_type=f32)


def place(terms, high, low, blocks):
    n = low.shape[1]
    ids = lax.broadcasted_iota(i32, (LOW, n), 0).astype(f32)
    picks = jnp.where(ids == low, 1.0, 0.0).astype(bf16)
    lhs = [jnp.where(high == h, t, 0.0).astype(bf16) for t in terms for h in range(blocks)]
    found = mm_nt(jnp.concatenate(lhs, axis=0), picks)
    out = []
    for h in range(blocks):
        parts = [
            found[(t * blocks + h) * RHS : (t * blocks + h + 1) * RHS] for t in range(len(terms))
        ]
        out.append(sum(parts[1:], parts[0]))
    return jnp.concatenate(out, axis=1)


def digits(targets, flag):
    n = targets.shape[1]
    ids = lax.broadcasted_iota(i32, (META, n), 0)
    high = jnp.broadcast_to(targets >> 8, (META, n))
    low = jnp.broadcast_to(targets & (LOW - 1), (META, n))
    rows = jnp.where(ids == 0, high, jnp.where(ids == 1, low, flag))
    return rows.astype(f32).astype(bf16)


def undigits(meta):
    m = meta.astype(f32)
    return m[0:1], m[1:2], m[2:3]


def tall_kernel(wide_ref, tall_ref):
    for b in range(ROWS // 512):
        wide = wide_ref[:, b * 512 : (b + 1) * 512]
        tall_ref[b * 512 : (b + 1) * 512, :] = jnp.concatenate([wide, wide], axis=0).T


def pick_kernel(asked_ref, tall_ref, out_hbm, buf, narrow, asked, sems):
    low = lax.broadcasted_iota(i32, (1, 128), 1) < RHS
    step = DEVICES // CHUNKS
    loads, stores = [], []
    for c in range(CHUNKS):
        part = slice(c * step, (c + 1) * step)
        loads.append(pltpu.make_async_copy(asked_ref.at[part], asked.at[part], sems.at[c]))
        loads[c].start()

    def gather(g, carry):
        base = pl.multiple_of(g * (GROUP * HALF), 8)
        for e in range(GROUP):
            d = g * GROUP + e
            for k in range(HALF):
                first = tall_ref[pl.ds(asked[d, k], 1), :]
                second = tall_ref[pl.ds(asked[d, k + HALF], 1), :]
                buf[pl.ds(base + (e * HALF + k), 1), :] = jnp.where(low, first, second)
        return carry

    for c in range(CHUNKS):
        loads[c].wait()
        lax.fori_loop(c * step // GROUP, (c + 1) * step // GROUP, gather, 0)
        part = slice(c * step * HALF, (c + 1) * step * HALF)
        narrow[part, :] = buf[part, :].astype(bf16)
        stores.append(
            pltpu.make_async_copy(narrow.at[part], out_hbm.at[part], sems.at[CHUNKS + c])
        )
        stores[c].start()
    for store in stores:
        store.wait()


def rank_kernel(index_ref, asked_ref, slot_ref):
    index = index_ref[...].astype(f32)
    source = jnp.floor((index + 0.5) * (1.0 / ROWS))
    local = index - source * ROWS
    high = jnp.floor(local * (1.0 / LANES))
    low = local - high * LANES
    rows = lax.broadcasted_iota(i32, (LANES, 2 * LANES), 0)
    columns = lax.broadcasted_iota(i32, (LANES, 2 * LANES), 1)
    before = jnp.where((rows < columns) | (columns >= LANES), 1.0, 0.0).astype(bf16)
    devices = lax.broadcasted_iota(i32, (DEVICES, LANES), 0).astype(f32)
    ranks = lax.broadcasted_iota(i32, (64, LANES), 0).astype(f32)
    seen = jnp.zeros((DEVICES, LANES), f32)
    mines, picks = [], []
    for b in range(BLOCKS):
        row = slice(b, b + 1)
        mine = jnp.where(devices == source[row], 1.0, 0.0)
        mine16 = mine.astype(bf16)
        counts = mm(mine16, before)
        rank = jnp.sum(mine * (seen + counts[:, :LANES]), axis=0, keepdims=True)
        seen = seen + counts[:, LANES:]
        at = ranks == rank
        values = [jnp.where(at, high[row], 0.0), jnp.where(at, low[row], 0.0)]
        mines.append(mine16)
        picks.append(jnp.concatenate(values, axis=0).astype(bf16))
        slot = source[row] * HALF + jnp.where(rank < HALF, rank, rank + (PAIRS - HALF))
        slot_ref[row, :] = slot.astype(i32)
    asked = mm_nt(jnp.concatenate(mines, axis=1), jnp.concatenate(picks, axis=1))
    asked_ref[...] = (asked * LANES + pltpu.roll(asked, 64, 1)).astype(i32)


def restore(first, last, slot_ref, both_ref, tall_ref):
    def gather(r, carry):
        base = pl.multiple_of((r - first // LANES) * LANES, LANES)
        for k in range(LANES):
            tall_ref[pl.ds(base + k, 1), :] = both_ref[pl.ds(slot_ref[r, k], 1), :]
        return carry

    lax.fori_loop(first // LANES, last // LANES, gather, 0)


def rhs_kernel(first, last, slot_vmem, both_ref, after_ref, rhs_ref, tall, slot_ref, sem):
    del after_ref
    part = slice(first // LANES // 8 * 8, last // LANES)
    load = pltpu.make_async_copy(slot_vmem.at[part], slot_ref.at[part], sem)
    load.start()
    load.wait()
    restore(first, last, slot_ref, both_ref, tall)
    rhs_ref[...] = tall[...].T[:RHS]


def late_rhs(first, last, slot, both, after):
    return pl.pallas_call(
        functools.partial(rhs_kernel, first, last),
        in_specs=[VMEM, VMEM, VMEM],
        out_specs=VMEM,
        out_shape=struct((RHS, last - first), f32),
        scratch_shapes=[
            pltpu.VMEM((last - first, 128), f32),
            pltpu.SMEM((BLOCKS, LANES), i32),
            pltpu.SemaphoreType.DMA,
        ],
        compiler_params=params(4),
        name="rhs",
    )(slot, both, after)


def leaf_kernel(
    slot_ref,
    parent_ref,
    arrived_ref,
    rows_ref,
    inverse_hbm,
    update_hbm,
    inverse1_hbm,
    update1_hbm,
    out_hbm,
    send_ref,
    rhs1_ref,
    both,
    inverse1_ref,
    update1_ref,
    tall,
    inverse_ref,
    update_ref,
    sol_ref,
    kept_ref,
    kept_rows,
    sems,
):
    load_inverse = pltpu.make_async_copy(inverse_hbm, inverse_ref, sems.at[0])
    load_update = pltpu.make_async_copy(update_hbm, update_ref, sems.at[1])
    load_inverse1 = pltpu.make_async_copy(inverse1_hbm, inverse1_ref, sems.at[3])
    load_update1 = pltpu.make_async_copy(update1_hbm, update1_ref, sems.at[4])
    load_inverse.start()
    load_update.start()
    load_inverse1.start()
    load_update1.start()
    piece = arrived_ref[...].astype(f32)
    both[0:PAIRS, :] = piece
    both[PAIRS : 2 * PAIRS, :] = pltpu.roll(piece, RHS, 1)
    restore(0, EDGE1, slot_ref, both, tall)
    load_inverse.wait()
    load_update.wait()
    sols, terms = [], []
    for n in range(LEAVES):
        lhs = tall[n * LEAF : (n + 1) * LEAF, :].T[:RHS].astype(bf16)
        sols.append(mm(lhs, inverse_ref[n]))
    for n in range(LEAVES):
        sol_ref[:, n * LEAF : (n + 1) * LEAF] = sols[n]
        terms.append(mm(sols[n].astype(bf16), update_ref[n]).astype(bf16))
    store = pltpu.make_async_copy(sol_ref, out_hbm.at[:, 0:EDGE0], sems.at[2])
    store.start()
    core = lax.axis_index("core")
    for n in range(LEAVES):
        node = parent_ref[n]
        slot = node & 1
        away = ((node >> 3) & 1) != core
        targets = rows_ref[n : n + 1, :]

        @pl.when(away)
        def _():
            send_ref[slot, 0:RHS, :] = terms[n]
            send_ref[slot, RHS : RHS + META, :] = digits(targets, 0)

        @pl.when(jnp.logical_not(away))
        def _():
            kept_ref[slot] = terms[n]
            kept_rows[slot] = jnp.broadcast_to(targets, (8, BORDER0))

    for q in range(NODES1):
        rhs = tall[EDGE0 + q * SEP1 : EDGE0 + (q + 1) * SEP1, :].T[:RHS]
        rows = kept_rows[q, 0:1, :]
        high, low = (rows >> 8).astype(f32), (rows & (LOW - 1)).astype(f32)
        rhs1_ref[q] = rhs - place([kept_ref[q].astype(f32)], high, low, SEP1 // LOW)
    store.wait()
    load_inverse1.wait()
    load_update1.wait()


def level1_kernel(
    parent_vmem,
    got_ref,
    rhs_ref,
    rows_ref,
    inverse_ref,
    update_ref,
    after_ref,
    out_in,
    out_hbm,
    send_ref,
    sol_ref,
    parent_ref,
    sems,
):
    del out_in, after_ref
    load = pltpu.make_async_copy(parent_vmem, parent_ref, sems.at[NODES1])
    load.start()
    stores = []
    for n in range(NODES1):
        high, low, _ = undigits(got_ref[n, RHS : RHS + META, :])
        got = got_ref[n, 0:RHS, :].astype(f32)
        rhs = rhs_ref[n] - place([got], high, low, SEP1 // LOW)
        sol = mm(rhs.astype(bf16), inverse_ref[n])
        own = slice(n * SEP1, (n + 1) * SEP1)
        sol_ref[:, own] = sol
        part = slice(EDGE0 + n * SEP1, EDGE0 + (n + 1) * SEP1)
        stores.append(
            pltpu.make_async_copy(sol_ref.at[:, own], out_hbm.at[:, part], sems.at[n])
        )
        stores[n].start()
        terms = mm(sol.astype(bf16), update_ref[n]).astype(bf16)
        if n == 0:
            load.wait()
        node = parent_ref[n]
        slot = node & 3
        side = (node >> 3) & 1
        for f in range(FRONT):
            own = slice(f * PART1, (f + 1) * PART1)
            targets = rows_ref[n : n + 1, own] + (slot * SHARE2 - f * SHARE2)
            meta = digits(targets, side)
            for x in range(2):
                send_ref[x * FRONT + f, n, 0:RHS, :] = terms[:, own]
                send_ref[x * FRONT + f, n, RHS : RHS + META, :] = meta
    for store in stores:
        store.wait()


def sum2_kernel(got_ref, rhs_ref, out_ref):
    x0 = lax.axis_index("x0").astype(f32)
    terms, highs, lows = [], [], []
    for e in range(2 * FRONT):
        for n in range(NODES1):
            terms.append(got_ref[e, n, 0:RHS, :].astype(f32))
            high, low, side = undigits(got_ref[e, n, RHS : RHS + META, :])
            highs.append(jnp.where(side == x0, high, -1.0))
            lows.append(low)
    total = place(
        [jnp.concatenate(terms, axis=1)],
        jnp.concatenate(highs, axis=1),
        jnp.concatenate(lows, axis=1),
        NODES2 * SHARE2 // LOW,
    )
    out_ref[...] = (rhs_ref[...] - total).astype(bf16)


def ahead(k, share):
    front = lax.axis_index("front")
    return pl.ds(pl.multiple_of(((front + FRONT - k) & (FRONT - 1)) * share, share), share)


def part_kernel(own_ref, third_ref, second_ref, inverse_ref, part_ref):
    nodes, share = inverse_ref.shape[0], inverse_ref.shape[2]
    for c in range(nodes):
        own = slice(c * share, (c + 1) * share)
        total = mm(own_ref[:, own], inverse_ref[c, ahead(0, share), :])
        total = total + mm(third_ref[:, own], inverse_ref[c, ahead(3, share), :])
        part_ref[:, own] = total + mm(second_ref[:, own], inverse_ref[c, ahead(2, share), :])


def three_pieces(side, pieces, inverse):
    return pl.pallas_call(
        part_kernel,
        in_specs=[VMEM] * 4,
        out_specs=VMEM,
        out_shape=struct(side.shape, f32),
        compiler_params=params(6),
        name="part",
    )(side, pieces[2], pieces[1], inverse)


def level2_kernel(
    parent_vmem,
    part_ref,
    first_ref,
    rows_ref,
    inverse_ref,
    update_ref,
    after_ref,
    out_in,
    out_hbm,
    send_ref,
    sol_ref,
    terms_ref,
    terms_rows,
    parent_ref,
    sems,
):
    del out_in, after_ref
    load = pltpu.make_async_copy(parent_vmem, parent_ref, sems.at[1])
    load.start()
    for c in range(NODES2):
        own = slice(c * SHARE2, (c + 1) * SHARE2)
        sol = part_ref[:, own] + mm(first_ref[:, own], inverse_ref[c, ahead(1, SHARE2), :])
        sol_ref[:, own] = sol
        if c == 0:
            load.wait()
        node = parent_ref[c]
        slot = ((node >> 3) & 1) * NODES3 + (node & 1)
        terms_ref[slot] = mm(sol.astype(bf16), update_ref[c])
        terms_rows[slot] = jnp.broadcast_to(rows_ref[c : c + 1, :], (8, BORDER2))
    store = pltpu.make_async_copy(sol_ref, out_hbm.at[:, EDGE1:EDGE2], sems.at[0])
    store.start()
    for x in range(2):
        for f in range(FRONT):
            ends, end_rows = [], []
            for q in range(NODES3):
                at = x * NODES3 + q
                terms = terms_ref[at, :, f * PART2 : (f + 1) * PART2]
                rows = terms_rows[at, 0:1, f * PART2 : (f + 1) * PART2] + (q - f) * SHARE3
                send_ref[x * FRONT + f, q, 0:RHS, :] = terms[:, :128].astype(bf16)
                send_ref[x * FRONT + f, q, RHS : RHS + META, :] = digits(rows[:, :128], 0)
                ends.append(terms[:, 128:])
                end_rows.append(rows[:, 128:])
            end = jnp.concatenate(ends, axis=1).astype(bf16)
            send_ref[x * FRONT + f, NODES3, 0:RHS, :] = end
            send_ref[x * FRONT + f, NODES3, RHS : RHS + META, :] = digits(
                jnp.concatenate(end_rows, axis=1), 0
            )
    store.wait()


def sum3_kernel(got_ref, rhs_ref, out_ref):
    parts, highs, lows = [], [], []
    for x in range(2):
        for b in range(NODES3 + 1):
            pieces = [got_ref[x * FRONT + g, b, 0:RHS, :].astype(f32) for g in range(FRONT)]
            parts.append((pieces[0] + pieces[1]) + (pieces[2] + pieces[3]))
            high, low, _ = undigits(got_ref[x * FRONT, b, RHS : RHS + META, :])
            highs.append(high)
            lows.append(low)
    part = jnp.concatenate(parts, axis=1)
    coarse = part.astype(bf16).astype(f32)
    total = place(
        [coarse, part - coarse],
        jnp.concatenate(highs, axis=1),
        jnp.concatenate(lows, axis=1),
        NODES3 * SHARE3 // LOW,
    )
    out_ref[...] = (rhs_ref[...] - total).astype(bf16)


def level3_kernel(
    part_ref,
    first_ref,
    inverse_ref,
    out_in,
    out_hbm,
    sol_ref,
    sems,
):
    del out_in
    stores = []
    for c in range(NODES3):
        own = slice(c * SHARE3, (c + 1) * SHARE3)
        last = mm(first_ref[:, own], inverse_ref[c, ahead(1, SHARE3), :])
        sol_ref[:, own] = part_ref[:, own] + last
        part = slice(EDGE2 + c * SHARE3, EDGE2 + (c + 1) * SHARE3)
        stores.append(
            pltpu.make_async_copy(sol_ref.at[:, own], out_hbm.at[:, part], sems.at[c])
        )
        stores[c].start()
    for store in stores:
        store.wait()


def front_pieces(side):
    return [
        lax.ppermute(side, "front", [(f, (f + k) % FRONT) for f in range(FRONT)])
        for k in range(1, FRONT)
    ]


def exchange(block, axes):
    return lax.all_to_all(block, axes, split_axis=0, concat_axis=0, tiled=True)


def per_device(
    right_hand_sides,
    elimination_natural_index,
    leaf_diagonal_inverse,
    leaf_update_block,
    leaf_parent_rows,
    leaf_parent_node,
    level1_diagonal_inverse,
    level1_update_block,
    level1_parent_rows,
    level1_parent_node,
    level2_diagonal_inverse,
    level2_update_block,
    level2_parent_rows,
    level2_parent_node,
    level3_diagonal_inverse,
):
    requests, slot = pl.pallas_call(
        rank_kernel,
        in_specs=[VMEM],
        out_specs=[VMEM, VMEM],
        out_shape=[struct((DEVICES, LANES), i32), struct((BLOCKS, LANES), i32)],
        compiler_params=params(6),
        name="rank",
    )(elimination_natural_index.reshape(BLOCKS, LANES))
    asked = exchange(requests.reshape(DEVICES, 1, LANES), ALL).reshape(DEVICES, LANES)
    tall = pl.pallas_call(
        tall_kernel,
        in_specs=[VMEM],
        out_specs=VMEM,
        out_shape=struct((ROWS, 128), f32),
        compiler_params=params(8),
        name="tall",
    )(right_hand_sides)
    picked = pl.pallas_call(
        pick_kernel,
        in_specs=[VMEM, VMEM],
        out_specs=HBM,
        out_shape=pltpu.HBM((DEVICES * HALF, 128), bf16),
        scratch_shapes=[
            pltpu.VMEM((DEVICES * HALF, 128), f32),
            pltpu.VMEM((DEVICES * HALF, 128), bf16),
            pltpu.SMEM((DEVICES, LANES), i32),
            pltpu.SemaphoreType.DMA((2 * CHUNKS,)),
        ],
        compiler_params=params(16),
        name="pick",
    )(asked, tall)
    arrived = exchange(picked.reshape(DEVICES, HALF // 2, 2, 128), ALL)
    out, send0, rhs1, both, inverse1, update1 = pl.pallas_call(
        leaf_kernel,
        in_specs=[SMEM, SMEM, VMEM, VMEM, HBM, HBM, HBM, HBM],
        out_specs=[HBM, VMEM, VMEM, VMEM, VMEM, VMEM],
        out_shape=[
            struct((RHS, ROWS), f32),
            struct((NODES1, RHS + META, BORDER0), bf16),
            struct((NODES1, RHS, SEP1), f32),
            struct((2 * PAIRS, 128), f32),
            struct((NODES1, SEP1, SEP1), bf16),
            struct((NODES1, SEP1, BORDER1), bf16),
        ],
        scratch_shapes=[
            pltpu.VMEM((EDGE1, 128), f32),
            pltpu.VMEM((LEAVES, LEAF, LEAF), bf16),
            pltpu.VMEM((LEAVES, LEAF, BORDER0), bf16),
            pltpu.VMEM((RHS, EDGE0), f32),
            pltpu.VMEM((NODES1, RHS, BORDER0), bf16),
            pltpu.VMEM((NODES1, 8, BORDER0), i32),
            pltpu.SemaphoreType.DMA((5,)),
        ],
        compiler_params=params(24),
        name="leaf",
    )(
        slot,
        leaf_parent_node,
        arrived.reshape(DEVICES * HALF, 128),
        leaf_parent_rows,
        in_hbm(leaf_diagonal_inverse),
        in_hbm(leaf_update_block),
        in_hbm(level1_diagonal_inverse),
        in_hbm(level1_update_block),
    )
    got0 = lax.ppermute(send0, "core", [(0, 1), (1, 0)])
    rhs2 = late_rhs(EDGE1, EDGE2, slot, both, send0)
    out, send1 = pl.pallas_call(
        level1_kernel,
        in_specs=[VMEM] * 7 + [HBM],
        out_specs=[HBM, VMEM],
        out_shape=[
            struct((RHS, ROWS), f32),
            struct((2 * FRONT, NODES1, RHS + META, PART1), bf16),
        ],
        scratch_shapes=[
            pltpu.VMEM((RHS, NODES1 * SEP1), f32),
            pltpu.SMEM((NODES1,), i32),
            pltpu.SemaphoreType.DMA((NODES1 + 1,)),
        ],
        input_output_aliases={7: 0},
        compiler_params=params(24),
        name="level1",
    )(
        level1_parent_node,
        got0,
        rhs1,
        level1_parent_rows,
        inverse1,
        update1,
        rhs2,
        out,
    )
    got1 = exchange(send1, ("x0", "front"))
    side2 = pl.pallas_call(
        sum2_kernel,
        in_specs=[VMEM, VMEM],
        out_specs=VMEM,
        out_shape=struct((RHS, NODES2 * SHARE2), bf16),
        compiler_params=params(24),
        name="sum2",
    )(got1, rhs2)
    pieces = front_pieces(side2)
    rhs3 = late_rhs(EDGE2, ROWS, slot, both, side2)
    out, send2 = pl.pallas_call(
        level2_kernel,
        in_specs=[VMEM] * 7 + [HBM],
        out_specs=[HBM, VMEM],
        out_shape=[
            struct((RHS, ROWS), f32),
            struct((2 * FRONT, NODES3 + 1, RHS + META, 128), bf16),
        ],
        scratch_shapes=[
            pltpu.VMEM((RHS, NODES2 * SHARE2), f32),
            pltpu.VMEM((2 * NODES3, RHS, BORDER2), f32),
            pltpu.VMEM((2 * NODES3, 8, BORDER2), i32),
            pltpu.SMEM((NODES2,), i32),
            pltpu.SemaphoreType.DMA((2,)),
        ],
        input_output_aliases={7: 0},
        compiler_params=params(24),
        name="level2",
    )(
        level2_parent_node,
        three_pieces(side2, pieces, level2_diagonal_inverse),
        pieces[0],
        level2_parent_rows,
        level2_diagonal_inverse,
        level2_update_block,
        rhs3,
        out,
    )
    got2 = exchange(send2, ("x1", "front"))
    side3 = pl.pallas_call(
        sum3_kernel,
        in_specs=[VMEM, VMEM],
        out_specs=VMEM,
        out_shape=struct((RHS, NODES3 * SHARE3), bf16),
        compiler_params=params(24),
        name="sum3",
    )(got2, rhs3)
    pieces = front_pieces(side3)
    return pl.pallas_call(
        level3_kernel,
        in_specs=[VMEM] * 3 + [HBM],
        out_specs=HBM,
        out_shape=struct((RHS, ROWS), f32),
        scratch_shapes=[
            pltpu.VMEM((RHS, NODES3 * SHARE3), f32),
            pltpu.SemaphoreType.DMA((NODES3,)),
        ],
        input_output_aliases={3: 0},
        compiler_params=params(24),
        name="level3",
    )(
        three_pieces(side3, pieces, level3_diagonal_inverse),
        pieces[0],
        level3_diagonal_inverse,
        out,
    )


def solution(mesh):
    fine = Mesh(mesh.devices.reshape(4, 2, 2, 2, 4), ALL)
    return jax.shard_map(
        per_device,
        mesh=fine,
        in_specs=(
            P(None, ALL),
            P(ALL),
            P(ALL, None, None),
            P(ALL, None, None),
            P(ALL, None),
            P(ALL),
            P(ALL, None, None),
            P(ALL, None, None),
            P(ALL, None),
            P(ALL),
            P(SUBTREE, None, "front"),
            P(SUBTREE, "front", None),
            P(SUBTREE, None),
            P(SUBTREE),
            P(SUBTREE, None, "front"),
        ),
        out_specs=P(None, ALL),
        check_vma=False,
    )
```
